1024 devices in a mesh: tile: 64 (over y_hi, x, core), node: 16 (over z, y_lo).
Axes of the slice: x: 8, y: 8 (y_hi: 4, y_lo: 2; y = y_hi * 2 + y_lo), z: 8, core: 2. Of those that a mesh axis runs over, the one named last changes fastest.
Arguments:
- mask_field: float32 [512, 8192], P(None, 'tile'), may hold values from -1 to 1
- kernel_taps: float32 [16, 8, 2, 48, 65], P('node'), may hold values from -0.5 to 0.5
- kernel_weights: float32 [16, 8], P('node'), may hold values from 0.02 to 0.2
- node_weights: float32 [16], replicated, may hold values from 0.03125 to 0.125
- node_index: int32 [16, 2], replicated, may hold values from 0 to 4
- freq_index: int32 [48], replicated, may hold values from -256 to 255, as said below
- chaos_weights: float32 [15], replicated, may hold values from 1 to 4
- target: bfloat16 [15, 512, 8192], P(None, None, 'tile'), may hold values from -3 to 3
Outputs:
- mask_gradient: float32 [512, 8192], P('node', 'tile')
The draws below stay inside these ranges and needn't reach their ends.
Inputs may be any that keep to these rules, and one draw needn't show every extreme that they name: `freq_index`: 48 distinct frequencies.
All inputs are finite; a program needn't handle non-finite values.
Results may differ from the reference program's by a relative error of at most 0.00085.
Values may be sent and summed in bfloat16 or wider, within the bound.
No kernel may reach another device: no remote copies, remote signals or barrier semaphores. Data moves between devices by JAX's collectives and lax.ppermute only.
A program may use at most 64 MiB of HBM per device.

```python
import math
import jax
import jax.numpy as jnp
from jax import lax

Y = 512
NF = 48
K = 8
TAPS = 65
NCH = 15
LEVELS = 5
NODES = 16
COLS = 8192


def draw_freq_index(key, part):
    order = jax.random.permutation(key, Y)
    return (order[:NF] - Y // 2).astype(jnp.int32)


def touch_ends(drawn, own_key, smallest, top_value):
    longest = drawn.shape.index(max(drawn.shape))
    spots = []
    for shift in (0, 1):
        where = [jax.random.randint(jax.random.fold_in(own_key, axis), (), 0, length) for axis, length in enumerate(drawn.shape)]
        where[longest] = (where[longest] + shift) % drawn.shape[longest]
        spots.append(tuple(where))
    return drawn.at[spots[0]].set(smallest).at[spots[1]].set(top_value)


def level_of(key, extent, split, least, top_value):
    factor_of, own = 1.0, jax.random.fold_in(key, 6)
    for position, parts in split:
        draws = jnp.exp(jax.random.uniform(jax.random.fold_in(own, position), (parts,), jnp.float32, least / len(split), top_value / len(split)))
        factor_of = factor_of * jnp.repeat(draws, extent[position] // parts).reshape([-1 if axis == position else 1 for axis in range(len(extent))])
    return factor_of


def gaussian(key, shape, deviation, bound, cuts=(), kind=jnp.bfloat16):
    loudness = level_of(key, shape, cuts, -0.22, 0.18) if cuts else 1.0
    entries = jax.random.normal(key, shape, jnp.float32) * deviation * loudness
    return jnp.minimum(jnp.maximum(entries, -bound), bound).astype(kind)


def setup_inputs(seed: int = 0) -> dict:
    splits = jax.random.split(jax.random.key(seed), 9)
    mask_field = jnp.clip(jax.random.uniform(splits[0], (Y, COLS), jnp.float32, -1.0, 1.0) * level_of(splits[0], (Y, COLS), ((1, 64),), -0.4, 0.0), -1.0, 1.0)
    kernel_taps = gaussian(splits[1], (NODES, K, 2, NF, TAPS), (2 * TAPS) ** -0.5, 0.5, ((0, 16),), jnp.float32)
    kernel_weights = jnp.clip(jnp.exp(math.log(0.2) - 2.3025851 * jax.random.uniform(splits[2], (NODES, K), jnp.float32) ** level_of(splits[2], (NODES, K), ((0, 16),), -0.2, 0.2)), 0.02, 0.2)
    node_weights = jnp.clip(jnp.exp(jax.random.uniform(splits[3], (NODES,), jnp.float32, math.log(0.03125), math.log(0.125))), 0.03125, 0.125)
    node_index = touch_ends(jax.random.randint(splits[4], (NODES, 2), 0, LEVELS), jax.random.fold_in(splits[4], 1), 0, LEVELS - 1).astype(jnp.int32)
    freq_index = draw_freq_index(jax.random.fold_in(splits[8], 71), 0)
    chaos_weights = jnp.clip(jnp.exp(jax.random.uniform(splits[6], (NCH,), jnp.float32, math.log(1.0), math.log(4.0))), 1.0, 4.0)
    target = gaussian(splits[7], (NCH, Y, COLS), 0.5, 3.0, ((2, 64),))
    return {"mask_field": mask_field, "kernel_taps": kernel_taps, "kernel_weights": kernel_weights, "node_weights": node_weights, "node_index": node_index, "freq_index": freq_index, "chaos_weights": chaos_weights, "target": target}


highest = lax.Precision.HIGHEST
resist_slope = 4.0
resist_level = 0.6

def spectra_tables(freq_index, pixel_rows):
    row_line = jnp.arange(pixel_rows, dtype=jnp.int32)
    phase_angle = jnp.mod(freq_index[:, None] * row_line[None, :], pixel_rows).astype(jnp.float32) * (2.0 * math.pi / pixel_rows)
    cosine_table = jnp.cos(phase_angle)
    sine_table = jnp.sin(phase_angle)
    forward = jnp.concatenate([cosine_table, -sine_table], 0) / math.sqrt(pixel_rows)
    freq_count = freq_index.shape[0]
    upper = jnp.concatenate([cosine_table.T, -sine_table.T], 1)
    lower = jnp.concatenate([sine_table.T, cosine_table.T], 1)
    inverse = jnp.concatenate([upper, lower], 0) / math.sqrt(freq_count)
    return (forward, inverse)

def legendre_set(coordinate):
    square = coordinate * coordinate
    return [jnp.ones_like(coordinate), coordinate, 1.5 * square - 0.5, (2.5 * square - 1.5) * coordinate, (4.375 * square - 3.75) * square + 0.375]

def level_coords(node_index):
    return node_index.astype(jnp.float32) * (2.0 / (LEVELS - 1)) - 1.0

def chaos_basis(node_index):
    coords = level_coords(node_index)
    focus_poly = legendre_set(coords[:, 0])
    dose_poly = legendre_set(coords[:, 1])
    columns = []
    for degree in range(5):
        for focus_order in range(degree, -1, -1):
            columns.append(focus_poly[focus_order] * dose_poly[degree - focus_order])
    return jnp.stack(columns, 1)

def dose_levels(node_index):
    return 1.0 + 0.1 * level_coords(node_index)[:, 1]

def resist_image(spectrum, taps_node, weights_node, dose_scale, inverse, col_count, radius):
    freq_count = taps_node.shape[2]
    shifted = jnp.stack([spectrum[:, offset:offset + col_count] for offset in range(2 * radius + 1)], 1)
    real_part = shifted[:freq_count]
    imag_part = shifted[freq_count:]
    taps_real = taps_node[:, 0]
    taps_imag = taps_node[:, 1]
    band_real = jnp.einsum('fsx,kfs->kfx', real_part, taps_real, precision=highest) - jnp.einsum('fsx,kfs->kfx', imag_part, taps_imag, precision=highest)
    band_imag = jnp.einsum('fsx,kfs->kfx', real_part, taps_imag, precision=highest) + jnp.einsum('fsx,kfs->kfx', imag_part, taps_real, precision=highest)
    stacked = jnp.concatenate([band_real, band_imag], 1)
    fields = jnp.einsum('yf,kfx->kyx', inverse, stacked, precision=highest)
    pixel_rows = inverse.shape[0] // 2
    powers = fields[:, :pixel_rows] * fields[:, :pixel_rows] + fields[:, pixel_rows:] * fields[:, pixel_rows:]
    intensity = jnp.einsum('k,kyx->yx', weights_node, powers, precision=highest)
    return jax.nn.sigmoid(resist_slope * (dose_scale * intensity - resist_level))

def reference(mask_field, kernel_taps, kernel_weights, node_weights, node_index, freq_index, chaos_weights, target):
    pixel_rows, col_count = mask_field.shape
    radius = (kernel_taps.shape[-1] - 1) // 2
    forward, inverse = spectra_tables(freq_index, pixel_rows)
    padded = jnp.pad(mask_field, ((0, 0), (radius, radius)))
    spectrum = jnp.dot(forward, padded, precision=highest)
    node_basis = chaos_basis(node_index)
    dose_scale = dose_levels(node_index)
    node_count = node_weights.shape[0]
    node_line = jnp.arange(node_count, dtype=jnp.int32)

    def image_of(spec, node_pos):
        return resist_image(spec, kernel_taps[node_pos], kernel_weights[node_pos], dose_scale[node_pos], inverse, col_count, radius)

    def add_node(running, node_pos):
        rounded = lax.optimization_barrier(image_of(spectrum, node_pos).astype(jnp.bfloat16))
        scaled = node_weights[node_pos] * node_basis[node_pos]
        return (running + scaled[:, None, None] * rounded.astype(jnp.float32)[None], None)
    coefficient, _ = lax.scan(add_node, jnp.zeros((node_basis.shape[1], pixel_rows, col_count), jnp.float32), node_line)
    mixed_terms = chaos_weights[:, None, None] * jnp.tanh(coefficient - target.astype(jnp.float32))

    def add_grad(running, node_pos):
        pressure = node_weights[node_pos] * jnp.einsum('j,jyx->yx', node_basis[node_pos], mixed_terms, precision=highest)
        resist, pullback = jax.vjp(lambda spec: image_of(spec, node_pos), spectrum)
        dspec, = pullback(pressure)
        return (running + dspec, None)
    dspec_sum, _ = lax.scan(add_grad, jnp.zeros_like(spectrum), node_line)
    grad_padded = jnp.dot(forward.T, dspec_sum, precision=highest)
    return grad_padded[:, radius:radius + col_count]
```

```python
import functools
import math

import jax
import jax.numpy as jnp
import ml_dtypes
import numpy as np
from jax import lax
from jax.experimental import pallas as pl
from jax.experimental.pallas import tpu as pltpu
from jax.sharding import PartitionSpec as P

LEVELS = 5
resist_slope = 4.0
resist_level = 0.6
degrees = [(d - q, q) for d in range(5) for q in range(d + 1)]
f32, bf16 = jnp.float32, jnp.bfloat16
vmem = pl.BlockSpec(memory_space=pltpu.VMEM)
smem = pl.BlockSpec(memory_space=pltpu.SMEM)
params = pltpu.CompilerParams(vmem_limit_bytes=48 << 20)


def parts_of(value):
    high = value.astype(bf16)
    return high, (value - high.astype(f32)).astype(bf16)


def mm(a, b):
    return jnp.dot(a, b, preferred_element_type=f32)


def mm3(a, b):
    return mm(a[0], b[0]) + mm(a[0], b[1]) + mm(a[1], b[0])


def cosine(turn, period):
    turn = jnp.bitwise_and(turn, period - 1)
    half = jnp.minimum(turn, period - turn)
    far = half > period // 4
    angle = jnp.where(far, period // 2 - half, half).astype(f32) * (2.0 * math.pi / period)
    z = angle * angle
    poly = jnp.full_like(z, 1.0 / math.factorial(12))
    for order in (10, 8, 6, 4, 2, 0):
        sign = -1.0 if order % 4 == 2 else 1.0
        poly = poly * z + sign / math.factorial(order)
    return jnp.where(far, -poly, poly)


def column_waves(length):
    turn = (np.arange(length)[:, None] * np.arange(length)[None, :]) % length
    wave = np.concatenate([np.cos(2 * np.pi * turn / length), np.sin(2 * np.pi * turn / length)], 1)
    high = wave.astype(np.float32).astype(ml_dtypes.bfloat16)
    low = (wave - high.astype(np.float64)).astype(np.float32).astype(ml_dtypes.bfloat16)
    return high, low


def tables_kernel(freq, taps, weights, wave_hi, wave_lo, u_ref, fh_ref, fl_ref, gr_ref, gi_ref):
    rows = u_ref.shape[0]
    count = freq.shape[0]
    kernels, tap_count = taps.shape[1], taps.shape[4]
    span = wave_hi.shape[0]
    radius = (tap_count - 1) // 2
    f_row = lax.broadcasted_iota(jnp.int32, (2 * count, rows), 0)
    f_freq = jnp.zeros((2 * count, 128), jnp.int32)
    line = lax.broadcasted_iota(jnp.int32, (2 * count, 128), 0)
    u_freq = jnp.zeros((8, 128), jnp.int32)
    lane = lax.broadcasted_iota(jnp.int32, (8, 128), 1)
    for i in range(count):
        value = freq[i]
        f_freq = jnp.where((line == i) | (line == i + count), value, f_freq)
        u_freq = jnp.where((lane == i) | (lane == i + count), value, u_freq)
    y_lane = lax.broadcasted_iota(jnp.int32, (2 * count, rows), 1)
    f_full = jnp.concatenate([f_freq] * (rows // 128), 1)
    quarter = rows // 4
    f_table = cosine(f_full * y_lane + jnp.where(f_row >= count, quarter, 0), rows)
    fh_ref[...], fl_ref[...] = parts_of(f_table)
    u_full = jnp.concatenate([u_freq] * (rows // 8), 0)
    u_lane = lax.broadcasted_iota(jnp.int32, (rows, 128), 1)
    u_y = lax.broadcasted_iota(jnp.int32, (rows, 128), 0)
    u_table = cosine(u_full * u_y + jnp.where(u_lane >= count, quarter, 0), rows)
    u_table = jnp.where(u_lane < 2 * count, u_table, 0.0)
    high, low = parts_of(u_table)
    u_ref[:, 0:128] = high
    u_ref[:, 128:256] = high
    u_ref[:, 256:384] = low
    side = [jnp.concatenate([w[span - radius : span], w[0 : tap_count - radius]], 0) for w in (wave_hi, wave_lo)]
    scale = jnp.sqrt(weights[...]) * (1.0 / (span * math.sqrt(count)))
    for k in range(kernels):
        both = parts_of(taps[0, k].reshape(2 * count, tap_count))
        prod = mm3(both, side)
        amount = scale[0:1, k : k + 1]
        gr_ref[k] = (prod[:count, :span] - prod[count:, span:]) * amount
        gi_ref[k] = (prod[:count, span:] + prod[count:, :span]) * amount


def forward_kernel(
    radius, dose, mask, before, after, fh, fl, gr, gi, u, wave_hi, wave_lo,
    image_ref, slope_ref, fields_ref, bh, bl, r, total,
):
    rows, cols = mask.shape
    kernels, count, span = gr.shape
    lane = lax.broadcasted_iota(jnp.int32, (rows, cols), 1)
    beyond = jnp.where(lane < radius, after[...], jnp.where(lane >= cols - radius, before[...], 0.0))
    padded = jnp.concatenate([mask[...], beyond], 1)
    spectrum = mm3((fh[...], fl[...]), parts_of(padded)) * (1.0 / math.sqrt(rows))
    wave = (wave_hi[...], wave_lo[...])
    prod = mm3(parts_of(spectrum), wave)
    a_re = prod[:count, :span] + prod[count:, span:]
    a_im = prod[count:, :span] - prod[:count, span:]
    for k in range(kernels):
        b_re = gr[k] * a_re - gi[k] * a_im
        b_im = gr[k] * a_im + gi[k] * a_re
        for d, value in ((0, b_re), (1, b_im)):
            at = pl.ds((2 * k + d) * count, count)
            bh[at, :], bl[at, :] = parts_of(value)
    near = [jnp.concatenate([w[:, 0:cols], w[:, span : span + cols]], 1) for w in (wave_hi, wave_lo)]
    r[...] = jnp.zeros(r.shape, bf16)
    for k in range(kernels):
        at = pl.ds(2 * k * count, 2 * count)
        q = mm3((bh[at, :], bl[at, :]), near)
        band_re = q[:count, :cols] - q[count:, cols:]
        band_im = q[:count, cols:] + q[count:, :cols]
        top = parts_of(jnp.concatenate([band_re, band_im], 1))
        bottom = parts_of(jnp.concatenate([band_im, -band_re], 1))
        for place, part in ((0, 0), (128, 1), (256, 0)):
            r[k, place : place + count, :] = top[part]
            r[k, place + count : place + 2 * count, :] = bottom[part]
    total[...] = jnp.zeros(total.shape, f32)

    @pl.loop(0, kernels)
    def _(k):
        field = mm(u[...], r[k])
        fields_ref[k] = field
        square = field * field
        total[...] += square[:, :cols] + square[:, cols:]

    value = dose[0]
    resist = jax.nn.sigmoid(resist_slope * (value * total[...] - resist_level))
    image_ref[...] = resist.astype(bf16)
    slope_ref[...] = resist * (1.0 - resist) * (2.0 * resist_slope * value)


def middle_kernel(index, node_weights, chaos, start, images, target, pressure_ref, rows_ref, sem, table):
    nodes, share, cols = images.shape
    terms = len(degrees)
    at = pl.multiple_of(start[0], share)
    copy = pltpu.make_async_copy(target.at[:, pl.ds(at, share), :], rows_ref, sem)
    copy.start()
    for n in range(nodes):
        poly = []
        for axis in range(2):
            c = index[n, axis].astype(f32) * (2.0 / (LEVELS - 1)) - 1.0
            s = c * c
            poly.append([None, c, 1.5 * s - 0.5, (2.5 * s - 1.5) * c, (4.375 * s - 3.75) * s + 0.375])
        weight = node_weights[n]
        for j, (p, q) in enumerate(degrees):
            value = weight
            if p:
                value = value * poly[0][p]
            if q:
                value = value * poly[1][q]
            table[n, j] = value
    copy.wait()
    slab = 16
    for first in range(0, share, slab):
        image = [images[n, first : first + slab, :].astype(f32) for n in range(nodes)]
        pressure = [None] * nodes
        for j in range(terms):
            coefficient = table[0, j] * image[0]
            for n in range(1, nodes):
                coefficient = coefficient + table[n, j] * image[n]
            wanted = rows_ref[j, first : first + slab, :].astype(f32)
            mixed = chaos[j] * jnp.tanh(coefficient - wanted)
            for n in range(nodes):
                term = table[n, j] * mixed
                pressure[n] = term if j == 0 else pressure[n] + term
        for n in range(nodes):
            pressure_ref[n, first : first + slab, :] = pressure[n]


def backward_kernel(pressure, slope, fields, fh, fl, gr, gi, wave_hi, wave_lo, own_ref, beyond_ref, dh, dl, scale):
    kernels, count, span = gr.shape
    rows, cols = slope.shape
    scale[...] = slope[...] * pressure[...]

    @pl.loop(0, kernels)
    def _(k):
        factor = scale[...]
        high, low = parts_of(fields[k] * jnp.concatenate([factor, factor], 1))
        prod = mm(fh[...], high) + mm(fh[...], low) + mm(fl[...], high)
        at = pl.multiple_of(2 * k * count, 2 * count)
        dh[pl.ds(at, count), :], dl[pl.ds(at, count), :] = parts_of(prod[:count, :cols] - prod[count:, cols:])
        at = pl.multiple_of(at + count, count)
        dh[pl.ds(at, count), :], dl[pl.ds(at, count), :] = parts_of(prod[:count, cols:] + prod[count:, :cols])

    near = (wave_hi[0:cols, :], wave_lo[0:cols, :])
    a_re = jnp.zeros((count, span), f32)
    a_im = jnp.zeros((count, span), f32)
    for k in range(kernels):
        at = pl.ds(2 * k * count, 2 * count)
        q = mm3((dh[at, :], dl[at, :]), near)
        b_re = q[:count, :span] + q[count:, span:]
        b_im = q[count:, :span] - q[:count, span:]
        a_re = a_re + gr[k] * b_re + gi[k] * b_im
        a_im = a_im + gr[k] * b_im - gi[k] * b_re
    wave = (wave_hi[...], wave_lo[...])
    prod = mm3(parts_of(jnp.concatenate([a_re, a_im], 0)), wave)
    d_re = prod[:count, :span] - prod[count:, span:]
    d_im = prod[:count, span:] + prod[count:, :span]
    own_ref[...] = jnp.concatenate([d_re[:, :cols], d_im[:, :cols]], 0)
    beyond_ref[...] = jnp.concatenate([d_re[:, cols:], d_im[:, cols:]], 0)


def rows_kernel(radius, own, before, after, u, out_ref):
    count, cols = own.shape
    rows = u.shape[0]
    lane = lax.broadcasted_iota(jnp.int32, (count, cols), 1)
    whole = own[...] + jnp.where(lane < radius, before[...], jnp.where(lane >= cols - radius, after[...], 0.0))
    high, low = parts_of(whole)
    high, low = (jnp.concatenate([v, jnp.zeros((128 - count, cols), bf16)], 0) for v in (high, low))
    out_ref[...] = mm(u[...], jnp.concatenate([high, low, high], 0)) * (1.0 / math.sqrt(rows))


def shape_of(*shape, dtype=f32):
    return jax.ShapeDtypeStruct(shape, dtype)


def call(kernel, spaces, outs, scratch=()):
    return pl.pallas_call(
        kernel,
        in_specs=spaces,
        out_specs=[vmem] * len(outs),
        out_shape=list(outs),
        scratch_shapes=list(scratch),
        compiler_params=params,
    )


def local(mask, taps, weights, node_weights, node_index, freq, chaos, target):
    rows, cols = mask.shape
    kernels, count, tap_count = taps.shape[1], taps.shape[3], taps.shape[4]
    radius = (tap_count - 1) // 2
    span = 2 * cols
    nodes, tiles = lax.axis_size("node"), lax.axis_size("tile")
    node = lax.axis_index("node")
    share = rows // nodes
    up = [(i, i + 1) for i in range(tiles - 1)]
    down = [(i + 1, i) for i in range(tiles - 1)]
    wave_hi, wave_lo = (jnp.asarray(w) for w in column_waves(span))
    before = lax.ppermute(mask, "tile", up)
    after = lax.ppermute(mask, "tile", down)
    dose = 1.0 + 0.1 * (node_index[node, 1:2].astype(f32) * (2.0 / (LEVELS - 1)) - 1.0)
    u, fh, fl, gr, gi = call(
        tables_kernel,
        [smem] + [vmem] * 4,
        [
            shape_of(rows, 384, dtype=bf16),
            shape_of(2 * count, rows, dtype=bf16),
            shape_of(2 * count, rows, dtype=bf16),
            shape_of(kernels, count, span),
            shape_of(kernels, count, span),
        ],
    )(freq, taps, weights, wave_hi, wave_lo)
    image, slope, fields = call(
        functools.partial(forward_kernel, radius),
        [smem] + [vmem] * 10,
        [shape_of(rows, cols, dtype=bf16), shape_of(rows, cols), shape_of(kernels, rows, 2 * cols)],
        [
            pltpu.VMEM((2 * kernels * count, span), bf16),
            pltpu.VMEM((2 * kernels * count, span), bf16),
            pltpu.VMEM((kernels, 384, 2 * cols), bf16),
            pltpu.VMEM((rows, cols), f32),
        ],
    )(dose, mask, before, after, fh, fl, gr, gi, u, wave_hi, wave_lo)
    images = lax.all_to_all(image.reshape(nodes, share, cols), "node", 0, 0)
    (pressure,) = call(
        middle_kernel,
        [smem, smem, smem, smem, vmem, pl.BlockSpec(memory_space=pl.ANY)],
        [shape_of(nodes, share, cols)],
        [
            pltpu.VMEM((target.shape[0], share, cols), bf16),
            pltpu.SemaphoreType.DMA,
            pltpu.SMEM((nodes, len(degrees)), f32),
        ],
    )(node_index, node_weights, chaos, (node * share).reshape(1), images, target)
    pressure = lax.all_to_all(pressure, "node", 0, 0).reshape(rows, cols)
    own, beyond = call(
        backward_kernel,
        [vmem] * 9,
        [shape_of(2 * count, cols), shape_of(2 * count, cols)],
        [
            pltpu.VMEM((2 * kernels * count, cols), bf16),
            pltpu.VMEM((2 * kernels * count, cols), bf16),
            pltpu.VMEM((rows, cols), f32),
        ],
    )(pressure, slope, fields, fh, fl, gr, gi, wave_hi, wave_lo)
    from_left = lax.ppermute(beyond, "tile", up)
    from_right = lax.ppermute(beyond, "tile", down)
    (spread,) = call(functools.partial(rows_kernel, radius), [vmem] * 4, [shape_of(rows, cols)])(
        own, from_left, from_right, u
    )
    return lax.all_to_all(spread.reshape(nodes, share, cols), "node", 0, 0).sum(0)


def solution(mesh):
    placed = (
        P(None, "tile"),
        P("node", None, None, None, None),
        P("node", None),
        P(),
        P(),
        P(),
        P(),
        P(None, None, "tile"),
    )
    return jax.shard_map(local, mesh=mesh, in_specs=placed, out_specs=P("node", "tile"), check_vma=False)
```

```python
import functools
import math

import jax
import jax.numpy as jnp
import ml_dtypes
import numpy as np
from jax import lax
from jax.experimental import pallas as pl
from jax.experimental.pallas import tpu as pltpu
from jax.sharding import PartitionSpec as P

LEVELS = 5
resist_slope = 4.0
resist_level = 0.6
degrees = [(d - q, q) for d in range(5) for q in range(d + 1)]
f32, bf16 = jnp.float32, jnp.bfloat16
vmem = pl.BlockSpec(memory_space=pltpu.VMEM)
smem = pl.BlockSpec(memory_space=pltpu.SMEM)
hbm = pl.BlockSpec(memory_space=pltpu.HBM)


def parts_of(value):
    high = value.astype(bf16)
    return high, (value - high.astype(f32)).astype(bf16)


def mm(a, b):
    return jnp.dot(a, b, preferred_element_type=f32)


def mm3(a, b):
    return mm(a[0], b[0]) + mm(a[0], b[1]) + mm(a[1], b[0])


def cosine(turn, period):
    turn = jnp.bitwise_and(turn, period - 1)
    half = jnp.minimum(turn, period - turn)
    far = half > period // 4
    angle = jnp.where(far, period // 2 - half, half).astype(f32) * (2.0 * math.pi / period)
    z = angle * angle
    poly = jnp.full_like(z, 1.0 / math.factorial(12))
    for order in (10, 8, 6, 4, 2, 0):
        sign = -1.0 if order % 4 == 2 else 1.0
        poly = poly * z + sign / math.factorial(order)
    return jnp.where(far, -poly, poly)


def column_waves(length):
    turn = (np.arange(length)[:, None] * np.arange(length)[None, :]) % length
    wave = np.concatenate([np.cos(2 * np.pi * turn / length), np.sin(2 * np.pi * turn / length)], 1)
    high = wave.astype(np.float32).astype(ml_dtypes.bfloat16)
    low = (wave - high.astype(np.float64)).astype(np.float32).astype(ml_dtypes.bfloat16)
    return high, low


def tables_kernel(
    start, freq_in, index_in, node_weights_in, chaos_in, weights_in, taps_in, wave_hi_in, wave_lo_in, mask_in, target_in,
    u_ref, fh_ref, fl_ref, gr_ref, gi_ref, wave_hi, wave_lo, spectrum_ref, wanted_ref, scalars_ref,
    freq, index, node_weights, chaos, weights, taps, mask, sems,
):
    rows, cols = mask.shape
    count = freq.shape[0]
    kernels, tap_count = taps.shape[1], taps.shape[4]
    span = wave_hi.shape[0]
    radius = (tap_count - 1) // 2
    nodes, share = index.shape[1], wanted_ref.shape[1]
    own = start[0]
    at = pl.multiple_of(own * share, share)
    moves = [
        (freq_in, freq),
        (index_in, index),
        (node_weights_in, node_weights),
        (chaos_in, chaos),
        (weights_in, weights),
        (mask_in, mask),
        (wave_hi_in, wave_hi),
        (wave_lo_in, wave_lo),
        (taps_in, taps),
        (target_in.at[:, pl.ds(at, share), :], wanted_ref),
    ]
    copies = [pltpu.make_async_copy(source, goal, sems.at[i]) for i, (source, goal) in enumerate(moves)]
    for copy in copies:
        copy.start()
    for copy in copies[:4]:
        copy.wait()
    f_row = lax.broadcasted_iota(jnp.int32, (2 * count, rows), 0)
    f_freq = jnp.zeros((2 * count, 128), jnp.int32)
    line = lax.broadcasted_iota(jnp.int32, (2 * count, 128), 0)
    u_freq = jnp.zeros((8, 128), jnp.int32)
    lane = lax.broadcasted_iota(jnp.int32, (8, 128), 1)
    for i in range(count):
        value = freq[i]
        f_freq = jnp.where((line == i) | (line == i + count), value, f_freq)
        u_freq = jnp.where((lane == i) | (lane == i + count), value, u_freq)
    y_lane = lax.broadcasted_iota(jnp.int32, (2 * count, rows), 1)
    f_full = jnp.concatenate([f_freq] * (rows // 128), 1)
    quarter = rows // 4
    f_table = cosine(f_full * y_lane + jnp.where(f_row >= count, quarter, 0), rows)
    f_parts = parts_of(f_table)
    fh_ref[...], fl_ref[...] = f_parts
    u_full = jnp.concatenate([u_freq] * (rows // 8), 0)
    u_lane = lax.broadcasted_iota(jnp.int32, (rows, 128), 1)
    u_y = lax.broadcasted_iota(jnp.int32, (rows, 128), 0)
    u_table = cosine(u_full * u_y + jnp.where(u_lane >= count, quarter, 0), rows)
    u_table = jnp.where(u_lane < 2 * count, u_table, 0.0)
    high, low = parts_of(u_table)
    u_ref[:, 0:128] = high
    u_ref[:, 128:256] = high
    u_ref[:, 256:384] = low
    for n in range(nodes):
        poly = []
        for axis in range(2):
            c = index[axis, n].astype(f32) * (2.0 / (LEVELS - 1)) - 1.0
            s = c * c
            poly.append([None, c, 1.5 * s - 0.5, (2.5 * s - 1.5) * c, (4.375 * s - 3.75) * s + 0.375])
        weight = node_weights[n]
        for j, (p, q) in enumerate(degrees):
            value = weight
            if p:
                value = value * poly[0][p]
            if q:
                value = value * poly[1][q]
            scalars_ref[16 * n + j : 16 * n + j + 1, :] = jnp.full((1, 128), value, f32)
    dose = 1.0 + 0.1 * (index[1, own].astype(f32) * (2.0 / (LEVELS - 1)) - 1.0)
    scalars_ref[15:16, :] = jnp.full((1, 128), dose, f32)
    for j in range(len(degrees)):
        scalars_ref[16 * nodes + j : 16 * nodes + j + 1, :] = jnp.full((1, 128), chaos[j], f32)
    for copy in copies[4:6]:
        copy.wait()
    spectrum_ref[...] = mm3(f_parts, parts_of(mask[...])) * (1.0 / math.sqrt(rows))
    for copy in copies[6:9]:
        copy.wait()
    side = [jnp.concatenate([w[span - radius : span], w[0 : tap_count - radius]], 0) for w in (wave_hi, wave_lo)]
    scale = jnp.sqrt(weights[...]) * (1.0 / (span * math.sqrt(count)))
    for k in range(kernels):
        both = parts_of(taps[0, k].reshape(2 * count, tap_count))
        prod = mm3(both, side)
        amount = scale[0:1, k : k + 1]
        gr_ref[k] = (prod[:count, :span] - prod[count:, span:]) * amount
        gi_ref[k] = (prod[:count, span:] + prod[count:, :span]) * amount
    copies[9].wait()


def forward_kernel(
    radius, scalars, spectrum, before, after, fh, fl, gr, gi, u, wave_hi, wave_lo,
    image_ref, slope_ref, fields_ref, bh, bl, r, total,
):
    rows, cols = before.shape
    kernels, count, span = gr.shape
    lane = lax.broadcasted_iota(jnp.int32, (rows, cols), 1)
    beyond = jnp.where(lane < radius, after[...], jnp.where(lane >= cols - radius, before[...], 0.0))
    outer = mm3((fh[...], fl[...]), parts_of(beyond)) * (1.0 / math.sqrt(rows))
    wave = (wave_hi[...], wave_lo[...])
    prod = mm3(parts_of(jnp.concatenate([spectrum[...], outer], 1)), wave)
    a_re = prod[:count, :span] + prod[count:, span:]
    a_im = prod[count:, :span] - prod[:count, span:]
    for k in range(kernels):
        b_re = gr[k] * a_re - gi[k] * a_im
        b_im = gr[k] * a_im + gi[k] * a_re
        for d, value in ((0, b_re), (1, b_im)):
            at = pl.ds((2 * k + d) * count, count)
            bh[at, :], bl[at, :] = parts_of(value)
    near = [jnp.concatenate([w[:, 0:cols], w[:, span : span + cols]], 1) for w in (wave_hi, wave_lo)]
    r[...] = jnp.zeros(r.shape, bf16)
    for k in range(kernels):
        at = pl.ds(2 * k * count, 2 * count)
        q = mm3((bh[at, :], bl[at, :]), near)
        band_re = q[:count, :cols] - q[count:, cols:]
        band_im = q[:count, cols:] + q[count:, :cols]
        top = parts_of(jnp.concatenate([band_re, band_im], 1))
        bottom = parts_of(jnp.concatenate([band_im, -band_re], 1))
        for place, part in ((0, 0), (128, 1), (256, 0)):
            r[k, place : place + count, :] = top[part]
            r[k, place + count : place + 2 * count, :] = bottom[part]
    total[...] = jnp.zeros(total.shape, f32)

    @pl.loop(0, kernels)
    def _(k):
        field = mm(u[...], r[k])
        fields_ref[k] = field
        square = field * field
        total[...] += square[:, :cols] + square[:, cols:]

    value = scalars[15:16, :]
    resist = jax.nn.sigmoid(resist_slope * (value * total[...] - resist_level))
    image_ref[...] = resist.astype(bf16)
    slope_ref[...] = resist * (1.0 - resist) * (2.0 * resist_slope * value)


def middle_kernel(images, wanted, scalars, pressure_ref):
    nodes, share, cols = images.shape
    slab = 16
    for first in range(0, share, slab):
        image = [images[n, first : first + slab, :].astype(f32) for n in range(nodes)]
        pressure = [None] * nodes
        for j in range(len(degrees)):
            weight = [scalars[16 * n + j : 16 * n + j + 1, :] for n in range(nodes)]
            coefficient = weight[0] * image[0]
            for n in range(1, nodes):
                coefficient = coefficient + weight[n] * image[n]
            goal = wanted[j, first : first + slab, :].astype(f32)
            mixed = scalars[16 * nodes + j : 16 * nodes + j + 1, :] * jnp.tanh(coefficient - goal)
            for n in range(nodes):
                term = weight[n] * mixed
                pressure[n] = term if j == 0 else pressure[n] + term
        for n in range(nodes):
            pressure_ref[n, first : first + slab, :] = pressure[n]


def backward_kernel(pressure, slope, fields, fh, fl, gr, gi, wave_hi, wave_lo, own_ref, beyond_ref, dh, dl, scale):
    kernels, count, span = gr.shape
    rows, cols = slope.shape
    scale[...] = slope[...] * pressure[...]

    @pl.loop(0, kernels)
    def _(k):
        factor = scale[...]
        high, low = parts_of(fields[k] * jnp.concatenate([factor, factor], 1))
        prod = mm(fh[...], high) + mm(fh[...], low) + mm(fl[...], high)
        at = pl.multiple_of(2 * k * count, 2 * count)
        dh[pl.ds(at, count), :], dl[pl.ds(at, count), :] = parts_of(prod[:count, :cols] - prod[count:, cols:])
        at = pl.multiple_of(at + count, count)
        dh[pl.ds(at, count), :], dl[pl.ds(at, count), :] = parts_of(prod[:count, cols:] + prod[count:, :cols])

    near = (wave_hi[0:cols, :], wave_lo[0:cols, :])
    a_re = jnp.zeros((count, span), f32)
    a_im = jnp.zeros((count, span), f32)
    for k in range(kernels):
        at = pl.ds(2 * k * count, 2 * count)
        q = mm3((dh[at, :], dl[at, :]), near)
        b_re = q[:count, :span] + q[count:, span:]
        b_im = q[count:, :span] - q[:count, span:]
        a_re = a_re + gr[k] * b_re + gi[k] * b_im
        a_im = a_im + gr[k] * b_im - gi[k] * b_re
    wave = (wave_hi[...], wave_lo[...])
    prod = mm3(parts_of(jnp.concatenate([a_re, a_im], 0)), wave)
    d_re = prod[:count, :span] - prod[count:, span:]
    d_im = prod[:count, span:] + prod[count:, :span]
    own_ref[...] = jnp.concatenate([d_re[:, :cols], d_im[:, :cols]], 0)
    beyond_ref[...] = jnp.concatenate([d_re[:, cols:], d_im[:, cols:]], 0)


def rows_kernel(radius, own, before, after, u, out_ref):
    count, cols = own.shape
    rows = u.shape[0]
    lane = lax.broadcasted_iota(jnp.int32, (count, cols), 1)
    whole = own[...] + jnp.where(lane < radius, before[...], jnp.where(lane >= cols - radius, after[...], 0.0))
    high, low = parts_of(whole)
    high, low = (jnp.concatenate([v, jnp.zeros((128 - count, cols), bf16)], 0) for v in (high, low))
    out_ref[...] = mm(u[...], jnp.concatenate([high, low, high], 0)) * (1.0 / math.sqrt(rows))


def shape_of(*shape, dtype=f32):
    return jax.ShapeDtypeStruct(shape, dtype)


def call(kernel, mebibytes, spaces, outs, scratch=()):
    return pl.pallas_call(
        kernel,
        in_specs=spaces,
        out_specs=[vmem] * len(outs),
        out_shape=list(outs),
        scratch_shapes=list(scratch),
        compiler_params=pltpu.CompilerParams(vmem_limit_bytes=mebibytes << 20),
    )


def local(mask, taps, weights, node_weights, node_index, freq, chaos, target):
    rows, cols = mask.shape
    kernels, count, tap_count = taps.shape[1], taps.shape[3], taps.shape[4]
    radius = (tap_count - 1) // 2
    span = 2 * cols
    nodes, tiles = lax.axis_size("node"), lax.axis_size("tile")
    node = lax.axis_index("node")
    share = rows // nodes
    up = [(i, i + 1) for i in range(tiles - 1)]
    down = [(i + 1, i) for i in range(tiles - 1)]
    wave_hi, wave_lo = (jnp.asarray(w) for w in column_waves(span))
    before = lax.ppermute(mask, "tile", up)
    after = lax.ppermute(mask, "tile", down)
    u, fh, fl, gr, gi, wave_hi, wave_lo, spectrum, wanted, scalars = call(
        tables_kernel,
        16,
        [smem] + [hbm] * 10,
        [
            shape_of(rows, 384, dtype=bf16),
            shape_of(2 * count, rows, dtype=bf16),
            shape_of(2 * count, rows, dtype=bf16),
            shape_of(kernels, count, span),
            shape_of(kernels, count, span),
            shape_of(span, 2 * span, dtype=bf16),
            shape_of(span, 2 * span, dtype=bf16),
            shape_of(2 * count, cols),
            shape_of(target.shape[0], share, cols, dtype=bf16),
            shape_of(16 * nodes + 16, 128),
        ],
        [
            pltpu.SMEM(freq.shape, jnp.int32),
            pltpu.SMEM((2, nodes), jnp.int32),
            pltpu.SMEM((nodes,), f32),
            pltpu.SMEM(chaos.shape, f32),
            pltpu.VMEM(weights.shape, f32),
            pltpu.VMEM(taps.shape, f32),
            pltpu.VMEM(mask.shape, f32),
            pltpu.SemaphoreType.DMA((10,)),
        ],
    )(
        node.reshape(1),
        *(
            pltpu.with_memory_space_constraint(a, pltpu.HBM)
            for a in (freq, node_index.T, node_weights, chaos, weights, taps, wave_hi, wave_lo, mask, target)
        ),
    )
    image, slope, fields = call(
        functools.partial(forward_kernel, radius),
        16,
        [vmem] * 11,
        [shape_of(rows, cols, dtype=bf16), shape_of(rows, cols), shape_of(kernels, rows, 2 * cols)],
        [
            pltpu.VMEM((2 * kernels * count, span), bf16),
            pltpu.VMEM((2 * kernels * count, span), bf16),
            pltpu.VMEM((kernels, 384, 2 * cols), bf16),
            pltpu.VMEM((rows, cols), f32),
        ],
    )(scalars, spectrum, before, after, fh, fl, gr, gi, u, wave_hi, wave_lo)
    images = lax.all_to_all(image.reshape(nodes, share, cols), "node", 0, 0)
    (pressure,) = call(middle_kernel, 8, [vmem] * 3, [shape_of(nodes, share, cols)])(images, wanted, scalars)
    pressure = lax.all_to_all(pressure, "node", 0, 0).reshape(rows, cols)
    own, beyond = call(
        backward_kernel,
        16,
        [vmem] * 9,
        [shape_of(2 * count, cols), shape_of(2 * count, cols)],
        [
            pltpu.VMEM((2 * kernels * count, cols), bf16),
            pltpu.VMEM((2 * kernels * count, cols), bf16),
            pltpu.VMEM((rows, cols), f32),
        ],
    )(pressure, slope, fields, fh, fl, gr, gi, wave_hi, wave_lo)
    from_left = lax.ppermute(beyond, "tile", up)
    from_right = lax.ppermute(beyond, "tile", down)
    (spread,) = call(functools.partial(rows_kernel, radius), 8, [vmem] * 4, [shape_of(rows, cols)])(
        own, from_left, from_right, u
    )
    return lax.all_to_all(spread.reshape(nodes, share, cols), "node", 0, 0).sum(0)


def solution(mesh):
    placed = (
        P(None, "tile"),
        P("node", None, None, None, None),
        P("node", None),
        P(),
        P(),
        P(),
        P(),
        P(None, None, "tile"),
    )
    return jax.shard_map(local, mesh=mesh, in_specs=placed, out_specs=P("node", "tile"), check_vma=False)
```

```python
import functools
import math

import jax
import jax.numpy as jnp
import ml_dtypes
import numpy as np
from jax import lax
from jax.experimental import pallas as pl
from jax.experimental.pallas import tpu as pltpu
from jax.sharding import PartitionSpec as P

LEVELS = 5
resist_slope = 4.0
resist_level = 0.6
degrees = [(d - q, q) for d in range(5) for q in range(d + 1)]
f32, bf16 = jnp.float32, jnp.bfloat16
vmem = pl.BlockSpec(memory_space=pltpu.VMEM)
smem = pl.BlockSpec(memory_space=pltpu.SMEM)
hbm = pl.BlockSpec(memory_space=pltpu.HBM)


def parts_of(value):
    high = value.astype(bf16)
    return high, (value - high.astype(f32)).astype(bf16)


def mm(a, b):
    return jnp.dot(a, b, preferred_element_type=f32)


def mm3(a, b):
    return mm(a[0], b[0]) + mm(a[0], b[1]) + mm(a[1], b[0])


def cosine(turn, period):
    turn = jnp.bitwise_and(turn, period - 1)
    half = jnp.minimum(turn, period - turn)
    far = half > period // 4
    angle = jnp.where(far, period // 2 - half, half).astype(f32) * (2.0 * math.pi / period)
    z = angle * angle
    poly = jnp.full_like(z, 1.0 / math.factorial(12))
    for order in (10, 8, 6, 4, 2, 0):
        sign = -1.0 if order % 4 == 2 else 1.0
        poly = poly * z + sign / math.factorial(order)
    return jnp.where(far, -poly, poly)


def column_waves(length):
    turn = (np.arange(length)[:, None] * np.arange(length)[None, :]) % length
    wave = np.concatenate([np.cos(2 * np.pi * turn / length), np.sin(2 * np.pi * turn / length)], 1)
    high = wave.astype(np.float32).astype(ml_dtypes.bfloat16)
    low = (wave - high.astype(np.float64)).astype(np.float32).astype(ml_dtypes.bfloat16)
    return high, low


def lanes(shape):
    return lax.broadcasted_iota(jnp.int32, shape, len(shape) - 1)


def turned(value):
    return pltpu.roll(value, value.shape[-1] // 2, len(value.shape) - 1)


def outer_lanes(shape, radius):
    lane = lanes(shape)
    return (lane < radius) | (lane >= shape[-1] - radius)


def right_lanes(shape, radius):
    lane, half = lanes(shape), shape[-1] // 2
    return (lane < radius) | ((lane >= half) & (lane < half + radius))


def spectrum_kernel(radius, node, freq_in, mask_in, target_in, packed_ref, wanted_ref, fh_ref, fl_ref, freq, mask, raw, sems):
    rows, cols = mask.shape
    count = freq.shape[0]
    terms, share = raw.shape[0], raw.shape[1]
    own = node[0]
    mirrored = own >= rows // (2 * share)
    at = jnp.where(mirrored, rows + rows // 2 - share - own * share, own * share)
    at = pl.multiple_of(at, share)
    moves = [(freq_in, freq), (mask_in, mask), (target_in.at[:, pl.ds(at, share), :], raw)]
    copies = [pltpu.make_async_copy(source, goal, sems.at[i]) for i, (source, goal) in enumerate(moves)]
    for copy in copies:
        copy.start()
    copies[0].wait()
    line = lax.broadcasted_iota(jnp.int32, (2 * count, 128), 0)
    f_freq = jnp.zeros((2 * count, 128), jnp.int32)
    for i in range(count):
        f_freq = jnp.where((line == i) | (line == i + count), freq[i], f_freq)
    f_full = jnp.concatenate([f_freq] * (rows // 128), 1)
    f_row = lax.broadcasted_iota(jnp.int32, (2 * count, rows), 0)
    turn = f_full * (2 * lanes((2 * count, rows)) + 1) + jnp.where(f_row >= count, rows // 2, 0)
    f_parts = parts_of(cosine(turn, 2 * rows))
    fh_ref[...], fl_ref[...] = f_parts
    copies[2].wait()
    row = lax.broadcasted_iota(jnp.int32, (share, share), 0)
    chosen = jnp.where(mirrored, share - 1 - row, row) == lanes((share, share))
    order = jnp.where(chosen, 1.0, 0.0).astype(bf16)
    half = share // 2
    outer = outer_lanes((half, cols), radius)
    for j in range(terms):
        goal = mm(order, raw[j])
        wanted_ref[j] = goal.astype(bf16)
        edge = jnp.where(outer, goal[:half], turned(goal[half:]))
        packed_ref[4 * count + half * j : 4 * count + half * (j + 1), :] = edge.astype(bf16)
    copies[1].wait()
    high, low = parts_of(mm3(f_parts, parts_of(mask[...])) * (1.0 / math.sqrt(rows)))
    packed_ref[0 : 2 * count, :] = high
    packed_ref[2 * count : 4 * count, :] = low


def tables_kernel(
    node, freq_in, index_in, node_weights_in, chaos_in, weights_in, taps_in, wave_hi_in, wave_lo_in,
    u_ref, cs_ref, gr_ref, gi_ref, wave_hi, wave_lo, scalars_ref,
    freq, index, node_weights, chaos, weights, taps, sems,
):
    rows = u_ref.shape[0]
    count = freq.shape[0]
    kernels, tap_count = taps.shape[1], taps.shape[4]
    span = wave_hi.shape[0]
    radius = (tap_count - 1) // 2
    nodes = index.shape[1]
    moves = [
        (freq_in, freq),
        (index_in, index),
        (node_weights_in, node_weights),
        (chaos_in, chaos),
        (weights_in, weights),
        (wave_hi_in, wave_hi),
        (wave_lo_in, wave_lo),
        (taps_in, taps),
    ]
    copies = [pltpu.make_async_copy(source, goal, sems.at[i]) for i, (source, goal) in enumerate(moves)]
    for copy in copies:
        copy.start()
    for copy in copies[:4]:
        copy.wait()
    lane = lanes((8, 256))
    u_freq = jnp.zeros((8, 256), jnp.int32)
    for i in range(count):
        u_freq = jnp.where((lane == i) | (lane == i + count) | (lane == i + 2 * count), freq[i], u_freq)
    quarter = rows // 2
    full = jnp.concatenate([u_freq[:, :128]] * (rows // 8), 0)
    u_lane = lanes((rows, 128))
    u_y = lax.broadcasted_iota(jnp.int32, (rows, 128), 0)
    table = cosine(full * (2 * u_y + 1) + jnp.where(u_lane >= count, quarter, 0), 2 * rows)
    high, low = parts_of(jnp.where(u_lane < 2 * count, table, 0.0))
    u_ref[:, 0:128] = high
    u_ref[:, 128:256] = high
    u_ref[:, 256:384] = low
    full = jnp.concatenate([u_freq] * (rows // 8), 0)
    c_row = lax.broadcasted_iota(jnp.int32, (rows, 256), 0)
    sine = c_row >= rows // 2
    c_y = jnp.where(sine, c_row - rows // 2, c_row)
    table = cosine(full * (2 * c_y + 1) - jnp.where(sine, quarter, 0), 2 * rows)
    high, low = parts_of(table)
    both = jnp.where(lanes((rows, 256)) < 2 * count, high.astype(f32), low.astype(f32))
    cs_ref[...] = both[:, : 3 * count].astype(bf16)
    for n in range(nodes):
        poly = []
        for axis in range(2):
            c = index[axis, n].astype(f32) * (2.0 / (LEVELS - 1)) - 1.0
            s = c * c
            poly.append([None, c, 1.5 * s - 0.5, (2.5 * s - 1.5) * c, (4.375 * s - 3.75) * s + 0.375])
        weight = node_weights[n]
        for j, (p, q) in enumerate(degrees):
            value = weight
            if p:
                value = value * poly[0][p]
            if q:
                value = value * poly[1][q]
            scalars_ref[16 * n + j : 16 * n + j + 1, :] = jnp.full((1, 128), value, f32)
    dose = 1.0 + 0.1 * (index[1, node[0]].astype(f32) * (2.0 / (LEVELS - 1)) - 1.0)
    scalars_ref[15:16, :] = jnp.full((1, 128), dose, f32)
    for j in range(len(degrees)):
        scalars_ref[16 * nodes + j : 16 * nodes + j + 1, :] = jnp.full((1, 128), chaos[j], f32)
    for copy in copies[4:]:
        copy.wait()
    side = [jnp.concatenate([w[span - radius : span], w[0 : tap_count - radius]], 0) for w in (wave_hi, wave_lo)]
    scale = jnp.sqrt(weights[...]) * (1.0 / (span * math.sqrt(count)))
    for k in range(kernels):
        parts = parts_of(taps[0, k].reshape(2 * count, tap_count))
        prod = mm3(parts, side)
        amount = scale[0:1, k : k + 1]
        gr_ref[k] = (prod[:count, :span] - prod[count:, span:]) * amount
        gi_ref[k] = (prod[:count, span:] + prod[count:, :span]) * amount


def forward_kernel(
    radius, tiles, tile, scalars, packed, before, after, gr, gi, cs, wave_hi, wave_lo,
    image_ref, slope_ref, fields_ref, bh, bl, x, total,
):
    kernels, count, span = gr.shape
    nodes, slab, cols = image_ref.shape
    rows = slope_ref.shape[0]
    share = rows // nodes
    half = share // 2
    near = lanes((2 * count, cols)) < 2 * radius
    pair = []
    for part in range(2):
        at = pl.ds(2 * part * count, 2 * count)
        beyond = jnp.where(near, after[at, :].astype(f32), before[at, :].astype(f32))
        pair.append(jnp.concatenate([packed[at, :], beyond.astype(bf16)], 1))
    wave = (wave_hi[...], wave_lo[...])
    prod = mm3(pair, wave)
    a_re = prod[:count, :span] + prod[count:, span:]
    a_im = prod[count:, :span] - prod[:count, span:]
    for k in range(kernels):
        b_re = gr[k] * a_re - gi[k] * a_im
        b_im = gr[k] * a_im + gi[k] * a_re
        for d, value in ((0, b_re), (1, b_im)):
            at = pl.ds((2 * k + d) * count, count)
            bh[at, :], bl[at, :] = parts_of(value)
    outer = outer_lanes((count, cols), radius)
    for k in range(kernels):
        at = pl.ds(2 * k * count, 2 * count)
        q = mm3((bh[at, :], bl[at, :]), wave)
        re = q[:count, :span] - q[count:, span:]
        im = q[:count, span:] + q[count:, :span]
        edge = jnp.where(outer, re[:, cols:], turned(im[:, cols:]))
        cross = jnp.where(outer, im[:, cols:], -turned(re[:, cols:]))
        straight = jnp.concatenate([re[:, :cols], im[:, :cols], edge], 1)
        crossed = jnp.concatenate([im[:, :cols], -re[:, :cols], cross], 1)
        for d, value in ((0, straight), (1, crossed)):
            high, low = parts_of(value)
            for place, part in ((0, high), (1, low), (2, high)):
                x[k, d, place * count : (place + 1) * count, :] = part
    total[...] = jnp.zeros(total.shape, f32)

    @pl.loop(0, kernels)
    def _(k):
        even = mm(cs[: rows // 2, :], x[k, 0])
        odd = mm(cs[rows // 2 :, :], x[k, 1])
        for first, field in ((0, even - odd), (rows // 2, even + odd)):
            at = pl.ds(first, rows // 2)
            fields_ref[k, at, :] = field
            square = field * field
            total[at, :cols] += square[:, :cols] + square[:, cols : 2 * cols]
            total[at, cols:] += square[:, 2 * cols :]

    value = scalars[15:16, :]
    inner = total[:, :cols]
    edge = total[:, cols:]
    edge = edge + turned(edge)
    right = right_lanes((rows, cols), radius)
    inside = (right & (tile[0] < tiles - 1)) | (jnp.logical_not(right) & (tile[0] > 0))
    outer = outer_lanes((half, cols), radius)
    for place, intensity in ((0, inner), (1, edge)):
        resist = jax.nn.sigmoid(resist_slope * (value * intensity - resist_level))
        slope = resist * (1.0 - resist) * (2.0 * resist_slope * value)
        if place:
            slope = jnp.where(inside, slope, 0.0)
        slope_ref[:, place * cols : (place + 1) * cols] = slope
        for n in range(nodes):
            rows_n = resist[n * share : (n + 1) * share]
            if place:
                image_ref[n, share:slab, :] = jnp.where(outer, rows_n[:half], rows_n[half:]).astype(bf16)
            else:
                image_ref[n, 0:share, :] = rows_n.astype(bf16)


def middle_kernel(radius, offset, images, wanted, before, after, scalars, pressure_ref):
    nodes, slab, cols = images.shape
    share = wanted.shape[1]
    step = slab - share
    right = right_lanes((step, cols), radius)
    for first in range(0, slab, step):
        image = [images[n, first : first + step, :].astype(f32) for n in range(nodes)]
        pressure = [None] * nodes
        for j in range(len(degrees)):
            weight = [scalars[16 * n + j : 16 * n + j + 1, :] for n in range(nodes)]
            coefficient = weight[0] * image[0]
            for n in range(1, nodes):
                coefficient = coefficient + weight[n] * image[n]
            if first < share:
                goal = wanted[j, first : first + step, :].astype(f32)
            else:
                at = pl.ds(offset + j * step, step)
                goal = jnp.where(right, after[at, :].astype(f32), before[at, :].astype(f32))
            mixed = scalars[16 * nodes + j : 16 * nodes + j + 1, :] * jnp.tanh(coefficient - goal)
            for n in range(nodes):
                term = weight[n] * mixed
                pressure[n] = term if j == 0 else pressure[n] + term
        for n in range(nodes):
            pressure_ref[n, first : first + step, :] = pressure[n]


def backward_kernel(radius, pressure, slope, fields, fh, fl, gr, gi, u, wave_hi, wave_lo, out_ref, dh, dl, scale):
    kernels, count, span = gr.shape
    nodes, slab, cols = pressure.shape
    rows = slope.shape[0]
    share = rows // nodes
    half = share // 2
    outer = outer_lanes((half, cols), radius)
    for n in range(nodes):
        at = pl.ds(n * share, share)
        scale[at, :cols] = slope[at, :cols] * pressure[n, :share, :]
        edge = pressure[n, share:, :]
        back = turned(edge)
        top, bottom = pl.ds(n * share, half), pl.ds(n * share + half, half)
        scale[top, cols:] = slope[top, cols:] * jnp.where(outer, edge, back)
        scale[bottom, cols:] = slope[bottom, cols:] * jnp.where(outer, back, edge)
    table = []
    for first in (0, count):
        table.append(jnp.concatenate([fh[first : first + count, : rows // 2], fl[first : first + count, : rows // 2]], 0))
    outer = outer_lanes((count, cols), radius)

    @pl.loop(0, kernels)
    def _(k):
        halves = []
        for first in (0, rows // 2):
            at = pl.ds(first, rows // 2)
            inner, edge = scale[at, :cols], scale[at, cols:]
            halves.append(fields[k, at, :] * jnp.concatenate([inner, inner, edge], 1))
        grads = []
        for lhs, value in zip(table, (halves[0] + halves[1], halves[0] - halves[1])):
            high, low = parts_of(value)
            prod = mm(lhs, high)
            grads.append(prod[:count] + prod[count:] + mm(lhs[:count], low))
        straight, crossed = grads
        edge, cross = straight[:, 2 * cols :], crossed[:, 2 * cols :]
        re_edge = jnp.where(outer, edge - turned(cross), 0.0)
        im_edge = jnp.where(outer, cross + turned(edge), 0.0)
        re = jnp.concatenate([straight[:, :cols] - crossed[:, cols : 2 * cols], re_edge], 1)
        im = jnp.concatenate([straight[:, cols : 2 * cols] + crossed[:, :cols], im_edge], 1)
        at = pl.multiple_of(2 * k * count, 2 * count)
        dh[pl.ds(at, count), :], dl[pl.ds(at, count), :] = parts_of(re)
        at = pl.multiple_of(at + count, count)
        dh[pl.ds(at, count), :], dl[pl.ds(at, count), :] = parts_of(im)

    wave = (wave_hi[...], wave_lo[...])
    a_re = jnp.zeros((count, span), f32)
    a_im = jnp.zeros((count, span), f32)
    for k in range(kernels):
        at = pl.ds(2 * k * count, 2 * count)
        q = mm3((dh[at, :], dl[at, :]), wave)
        b_re = q[:count, :span] + q[count:, span:]
        b_im = q[count:, :span] - q[:count, span:]
        a_re = a_re + gr[k] * b_re + gi[k] * b_im
        a_im = a_im + gr[k] * b_im - gi[k] * b_re
    near = [jnp.concatenate([w[:, 0:cols], w[:, span : span + cols]], 1) for w in (wave_hi, wave_lo)]
    prod = mm3(parts_of(jnp.concatenate([a_re, a_im], 0)), near)
    d_re = prod[:count, :cols] - prod[count:, cols:]
    d_im = prod[:count, cols:] + prod[count:, :cols]
    rest = jnp.zeros((128 - 2 * count, cols), f32)
    high, low = parts_of(jnp.concatenate([d_re, d_im, rest], 0))
    out_ref[...] = mm(u[...], jnp.concatenate([high, low, high], 0)) * (1.0 / math.sqrt(rows))


def shape_of(*shape, dtype=f32):
    return jax.ShapeDtypeStruct(shape, dtype)


def call(kernel, mebibytes, spaces, outs, scratch=()):
    return pl.pallas_call(
        kernel,
        in_specs=spaces,
        out_specs=[vmem] * len(outs),
        out_shape=list(outs),
        scratch_shapes=list(scratch),
        compiler_params=pltpu.CompilerParams(vmem_limit_bytes=mebibytes << 20),
    )


def kept(*arrays):
    return [pltpu.with_memory_space_constraint(a, pltpu.HBM) for a in arrays]


def local(mask, taps, weights, node_weights, node_index, freq, chaos, target):
    rows, cols = mask.shape
    kernels, count, tap_count = taps.shape[1], taps.shape[3], taps.shape[4]
    terms = target.shape[0]
    radius = (tap_count - 1) // 2
    span = 2 * cols
    nodes, tiles = lax.axis_size("node"), lax.axis_size("tile")
    node, tile = lax.axis_index("node").reshape(1), lax.axis_index("tile").reshape(1)
    share = rows // nodes
    half = share // 2
    slab = share + half
    up = [(i, i + 1) for i in range(tiles - 1)]
    down = [(i + 1, i) for i in range(tiles - 1)]
    wave_hi, wave_lo = (jnp.asarray(w) for w in column_waves(span))
    packed, wanted, fh, fl = call(
        functools.partial(spectrum_kernel, radius),
        8,
        [smem] + [hbm] * 3,
        [
            shape_of(4 * count + half * terms, cols, dtype=bf16),
            shape_of(terms, share, cols, dtype=bf16),
            shape_of(2 * count, rows, dtype=bf16),
            shape_of(2 * count, rows, dtype=bf16),
        ],
        [
            pltpu.SMEM(freq.shape, jnp.int32),
            pltpu.VMEM(mask.shape, f32),
            pltpu.VMEM((terms, share, cols), bf16),
            pltpu.SemaphoreType.DMA((3,)),
        ],
    )(node, *kept(freq, mask, target))
    before = lax.ppermute(packed, "tile", up)
    after = lax.ppermute(packed, "tile", down)
    u, cs, gr, gi, wave_hi, wave_lo, scalars = call(
        tables_kernel,
        16,
        [smem] + [hbm] * 8,
        [
            shape_of(rows, 384, dtype=bf16),
            shape_of(rows, 3 * count, dtype=bf16),
            shape_of(kernels, count, span),
            shape_of(kernels, count, span),
            shape_of(span, 2 * span, dtype=bf16),
            shape_of(span, 2 * span, dtype=bf16),
            shape_of(16 * nodes + 16, 128),
        ],
        [
            pltpu.SMEM(freq.shape, jnp.int32),
            pltpu.SMEM((2, nodes), jnp.int32),
            pltpu.SMEM((nodes,), f32),
            pltpu.SMEM(chaos.shape, f32),
            pltpu.VMEM(weights.shape, f32),
            pltpu.VMEM(taps.shape, f32),
            pltpu.SemaphoreType.DMA((8,)),
        ],
    )(node, *kept(freq, node_index.T, node_weights, chaos, weights, taps, wave_hi, wave_lo))
    image, slope, fields = call(
        functools.partial(forward_kernel, radius, tiles),
        20,
        [smem] + [vmem] * 9,
        [
            shape_of(nodes, slab, cols, dtype=bf16),
            shape_of(rows, 2 * cols),
            shape_of(kernels, rows, 3 * cols),
        ],
        [
            pltpu.VMEM((2 * kernels * count, span), bf16),
            pltpu.VMEM((2 * kernels * count, span), bf16),
            pltpu.VMEM((kernels, 2, 3 * count, 3 * cols), bf16),
            pltpu.VMEM((rows, 2 * cols), f32),
        ],
    )(tile, scalars, packed, before, after, gr, gi, cs, wave_hi, wave_lo)
    images = lax.all_to_all(image, "node", 0, 0)
    (pressure,) = call(
        functools.partial(middle_kernel, radius, 4 * count), 8, [vmem] * 5, [shape_of(nodes, slab, cols)]
    )(images, wanted, before, after, scalars)
    pressure = lax.all_to_all((pressure * 8192.0).astype(jnp.float16), "node", 0, 0).astype(f32) * (1.0 / 8192.0)
    (spread,) = call(
        functools.partial(backward_kernel, radius),
        16,
        [vmem] * 10,
        [shape_of(rows, cols)],
        [
            pltpu.VMEM((2 * kernels * count, span), bf16),
            pltpu.VMEM((2 * kernels * count, span), bf16),
            pltpu.VMEM((rows, 2 * cols), f32),
        ],
    )(pressure, slope, fields, fh, fl, gr, gi, u, wave_hi, wave_lo)
    return lax.all_to_all(spread.reshape(nodes, share, cols), "node", 0, 0).sum(0)


def solution(mesh):
    placed = (
        P(None, "tile"),
        P("node", None, None, None, None),
        P("node", None),
        P(),
        P(),
        P(),
        P(),
        P(None, None, "tile"),
    )
    return jax.shard_map(local, mesh=mesh, in_specs=placed, out_specs=P("node", "tile"), check_vma=False)
```

```python
import functools
import math

import jax
import jax.numpy as jnp
import ml_dtypes
import numpy as np
from jax import lax
from jax.experimental import pallas as pl
from jax.experimental.pallas import tpu as pltpu
from jax.sharding import PartitionSpec as P

LEVELS = 5
resist_slope = 4.0
resist_level = 0.6
degrees = [(d - q, q) for d in range(5) for q in range(d + 1)]
f32, bf16 = jnp.float32, jnp.bfloat16
vmem = pl.BlockSpec(memory_space=pltpu.VMEM)
smem = pl.BlockSpec(memory_space=pltpu.SMEM)
hbm = pl.BlockSpec(memory_space=pltpu.HBM)


def parts_of(value):
    high = value.astype(bf16)
    return high, (value - high.astype(f32)).astype(bf16)


def mm(a, b):
    return jnp.dot(a, b, preferred_element_type=f32)


def mm3(a, b):
    return mm(jnp.concatenate([a[0], a[0], a[1]], 1), jnp.concatenate([b[0], b[1], b[0]], 0))


def cosine(turn, period):
    turn = jnp.bitwise_and(turn, period - 1)
    half = jnp.minimum(turn, period - turn)
    far = half > period // 4
    angle = jnp.where(far, period // 2 - half, half).astype(f32) * (2.0 * math.pi / period)
    z = angle * angle
    poly = jnp.full_like(z, 1.0 / math.factorial(12))
    for order in (10, 8, 6, 4, 2, 0):
        sign = -1.0 if order % 4 == 2 else 1.0
        poly = poly * z + sign / math.factorial(order)
    return jnp.where(far, -poly, poly)


def column_waves(length):
    turn = (np.arange(length)[:, None] * np.arange(length)[None, :]) % length
    wave = np.concatenate([np.cos(2 * np.pi * turn / length), np.sin(2 * np.pi * turn / length)], 1)
    high = wave.astype(np.float32).astype(ml_dtypes.bfloat16)
    low = (wave - high.astype(np.float64)).astype(np.float32).astype(ml_dtypes.bfloat16)
    return high, low


def lanes(shape):
    return lax.broadcasted_iota(jnp.int32, shape, len(shape) - 1)


def turned(value):
    return pltpu.roll(value, value.shape[-1] // 2, len(value.shape) - 1)


def outer_lanes(shape, radius):
    lane = lanes(shape)
    return (lane < radius) | (lane >= shape[-1] - radius)


def right_lanes(shape, radius):
    lane, half = lanes(shape), shape[-1] // 2
    return (lane < radius) | ((lane >= half) & (lane < half + radius))


def spectrum_kernel(radius, node, freq_in, mask_in, target_in, packed_ref, wanted_ref, fh_ref, fl_ref, freq, mask, raw, sems):
    rows, cols = mask.shape
    count = freq.shape[0]
    terms, share = raw.shape[0], raw.shape[1]
    own = node[0]
    mirrored = own >= rows // (2 * share)
    at = jnp.where(mirrored, rows + rows // 2 - share - own * share, own * share)
    at = pl.multiple_of(at, share)
    moves = [(freq_in, freq), (mask_in, mask), (target_in.at[:, pl.ds(at, share), :], raw)]
    copies = [pltpu.make_async_copy(source, goal, sems.at[i]) for i, (source, goal) in enumerate(moves)]
    for copy in copies:
        copy.start()
    copies[0].wait()
    line = lax.broadcasted_iota(jnp.int32, (2 * count, 128), 0)
    f_freq = jnp.zeros((2 * count, 128), jnp.int32)
    for i in range(count):
        f_freq = jnp.where((line == i) | (line == i + count), freq[i], f_freq)
    f_full = jnp.concatenate([f_freq] * (rows // 128), 1)
    f_row = lax.broadcasted_iota(jnp.int32, (2 * count, rows), 0)
    turn = f_full * (2 * lanes((2 * count, rows)) + 1) + jnp.where(f_row >= count, rows // 2, 0)
    f_parts = parts_of(cosine(turn, 2 * rows))
    fh_ref[...], fl_ref[...] = f_parts
    copies[2].wait()
    row = lax.broadcasted_iota(jnp.int32, (share, share), 0)
    chosen = jnp.where(mirrored, share - 1 - row, row) == lanes((share, share))
    order = jnp.where(chosen, 1.0, 0.0).astype(bf16)
    half = share // 2
    outer = outer_lanes((half, cols), radius)
    for j in range(terms):
        goal = mm(order, raw[j])
        wanted_ref[j] = goal.astype(bf16)
        edge = jnp.where(outer, goal[:half], turned(goal[half:]))
        packed_ref[4 * count + half * j : 4 * count + half * (j + 1), :] = edge.astype(bf16)
    copies[1].wait()
    high, low = parts_of(mm3(f_parts, parts_of(mask[...])) * (1.0 / math.sqrt(rows)))
    packed_ref[0 : 2 * count, :] = high
    packed_ref[2 * count : 4 * count, :] = low


def tables_kernel(
    node, freq_in, index_in, node_weights_in, chaos_in, weights_in, taps_in, wave_hi_in, wave_lo_in,
    u_ref, cs_ref, gr_ref, gi_ref, wave_hi, wave_lo, scalars_ref,
    freq, index, node_weights, chaos, weights, taps, sems,
):
    rows = u_ref.shape[0]
    count = freq.shape[0]
    kernels, tap_count = taps.shape[1], taps.shape[4]
    span = wave_hi.shape[0]
    radius = (tap_count - 1) // 2
    nodes = index.shape[1]
    moves = [
        (freq_in, freq),
        (index_in, index),
        (node_weights_in, node_weights),
        (chaos_in, chaos),
        (weights_in, weights),
        (wave_hi_in, wave_hi),
        (wave_lo_in, wave_lo),
        (taps_in, taps),
    ]
    copies = [pltpu.make_async_copy(source, goal, sems.at[i]) for i, (source, goal) in enumerate(moves)]
    for copy in copies:
        copy.start()
    for copy in copies[:4]:
        copy.wait()
    lane = lanes((8, 256))
    u_freq = jnp.zeros((8, 256), jnp.int32)
    for i in range(count):
        u_freq = jnp.where((lane == i) | (lane == i + count) | (lane == i + 2 * count), freq[i], u_freq)
    quarter = rows // 2
    full = jnp.concatenate([u_freq[:, :128]] * (rows // 8), 0)
    u_lane = lanes((rows, 128))
    u_y = lax.broadcasted_iota(jnp.int32, (rows, 128), 0)
    table = cosine(full * (2 * u_y + 1) + jnp.where(u_lane >= count, quarter, 0), 2 * rows)
    high, low = parts_of(jnp.where(u_lane < 2 * count, table, 0.0))
    u_ref[:, 0:128] = high
    u_ref[:, 128:256] = high
    u_ref[:, 256:384] = low
    full = jnp.concatenate([u_freq] * (rows // 8), 0)
    c_row = lax.broadcasted_iota(jnp.int32, (rows, 256), 0)
    sine = c_row >= rows // 2
    c_y = jnp.where(sine, c_row - rows // 2, c_row)
    table = cosine(full * (2 * c_y + 1) - jnp.where(sine, quarter, 0), 2 * rows)
    high, low = parts_of(table)
    both = jnp.where(lanes((rows, 256)) < 2 * count, high.astype(f32), low.astype(f32))
    cs_ref[...] = both[:, : 3 * count].astype(bf16)
    for n in range(nodes):
        poly = []
        for axis in range(2):
            c = index[axis, n].astype(f32) * (2.0 / (LEVELS - 1)) - 1.0
            s = c * c
            poly.append([None, c, 1.5 * s - 0.5, (2.5 * s - 1.5) * c, (4.375 * s - 3.75) * s + 0.375])
        weight = node_weights[n]
        for j, (p, q) in enumerate(degrees):
            value = weight
            if p:
                value = value * poly[0][p]
            if q:
                value = value * poly[1][q]
            scalars_ref[16 * n + j : 16 * n + j + 1, :] = jnp.full((1, 128), value, f32)
    dose = 1.0 + 0.1 * (index[1, node[0]].astype(f32) * (2.0 / (LEVELS - 1)) - 1.0)
    scalars_ref[15:16, :] = jnp.full((1, 128), dose, f32)
    for j in range(len(degrees)):
        scalars_ref[16 * nodes + j : 16 * nodes + j + 1, :] = jnp.full((1, 128), chaos[j], f32)
    for copy in copies[4:]:
        copy.wait()
    side = [jnp.concatenate([w[span - radius : span], w[0 : tap_count - radius]], 0) for w in (wave_hi, wave_lo)]
    scale = jnp.sqrt(weights[...]) * (1.0 / (span * math.sqrt(count)))
    for k in range(kernels):
        parts = parts_of(taps[0, k].reshape(2 * count, tap_count))
        prod = mm3(parts, side)
        amount = scale[0:1, k : k + 1]
        gr_ref[k] = (prod[:count, :span] - prod[count:, span:]) * amount
        gi_ref[k] = (prod[:count, span:] + prod[count:, :span]) * amount


def forward_kernel(
    radius, tiles, tile, scalars, packed, after, before, gr, gi, cs, wave_hi, wave_lo,
    image_ref, slope_ref, fields_ref, bh, bl, x, total,
):
    kernels, count, span = gr.shape
    nodes, slab, cols = image_ref.shape
    rows = slope_ref.shape[0]
    share = rows // nodes
    half = share // 2
    near = lanes((2 * count, cols)) < 2 * radius
    pair = []
    for part in range(2):
        at = pl.ds(2 * part * count, 2 * count)
        beyond = jnp.where(near, after[at, :].astype(f32), before[at, :].astype(f32))
        pair.append(jnp.concatenate([packed[at, :], beyond.astype(bf16)], 1))
    wave = (wave_hi[...], wave_lo[...])
    prod = mm3(pair, wave)
    a_re = prod[:count, :span] + prod[count:, span:]
    a_im = prod[count:, :span] - prod[:count, span:]
    for k in range(kernels):
        b_re = gr[k] * a_re - gi[k] * a_im
        b_im = gr[k] * a_im + gi[k] * a_re
        for d, value in ((0, b_re), (1, b_im)):
            at = pl.ds((2 * k + d) * count, count)
            bh[at, :], bl[at, :] = parts_of(value)
    outer = outer_lanes((count, cols), radius)
    for k in range(kernels):
        if k % 2 == 0:
            at = pl.ds(2 * k * count, 2 * 2 * count)
            qq = mm3((bh[at, :], bl[at, :]), wave)
        q = qq[(k % 2) * 2 * count : (k % 2 + 1) * 2 * count]
        re = q[:count, :span] - q[count:, span:]
        im = q[:count, span:] + q[count:, :span]
        edge = jnp.where(outer, re[:, cols:], turned(im[:, cols:]))
        cross = jnp.where(outer, im[:, cols:], -turned(re[:, cols:]))
        straight = jnp.concatenate([re[:, :cols], im[:, :cols], edge], 1)
        crossed = jnp.concatenate([im[:, :cols], -re[:, :cols], cross], 1)
        for d, value in ((0, straight), (1, crossed)):
            high, low = parts_of(value)
            for place, part in ((0, high), (1, low), (2, high)):
                x[k, d, place * count : (place + 1) * count, :] = part
    total[...] = jnp.zeros(total.shape, f32)

    @pl.loop(0, kernels, unroll=True)
    def _(k):
        even = mm(cs[: rows // 2, :], x[k, 0])
        odd = mm(cs[rows // 2 :, :], x[k, 1])
        for first, field in ((0, even - odd), (rows // 2, even + odd)):
            at = pl.ds(first, rows // 2)
            fields_ref[k, at, :] = field
            square = field * field
            total[at, :cols] += square[:, :cols] + square[:, cols : 2 * cols]
            total[at, cols:] += square[:, 2 * cols :]

    value = scalars[15:16, :]
    inner = total[:, :cols]
    edge = total[:, cols:]
    edge = edge + turned(edge)
    right = right_lanes((rows, cols), radius)
    inside = (right & (tile[0] < tiles - 1)) | (jnp.logical_not(right) & (tile[0] > 0))
    outer = outer_lanes((half, cols), radius)
    for place, intensity in ((0, inner), (1, edge)):
        resist = jax.nn.sigmoid(resist_slope * (value * intensity - resist_level))
        slope = resist * (1.0 - resist) * (2.0 * resist_slope * value)
        if place:
            slope = jnp.where(inside, slope, 0.0)
        slope_ref[:, place * cols : (place + 1) * cols] = slope
        for n in range(nodes):
            rows_n = resist[n * share : (n + 1) * share]
            if place:
                image_ref[n, share:slab, :] = jnp.where(outer, rows_n[:half], rows_n[half:]).astype(bf16)
            else:
                image_ref[n, 0:share, :] = rows_n.astype(bf16)


def middle_kernel(radius, offset, images, wanted, after, before, scalars, pressure_ref):
    nodes, slab, cols = images.shape
    share = wanted.shape[1]
    step = slab - share
    right = right_lanes((step, cols), radius)
    for first in range(0, slab, step):
        image = [images[n, first : first + step, :].astype(f32) for n in range(nodes)]
        pressure = [None] * nodes
        for j in range(len(degrees)):
            weight = [scalars[16 * n + j : 16 * n + j + 1, :] for n in range(nodes)]
            coefficient = weight[0] * image[0]
            for n in range(1, nodes):
                coefficient = coefficient + weight[n] * image[n]
            if first < share:
                goal = wanted[j, first : first + step, :].astype(f32)
            else:
                at = pl.ds(offset + j * step, step)
                goal = jnp.where(right, after[at, :].astype(f32), before[at, :].astype(f32))
            mixed = scalars[16 * nodes + j : 16 * nodes + j + 1, :] * jnp.tanh(coefficient - goal)
            for n in range(nodes):
                term = weight[n] * mixed
                pressure[n] = term if j == 0 else pressure[n] + term
        for n in range(nodes):
            pressure_ref[n, first : first + step, :] = pressure[n]


def backward_kernel(radius, pressure, slope, fields, fh, fl, gr, gi, u, wave_hi, wave_lo, out_ref, dh, dl, scale):
    kernels, count, span = gr.shape
    nodes, slab, cols = pressure.shape
    rows = slope.shape[0]
    share = rows // nodes
    half = share // 2
    outer = outer_lanes((half, cols), radius)
    for n in range(nodes):
        at = pl.ds(n * share, share)
        scale[at, :cols] = slope[at, :cols] * pressure[n, :share, :]
        edge = pressure[n, share:, :]
        back = turned(edge)
        top, bottom = pl.ds(n * share, half), pl.ds(n * share + half, half)
        scale[top, cols:] = slope[top, cols:] * jnp.where(outer, edge, back)
        scale[bottom, cols:] = slope[bottom, cols:] * jnp.where(outer, back, edge)
    table = []
    for first in (0, count):
        table.append(jnp.concatenate([fh[first : first + count, : rows // 2], fl[first : first + count, : rows // 2]], 0))
    outer = outer_lanes((count, cols), radius)

    @pl.loop(0, kernels, unroll=True)
    def _(k):
        halves = []
        for first in (0, rows // 2):
            at = pl.ds(first, rows // 2)
            inner, edge = scale[at, :cols], scale[at, cols:]
            halves.append(fields[k, at, :] * jnp.concatenate([inner, inner, edge], 1))
        grads = []
        for lhs, value in zip(table, (halves[0] + halves[1], halves[0] - halves[1])):
            high, low = parts_of(value)
            prod = mm(lhs, high)
            grads.append(prod[:count] + prod[count:] + mm(lhs[:count], low))
        straight, crossed = grads
        edge, cross = straight[:, 2 * cols :], crossed[:, 2 * cols :]
        re_edge = jnp.where(outer, edge - turned(cross), 0.0)
        im_edge = jnp.where(outer, cross + turned(edge), 0.0)
        re = jnp.concatenate([straight[:, :cols] - crossed[:, cols : 2 * cols], re_edge], 1)
        im = jnp.concatenate([straight[:, cols : 2 * cols] + crossed[:, :cols], im_edge], 1)
        at = pl.multiple_of(2 * k * count, 2 * count)
        dh[pl.ds(at, count), :], dl[pl.ds(at, count), :] = parts_of(re)
        at = pl.multiple_of(at + count, count)
        dh[pl.ds(at, count), :], dl[pl.ds(at, count), :] = parts_of(im)

    wave = (wave_hi[...], wave_lo[...])
    a_re = jnp.zeros((count, span), f32)
    a_im = jnp.zeros((count, span), f32)
    for k in range(kernels):
        if k % 2 == 0:
            at = pl.ds(2 * k * count, 2 * 2 * count)
            qq = mm3((dh[at, :], dl[at, :]), wave)
        q = qq[(k % 2) * 2 * count : (k % 2 + 1) * 2 * count]
        b_re = q[:count, :span] + q[count:, span:]
        b_im = q[count:, :span] - q[:count, span:]
        a_re = a_re + gr[k] * b_re + gi[k] * b_im
        a_im = a_im + gr[k] * b_im - gi[k] * b_re
    near = [jnp.concatenate([w[:, 0:cols], w[:, span : span + cols]], 1) for w in (wave_hi, wave_lo)]
    prod = mm3(parts_of(jnp.concatenate([a_re, a_im], 0)), near)
    d_re = prod[:count, :cols] - prod[count:, cols:]
    d_im = prod[:count, cols:] + prod[count:, :cols]
    rest = jnp.zeros((128 - 2 * count, cols), f32)
    high, low = parts_of(jnp.concatenate([d_re, d_im, rest], 0))
    out_ref[...] = mm(u[...], jnp.concatenate([high, low, high], 0)) * (1.0 / math.sqrt(rows))


def shape_of(*shape, dtype=f32):
    return jax.ShapeDtypeStruct(shape, dtype)


def call(kernel, mebibytes, spaces, outs, scratch=()):
    return pl.pallas_call(
        kernel,
        in_specs=spaces,
        out_specs=[vmem] * len(outs),
        out_shape=list(outs),
        scratch_shapes=list(scratch),
        compiler_params=pltpu.CompilerParams(vmem_limit_bytes=mebibytes << 20),
    )


def kept(*arrays):
    return [pltpu.with_memory_space_constraint(a, pltpu.HBM) for a in arrays]


def local(mask, taps, weights, node_weights, node_index, freq, chaos, target):
    rows, cols = mask.shape
    kernels, count, tap_count = taps.shape[1], taps.shape[3], taps.shape[4]
    terms = target.shape[0]
    radius = (tap_count - 1) // 2
    span = 2 * cols
    nodes, tiles = lax.axis_size("node"), lax.axis_size("tile")
    node, tile = lax.axis_index("node").reshape(1), lax.axis_index("tile").reshape(1)
    share = rows // nodes
    half = share // 2
    slab = share + half
    up = [(i, i + 1) for i in range(tiles - 1)]
    down = [(i + 1, i) for i in range(tiles - 1)]
    wave_hi, wave_lo = (jnp.asarray(w) for w in column_waves(span))
    packed, wanted, fh, fl = call(
        functools.partial(spectrum_kernel, radius),
        8,
        [smem] + [hbm] * 3,
        [
            shape_of(4 * count + half * terms, cols, dtype=bf16),
            shape_of(terms, share, cols, dtype=bf16),
            shape_of(2 * count, rows, dtype=bf16),
            shape_of(2 * count, rows, dtype=bf16),
        ],
        [
            pltpu.SMEM(freq.shape, jnp.int32),
            pltpu.VMEM(mask.shape, f32),
            pltpu.VMEM((terms, share, cols), bf16),
            pltpu.SemaphoreType.DMA((3,)),
        ],
    )(node, *kept(freq, mask, target))
    after = lax.ppermute(packed, "tile", down)
    before = lax.ppermute(packed, "tile", up)
    u, cs, gr, gi, wave_hi, wave_lo, scalars = call(
        tables_kernel,
        16,
        [smem] + [hbm] * 8,
        [
            shape_of(rows, 384, dtype=bf16),
            shape_of(rows, 3 * count, dtype=bf16),
            shape_of(kernels, count, span),
            shape_of(kernels, count, span),
            shape_of(span, 2 * span, dtype=bf16),
            shape_of(span, 2 * span, dtype=bf16),
            shape_of(16 * nodes + 16, 128),
        ],
        [
            pltpu.SMEM(freq.shape, jnp.int32),
            pltpu.SMEM((2, nodes), jnp.int32),
            pltpu.SMEM((nodes,), f32),
            pltpu.SMEM(chaos.shape, f32),
            pltpu.VMEM(weights.shape, f32),
            pltpu.VMEM(taps.shape, f32),
            pltpu.SemaphoreType.DMA((8,)),
        ],
    )(node, *kept(freq, node_index.T, node_weights, chaos, weights, taps, wave_hi, wave_lo))
    image, slope, fields = call(
        functools.partial(forward_kernel, radius, tiles),
        20,
        [smem] + [vmem] * 9,
        [
            shape_of(nodes, slab, cols, dtype=bf16),
            shape_of(rows, 2 * cols),
            shape_of(kernels, rows, 3 * cols),
        ],
        [
            pltpu.VMEM((2 * kernels * count, span), bf16),
            pltpu.VMEM((2 * kernels * count, span), bf16),
            pltpu.VMEM((kernels, 2, 3 * count, 3 * cols), bf16),
            pltpu.VMEM((rows, 2 * cols), f32),
        ],
    )(tile, scalars, packed, after, before, gr, gi, cs, wave_hi, wave_lo)
    images = lax.all_to_all(image, "node", 0, 0)
    (pressure,) = call(
        functools.partial(middle_kernel, radius, 4 * count), 8, [vmem] * 5, [shape_of(nodes, slab, cols)]
    )(images, wanted, after, before, scalars)
    pressure = lax.all_to_all((pressure * 8192.0).astype(jnp.float16), "node", 0, 0).astype(f32) * (1.0 / 8192.0)
    (spread,) = call(
        functools.partial(backward_kernel, radius),
        16,
        [vmem] * 10,
        [shape_of(rows, cols)],
        [
            pltpu.VMEM((2 * kernels * count, span), bf16),
            pltpu.VMEM((2 * kernels * count, span), bf16),
            pltpu.VMEM((rows, 2 * cols), f32),
        ],
    )(pressure, slope, fields, fh, fl, gr, gi, u, wave_hi, wave_lo)
    return lax.all_to_all(spread.reshape(nodes, share, cols), "node", 0, 0).sum(0)


def solution(mesh):
    placed = (
        P(None, "tile"),
        P("node", None, None, None, None),
        P("node", None),
        P(),
        P(),
        P(),
        P(),
        P(None, None, "tile"),
    )
    return jax.shard_map(local, mesh=mesh, in_specs=placed, out_specs=P("node", "tile"), check_vma=False)
```

```python
import functools
import math

import jax
import jax.numpy as jnp
import ml_dtypes
import numpy as np
from jax import lax
from jax.experimental import pallas as pl
from jax.experimental.pallas import tpu as pltpu
from jax.sharding import PartitionSpec as P

LEVELS = 5
resist_slope = 4.0
resist_level = 0.6
degrees = [(d - q, q) for d in range(5) for q in range(d + 1)]
f32, bf16 = jnp.float32, jnp.bfloat16
vmem = pl.BlockSpec(memory_space=pltpu.VMEM)
smem = pl.BlockSpec(memory_space=pltpu.SMEM)
hbm = pl.BlockSpec(memory_space=pltpu.HBM)


def parts_of(value):
    high = value.astype(bf16)
    return high, (value - high.astype(f32)).astype(bf16)


def mm(a, b):
    return jnp.dot(a, b, preferred_element_type=f32)


def mm3(a, b):
    return mm(jnp.concatenate([a[0], a[0], a[1]], 1), jnp.concatenate([b[0], b[1], b[0]], 0))


def cosine(turn, period):
    turn = jnp.bitwise_and(turn, period - 1)
    half = jnp.minimum(turn, period - turn)
    far = half > period // 4
    angle = jnp.where(far, period // 2 - half, half).astype(f32) * (2.0 * math.pi / period)
    z = angle * angle
    poly = jnp.full_like(z, 1.0 / math.factorial(12))
    for order in (10, 8, 6, 4, 2, 0):
        sign = -1.0 if order % 4 == 2 else 1.0
        poly = poly * z + sign / math.factorial(order)
    return jnp.where(far, -poly, poly)


def column_waves(length):
    turn = (np.arange(length)[:, None] * np.arange(length)[None, :]) % length
    wave = np.concatenate([np.cos(2 * np.pi * turn / length), np.sin(2 * np.pi * turn / length)], 1)
    high = wave.astype(np.float32).astype(ml_dtypes.bfloat16)
    low = (wave - high.astype(np.float64)).astype(np.float32).astype(ml_dtypes.bfloat16)
    return high, low


def lanes(shape):
    return lax.broadcasted_iota(jnp.int32, shape, len(shape) - 1)


def turned(value):
    return pltpu.roll(value, value.shape[-1] // 2, len(value.shape) - 1)


def outer_lanes(shape, radius):
    lane = lanes(shape)
    return (lane < radius) | (lane >= shape[-1] - radius)


def right_lanes(shape, radius):
    lane, half = lanes(shape), shape[-1] // 2
    return (lane < radius) | ((lane >= half) & (lane < half + radius))


def spectrum_kernel(radius, node, freq_in, mask_in, target_in, packed_ref, wanted_ref, fh_ref, fl_ref, freq, mask, raw, sems):
    rows, cols = mask.shape
    count = freq.shape[0]
    terms, share = raw.shape[0], raw.shape[1]
    own = node[0]
    mirrored = own >= rows // (2 * share)
    at = jnp.where(mirrored, rows + rows // 2 - share - own * share, own * share)
    at = pl.multiple_of(at, share)
    moves = [(freq_in, freq), (mask_in, mask), (target_in.at[:, pl.ds(at, share), :], raw)]
    copies = [pltpu.make_async_copy(source, goal, sems.at[i]) for i, (source, goal) in enumerate(moves)]
    for copy in copies:
        copy.start()
    copies[0].wait()
    line = lax.broadcasted_iota(jnp.int32, (2 * count, 128), 0)
    f_freq = jnp.zeros((2 * count, 128), jnp.int32)
    for i in range(count):
        f_freq = jnp.where((line == i) | (line == i + count), freq[i], f_freq)
    f_full = jnp.concatenate([f_freq] * (rows // 128), 1)
    f_row = lax.broadcasted_iota(jnp.int32, (2 * count, rows), 0)
    turn = f_full * (2 * lanes((2 * count, rows)) + 1) + jnp.where(f_row >= count, rows // 2, 0)
    f_parts = parts_of(cosine(turn, 2 * rows))
    fh_ref[...], fl_ref[...] = f_parts
    copies[2].wait()
    row = lax.broadcasted_iota(jnp.int32, (share, share), 0)
    chosen = jnp.where(mirrored, share - 1 - row, row) == lanes((share, share))
    order = jnp.where(chosen, 1.0, 0.0).astype(bf16)
    half = share // 2
    outer = outer_lanes((half, cols), radius)
    for j in range(terms):
        goal = mm(order, raw[j])
        wanted_ref[j] = goal.astype(bf16)
        edge = jnp.where(outer, goal[:half], turned(goal[half:]))
        packed_ref[4 * count + half * j : 4 * count + half * (j + 1), :] = edge.astype(bf16)
    copies[1].wait()
    high, low = parts_of(mm3(f_parts, parts_of(mask[...])) * (1.0 / math.sqrt(rows)))
    packed_ref[0 : 2 * count, :] = high
    packed_ref[2 * count : 4 * count, :] = low


def tables_kernel(
    node, freq_in, index_in, node_weights_in, chaos_in, weights_in, taps_in, wave_hi_in, wave_lo_in,
    u_ref, cs_ref, gr_ref, gi_ref, wave_hi, wave_lo, scalars_ref,
    freq, index, node_weights, chaos, weights, taps, sems,
):
    rows = u_ref.shape[0]
    count = freq.shape[0]
    kernels, tap_count = taps.shape[1], taps.shape[4]
    span = wave_hi.shape[0]
    radius = (tap_count - 1) // 2
    nodes = index.shape[1]
    moves = [
        (freq_in, freq),
        (index_in, index),
        (node_weights_in, node_weights),
        (chaos_in, chaos),
        (weights_in, weights),
        (wave_hi_in, wave_hi),
        (wave_lo_in, wave_lo),
        (taps_in, taps),
    ]
    copies = [pltpu.make_async_copy(source, goal, sems.at[i]) for i, (source, goal) in enumerate(moves)]
    for copy in copies:
        copy.start()
    for copy in copies[:4]:
        copy.wait()
    lane = lanes((8, 256))
    u_freq = jnp.zeros((8, 256), jnp.int32)
    for i in range(count):
        u_freq = jnp.where((lane == i) | (lane == i + count) | (lane == i + 2 * count), freq[i], u_freq)
    quarter = rows // 2
    full = jnp.concatenate([u_freq[:, :128]] * (rows // 8), 0)
    u_lane = lanes((rows, 128))
    u_y = lax.broadcasted_iota(jnp.int32, (rows, 128), 0)
    table = cosine(full * (2 * u_y + 1) + jnp.where(u_lane >= count, quarter, 0), 2 * rows)
    high, low = parts_of(jnp.where(u_lane < 2 * count, table, 0.0))
    u_ref[:, 0:128] = high
    u_ref[:, 128:256] = high
    u_ref[:, 256:384] = low
    full = jnp.concatenate([u_freq] * (rows // 8), 0)
    c_row = lax.broadcasted_iota(jnp.int32, (rows, 256), 0)
    sine = c_row >= rows // 2
    c_y = jnp.where(sine, c_row - rows // 2, c_row)
    table = cosine(full * (2 * c_y + 1) - jnp.where(sine, quarter, 0), 2 * rows)
    high, low = parts_of(table)
    both = jnp.where(lanes((rows, 256)) < 2 * count, high.astype(f32), low.astype(f32))
    cs_ref[...] = both[:, : 3 * count].astype(bf16)
    for n in range(nodes):
        poly = []
        for axis in range(2):
            c = index[axis, n].astype(f32) * (2.0 / (LEVELS - 1)) - 1.0
            s = c * c
            poly.append([None, c, 1.5 * s - 0.5, (2.5 * s - 1.5) * c, (4.375 * s - 3.75) * s + 0.375])
        weight = node_weights[n]
        for j, (p, q) in enumerate(degrees):
            value = weight
            if p:
                value = value * poly[0][p]
            if q:
                value = value * poly[1][q]
            scalars_ref[16 * n + j : 16 * n + j + 1, :] = jnp.full((1, 128), value, f32)
    dose = 1.0 + 0.1 * (index[1, node[0]].astype(f32) * (2.0 / (LEVELS - 1)) - 1.0)
    scalars_ref[15:16, :] = jnp.full((1, 128), dose, f32)
    for j in range(len(degrees)):
        scalars_ref[16 * nodes + j : 16 * nodes + j + 1, :] = jnp.full((1, 128), chaos[j], f32)
    for copy in copies[4:]:
        copy.wait()
    side = [jnp.concatenate([w[span - radius : span], w[0 : tap_count - radius]], 0) for w in (wave_hi, wave_lo)]
    scale = jnp.sqrt(weights[...]) * (1.0 / (span * math.sqrt(count)))
    for k in range(kernels):
        parts = parts_of(taps[0, k].reshape(2 * count, tap_count))
        prod = mm3(parts, side)
        amount = scale[0:1, k : k + 1]
        gr_ref[k] = (prod[:count, :span] - prod[count:, span:]) * amount
        gi_ref[k] = (prod[:count, span:] + prod[count:, :span]) * amount


def forward_kernel(
    radius, tiles, tile, scalars, packed, twin, border, gr, gi, cs, wave_hi, wave_lo,
    image_ref, slope_ref, fields_ref, bh, bl, x, total,
):
    kernels, count, span = gr.shape
    nodes, slab, cols = image_ref.shape
    rows = slope_ref.shape[0]
    share = rows // nodes
    half = share // 2
    even = lax.rem(tile[0], 2) == 0
    near = (lanes((2 * count, cols)) < 2 * radius) == even
    pair = []
    for part in range(2):
        at = pl.ds(2 * part * count, 2 * count)
        beyond = jnp.where(near, twin[at, :].astype(f32), border[at, :].astype(f32))
        pair.append(jnp.concatenate([packed[at, :], beyond.astype(bf16)], 1))
    wave = (wave_hi[...], wave_lo[...])
    prod = mm3(pair, wave)
    a_re = prod[:count, :span] + prod[count:, span:]
    a_im = prod[count:, :span] - prod[:count, span:]
    for k in range(kernels):
        b_re = gr[k] * a_re - gi[k] * a_im
        b_im = gr[k] * a_im + gi[k] * a_re
        for d, value in ((0, b_re), (1, b_im)):
            at = pl.ds((2 * k + d) * count, count)
            bh[at, :], bl[at, :] = parts_of(value)
    outer = outer_lanes((count, cols), radius)
    for k in range(kernels):
        if k % 2 == 0:
            at = pl.ds(2 * k * count, 2 * 2 * count)
            qq = mm3((bh[at, :], bl[at, :]), wave)
        q = qq[(k % 2) * 2 * count : (k % 2 + 1) * 2 * count]
        re = q[:count, :span] - q[count:, span:]
        im = q[:count, span:] + q[count:, :span]
        edge = jnp.where(outer, re[:, cols:], turned(im[:, cols:]))
        cross = jnp.where(outer, im[:, cols:], -turned(re[:, cols:]))
        straight = jnp.concatenate([re[:, :cols], im[:, :cols], edge], 1)
        crossed = jnp.concatenate([im[:, :cols], -re[:, :cols], cross], 1)
        for d, value in ((0, straight), (1, crossed)):
            high, low = parts_of(value)
            for place, part in ((0, high), (1, low), (2, high)):
                x[k, d, place * count : (place + 1) * count, :] = part
    total[...] = jnp.zeros(total.shape, f32)

    @pl.loop(0, kernels, unroll=True)
    def _(k):
        even = mm(cs[: rows // 2, :], x[k, 0])
        odd = mm(cs[rows // 2 :, :], x[k, 1])
        for first, field in ((0, even - odd), (rows // 2, even + odd)):
            at = pl.ds(first, rows // 2)
            fields_ref[k, at, :] = field
            square = field * field
            total[at, :cols] += square[:, :cols] + square[:, cols : 2 * cols]
            total[at, cols:] += square[:, 2 * cols :]

    value = scalars[15:16, :]
    inner = total[:, :cols]
    edge = total[:, cols:]
    edge = edge + turned(edge)
    right = right_lanes((rows, cols), radius)
    inside = (right & (tile[0] < tiles - 1)) | (jnp.logical_not(right) & (tile[0] > 0))
    outer = outer_lanes((half, cols), radius)
    for place, intensity in ((0, inner), (1, edge)):
        resist = jax.nn.sigmoid(resist_slope * (value * intensity - resist_level))
        slope = resist * (1.0 - resist) * (2.0 * resist_slope * value)
        if place:
            slope = jnp.where(inside, slope, 0.0)
        slope_ref[:, place * cols : (place + 1) * cols] = slope
        for n in range(nodes):
            rows_n = resist[n * share : (n + 1) * share]
            if place:
                image_ref[n, share:slab, :] = jnp.where(outer, rows_n[:half], rows_n[half:]).astype(bf16)
            else:
                image_ref[n, 0:share, :] = rows_n.astype(bf16)


def middle_kernel(radius, offset, tile, images, wanted, twin, border, scalars, pressure_ref):
    nodes, slab, cols = images.shape
    share = wanted.shape[1]
    step = slab - share
    near = right_lanes((step, cols), radius) == (lax.rem(tile[0], 2) == 0)
    for first in range(0, slab, step):
        image = [images[n, first : first + step, :].astype(f32) for n in range(nodes)]
        pressure = [None] * nodes
        for j in range(len(degrees)):
            weight = [scalars[16 * n + j : 16 * n + j + 1, :] for n in range(nodes)]
            coefficient = weight[0] * image[0]
            for n in range(1, nodes):
                coefficient = coefficient + weight[n] * image[n]
            if first < share:
                goal = wanted[j, first : first + step, :].astype(f32)
            else:
                at = pl.ds(offset + j * step, step)
                goal = jnp.where(near, twin[at, :].astype(f32), border[at, :].astype(f32))
            mixed = scalars[16 * nodes + j : 16 * nodes + j + 1, :] * jnp.tanh(coefficient - goal)
            for n in range(nodes):
                term = weight[n] * mixed
                pressure[n] = term if j == 0 else pressure[n] + term
        for n in range(nodes):
            pressure_ref[n, first : first + step, :] = pressure[n]


def backward_kernel(radius, pressure, slope, fields, fh, fl, gr, gi, u, wave_hi, wave_lo, out_ref, dh, dl, scale):
    kernels, count, span = gr.shape
    nodes, slab, cols = pressure.shape
    rows = slope.shape[0]
    share = rows // nodes
    half = share // 2
    outer = outer_lanes((half, cols), radius)
    for n in range(nodes):
        at = pl.ds(n * share, share)
        scale[at, :cols] = slope[at, :cols] * pressure[n, :share, :]
        edge = pressure[n, share:, :]
        back = turned(edge)
        top, bottom = pl.ds(n * share, half), pl.ds(n * share + half, half)
        scale[top, cols:] = slope[top, cols:] * jnp.where(outer, edge, back)
        scale[bottom, cols:] = slope[bottom, cols:] * jnp.where(outer, back, edge)
    table = []
    for first in (0, count):
        table.append(jnp.concatenate([fh[first : first + count, : rows // 2], fl[first : first + count, : rows // 2]], 0))
    outer = outer_lanes((count, cols), radius)

    @pl.loop(0, kernels, unroll=True)
    def _(k):
        halves = []
        for first in (0, rows // 2):
            at = pl.ds(first, rows // 2)
            inner, edge = scale[at, :cols], scale[at, cols:]
            halves.append(fields[k, at, :] * jnp.concatenate([inner, inner, edge], 1))
        grads = []
        for lhs, value in zip(table, (halves[0] + halves[1], halves[0] - halves[1])):
            high, low = parts_of(value)
            prod = mm(lhs, high)
            grads.append(prod[:count] + prod[count:] + mm(lhs[:count], low))
        straight, crossed = grads
        edge, cross = straight[:, 2 * cols :], crossed[:, 2 * cols :]
        re_edge = jnp.where(outer, edge - turned(cross), 0.0)
        im_edge = jnp.where(outer, cross + turned(edge), 0.0)
        re = jnp.concatenate([straight[:, :cols] - crossed[:, cols : 2 * cols], re_edge], 1)
        im = jnp.concatenate([straight[:, cols : 2 * cols] + crossed[:, :cols], im_edge], 1)
        at = pl.multiple_of(2 * k * count, 2 * count)
        dh[pl.ds(at, count), :], dl[pl.ds(at, count), :] = parts_of(re)
        at = pl.multiple_of(at + count, count)
        dh[pl.ds(at, count), :], dl[pl.ds(at, count), :] = parts_of(im)

    wave = (wave_hi[...], wave_lo[...])
    a_re = jnp.zeros((count, span), f32)
    a_im = jnp.zeros((count, span), f32)
    for k in range(kernels):
        if k % 2 == 0:
            at = pl.ds(2 * k * count, 2 * 2 * count)
            qq = mm3((dh[at, :], dl[at, :]), wave)
        q = qq[(k % 2) * 2 * count : (k % 2 + 1) * 2 * count]
        b_re = q[:count, :span] + q[count:, span:]
        b_im = q[count:, :span] - q[:count, span:]
        a_re = a_re + gr[k] * b_re + gi[k] * b_im
        a_im = a_im + gr[k] * b_im - gi[k] * b_re
    near = [jnp.concatenate([w[:, 0:cols], w[:, span : span + cols]], 1) for w in (wave_hi, wave_lo)]
    prod = mm3(parts_of(jnp.concatenate([a_re, a_im], 0)), near)
    d_re = prod[:count, :cols] - prod[count:, cols:]
    d_im = prod[:count, cols:] + prod[count:, :cols]
    rest = jnp.zeros((128 - 2 * count, cols), f32)
    high, low = parts_of(jnp.concatenate([d_re, d_im, rest], 0))
    out_ref[...] = mm(u[...], jnp.concatenate([high, low, high], 0)) * (1.0 / math.sqrt(rows))


def shape_of(*shape, dtype=f32):
    return jax.ShapeDtypeStruct(shape, dtype)


def call(kernel, mebibytes, spaces, outs, scratch=()):
    return pl.pallas_call(
        kernel,
        in_specs=spaces,
        out_specs=[vmem] * len(outs),
        out_shape=list(outs),
        scratch_shapes=list(scratch),
        compiler_params=pltpu.CompilerParams(vmem_limit_bytes=mebibytes << 20),
    )


def kept(*arrays):
    return [pltpu.with_memory_space_constraint(a, pltpu.HBM) for a in arrays]


def local(mask, taps, weights, node_weights, node_index, freq, chaos, target):
    rows, cols = mask.shape
    kernels, count, tap_count = taps.shape[1], taps.shape[3], taps.shape[4]
    terms = target.shape[0]
    radius = (tap_count - 1) // 2
    span = 2 * cols
    nodes, tiles = lax.axis_size("node"), lax.axis_size("tile")
    node, tile = lax.axis_index("node").reshape(1), lax.axis_index("tile").reshape(1)
    share = rows // nodes
    half = share // 2
    slab = share + half
    inside = [(i, i ^ 1) for i in range(tiles) if i ^ 1 < tiles]
    across = [(i, ((i + 1) ^ 1) - 1) for i in range(tiles) if 0 <= ((i + 1) ^ 1) - 1 < tiles]
    wave_hi, wave_lo = (jnp.asarray(w) for w in column_waves(span))
    packed, wanted, fh, fl = call(
        functools.partial(spectrum_kernel, radius),
        8,
        [smem] + [hbm] * 3,
        [
            shape_of(4 * count + half * terms, cols, dtype=bf16),
            shape_of(terms, share, cols, dtype=bf16),
            shape_of(2 * count, rows, dtype=bf16),
            shape_of(2 * count, rows, dtype=bf16),
        ],
        [
            pltpu.SMEM(freq.shape, jnp.int32),
            pltpu.VMEM(mask.shape, f32),
            pltpu.VMEM((terms, share, cols), bf16),
            pltpu.SemaphoreType.DMA((3,)),
        ],
    )(node, *kept(freq, mask, target))
    border = lax.ppermute(packed, "tile", across)
    twin = lax.ppermute(packed, "tile", inside)
    u, cs, gr, gi, wave_hi, wave_lo, scalars = call(
        tables_kernel,
        16,
        [smem] + [hbm] * 8,
        [
            shape_of(rows, 384, dtype=bf16),
            shape_of(rows, 3 * count, dtype=bf16),
            shape_of(kernels, count, span),
            shape_of(kernels, count, span),
            shape_of(span, 2 * span, dtype=bf16),
            shape_of(span, 2 * span, dtype=bf16),
            shape_of(16 * nodes + 16, 128),
        ],
        [
            pltpu.SMEM(freq.shape, jnp.int32),
            pltpu.SMEM((2, nodes), jnp.int32),
            pltpu.SMEM((nodes,), f32),
            pltpu.SMEM(chaos.shape, f32),
            pltpu.VMEM(weights.shape, f32),
            pltpu.VMEM(taps.shape, f32),
            pltpu.SemaphoreType.DMA((8,)),
        ],
    )(node, *kept(freq, node_index.T, node_weights, chaos, weights, taps, wave_hi, wave_lo))
    image, slope, fields = call(
        functools.partial(forward_kernel, radius, tiles),
        20,
        [smem] + [vmem] * 9,
        [
            shape_of(nodes, slab, cols, dtype=bf16),
            shape_of(rows, 2 * cols),
            shape_of(kernels, rows, 3 * cols),
        ],
        [
            pltpu.VMEM((2 * kernels * count, span), bf16),
            pltpu.VMEM((2 * kernels * count, span), bf16),
            pltpu.VMEM((kernels, 2, 3 * count, 3 * cols), bf16),
            pltpu.VMEM((rows, 2 * cols), f32),
        ],
    )(tile, scalars, packed, twin, border, gr, gi, cs, wave_hi, wave_lo)
    images = lax.all_to_all(image, "node", 0, 0)
    (pressure,) = call(
        functools.partial(middle_kernel, radius, 4 * count), 8, [smem] + [vmem] * 5, [shape_of(nodes, slab, cols)]
    )(tile, images, wanted, twin, border, scalars)
    pressure = lax.all_to_all((pressure * 8192.0).astype(jnp.float16), "node", 0, 0).astype(f32) * (1.0 / 8192.0)
    (spread,) = call(
        functools.partial(backward_kernel, radius),
        16,
        [vmem] * 10,
        [shape_of(rows, cols)],
        [
            pltpu.VMEM((2 * kernels * count, span), bf16),
            pltpu.VMEM((2 * kernels * count, span), bf16),
            pltpu.VMEM((rows, 2 * cols), f32),
        ],
    )(pressure, slope, fields, fh, fl, gr, gi, u, wave_hi, wave_lo)
    return lax.all_to_all(spread.reshape(nodes, share, cols), "node", 0, 0).sum(0)


def solution(mesh):
    placed = (
        P(None, "tile"),
        P("node", None, None, None, None),
        P("node", None),
        P(),
        P(),
        P(),
        P(),
        P(None, None, "tile"),
    )
    return jax.shard_map(local, mesh=mesh, in_specs=placed, out_specs=P("node", "tile"), check_vma=False)
```

```python
import functools
import math

import jax
import jax.numpy as jnp
import ml_dtypes
import numpy as np
from jax import lax
from jax.experimental import pallas as pl
from jax.experimental.pallas import tpu as pltpu
from jax.sharding import PartitionSpec as P

LEVELS = 5
resist_slope = 4.0
resist_level = 0.6
degrees = [(d - q, q) for d in range(5) for q in range(d + 1)]
f32, bf16 = jnp.float32, jnp.bfloat16
vmem = pl.BlockSpec(memory_space=pltpu.VMEM)
smem = pl.BlockSpec(memory_space=pltpu.SMEM)
hbm = pl.BlockSpec(memory_space=pltpu.HBM)


def parts_of(value):
    high = value.astype(bf16)
    return high, (value - high.astype(f32)).astype(bf16)


def mm(a, b):
    return jnp.dot(a, b, preferred_element_type=f32)


def mm3(a, b):
    return mm(jnp.concatenate([a[0], a[0], a[1]], 1), jnp.concatenate([b[0], b[1], b[0]], 0))


def cosine(turn, period):
    turn = jnp.bitwise_and(turn, period - 1)
    half = jnp.minimum(turn, period - turn)
    far = half > period // 4
    angle = jnp.where(far, period // 2 - half, half).astype(f32) * (2.0 * math.pi / period)
    z = angle * angle
    poly = jnp.full_like(z, 1.0 / math.factorial(12))
    for order in (10, 8, 6, 4, 2, 0):
        sign = -1.0 if order % 4 == 2 else 1.0
        poly = poly * z + sign / math.factorial(order)
    return jnp.where(far, -poly, poly)


def column_waves(length):
    turn = (np.arange(length)[:, None] * np.arange(length)[None, :]) % length
    wave = np.concatenate([np.cos(2 * np.pi * turn / length), np.sin(2 * np.pi * turn / length)], 1)
    high = wave.astype(np.float32).astype(ml_dtypes.bfloat16)
    low = (wave - high.astype(np.float64)).astype(np.float32).astype(ml_dtypes.bfloat16)
    return high, low


def lanes(shape):
    return lax.broadcasted_iota(jnp.int32, shape, len(shape) - 1)


def turned(value):
    return pltpu.roll(value, value.shape[-1] // 2, len(value.shape) - 1)


def outer_lanes(shape, radius):
    lane = lanes(shape)
    return (lane < radius) | (lane >= shape[-1] - radius)


def right_lanes(shape, radius):
    lane, half = lanes(shape), shape[-1] // 2
    return (lane < radius) | ((lane >= half) & (lane < half + radius))


def first_kernel(
    radius, node, freq_in, index_in, node_weights_in, chaos_in, target_in, mask_in, wave_hi_in, wave_lo_in, taps_in, weights_in,
    packed_ref, wanted_ref, fh_ref, fl_ref, freq_ref, scalars_ref, wave_hi, wave_lo, taps, weights,
    freq, index, node_weights, chaos, raw, mask, sems,
):
    rows, cols = mask.shape
    count = freq.shape[0]
    terms, share = raw.shape[0], raw.shape[1]
    nodes = index.shape[1]
    own = node[0]
    mirrored = own >= rows // (2 * share)
    at = jnp.where(mirrored, rows + rows // 2 - share - own * share, own * share)
    at = pl.multiple_of(at, share)
    moves = [
        (freq_in, freq),
        (index_in, index),
        (node_weights_in, node_weights),
        (chaos_in, chaos),
        (target_in.at[:, pl.ds(at, share), :], raw),
        (mask_in, mask),
        (wave_hi_in, wave_hi),
        (wave_lo_in, wave_lo),
        (taps_in, taps),
        (weights_in, weights),
    ]
    copies = [pltpu.make_async_copy(source, goal, sems.at[i]) for i, (source, goal) in enumerate(moves)]
    for copy in copies:
        copy.start()
    for copy in copies[:4]:
        copy.wait()
    line = lax.broadcasted_iota(jnp.int32, (2 * count, 128), 0)
    f_freq = jnp.zeros((2 * count, 128), jnp.int32)
    lane = lanes((8, 256))
    u_freq = jnp.zeros((8, 256), jnp.int32)
    for i in range(count):
        f_freq = jnp.where((line == i) | (line == i + count), freq[i], f_freq)
        u_freq = jnp.where((lane == i) | (lane == i + count) | (lane == i + 2 * count), freq[i], u_freq)
    f_full = jnp.concatenate([f_freq] * (rows // 128), 1)
    f_row = lax.broadcasted_iota(jnp.int32, (2 * count, rows), 0)
    quarter = rows // 2
    turn = f_full * (2 * lanes((2 * count, rows)) + 1) + jnp.where(f_row >= count, quarter, 0)
    f_parts = parts_of(cosine(turn, 2 * rows))
    fh_ref[...], fl_ref[...] = f_parts
    for n in range(nodes):
        poly = []
        for axis in range(2):
            c = index[axis, n].astype(f32) * (2.0 / (LEVELS - 1)) - 1.0
            s = c * c
            poly.append([None, c, 1.5 * s - 0.5, (2.5 * s - 1.5) * c, (4.375 * s - 3.75) * s + 0.375])
        weight = node_weights[n]
        for j, (p, q) in enumerate(degrees):
            value = weight
            if p:
                value = value * poly[0][p]
            if q:
                value = value * poly[1][q]
            scalars_ref[16 * n + j : 16 * n + j + 1, :] = jnp.full((1, 128), value, f32)
    dose = 1.0 + 0.1 * (index[1, own].astype(f32) * (2.0 / (LEVELS - 1)) - 1.0)
    scalars_ref[15:16, :] = jnp.full((1, 128), dose, f32)
    for j in range(len(degrees)):
        scalars_ref[16 * nodes + j : 16 * nodes + j + 1, :] = jnp.full((1, 128), chaos[j], f32)
    freq_ref[...] = u_freq
    copies[4].wait()
    row = lax.broadcasted_iota(jnp.int32, (share, share), 0)
    chosen = jnp.where(mirrored, share - 1 - row, row) == lanes((share, share))
    order = jnp.where(chosen, 1.0, 0.0).astype(bf16)
    half = share // 2
    outer = outer_lanes((half, cols), radius)
    for j in range(terms):
        goal = mm(order, raw[j])
        wanted_ref[j] = goal.astype(bf16)
        edge = jnp.where(outer, goal[:half], turned(goal[half:]))
        packed_ref[4 * count + half * j : 4 * count + half * (j + 1), :] = edge.astype(bf16)
    copies[5].wait()
    high, low = parts_of(mm3(f_parts, parts_of(mask[...])) * (1.0 / math.sqrt(rows)))
    packed_ref[0 : 2 * count, :] = high
    packed_ref[2 * count : 4 * count, :] = low
    for copy in copies[6:]:
        copy.wait()


def taps_kernel(freq, weights, taps, wave_hi, wave_lo, u_ref, cs_ref, gr_ref, gi_ref):
    kernels, count, span = gr_ref.shape
    tap_count = taps.shape[4]
    radius = (tap_count - 1) // 2
    rows = u_ref.shape[0]
    quarter = rows // 2
    steps = lax.broadcasted_iota(jnp.int32, (8, 256), 0)

    def spread_out(frequency, first, lead):
        width = frequency.shape[1]
        full = jnp.concatenate([frequency] * (first // 8), 0)
        turn = full * (2 * lax.broadcasted_iota(jnp.int32, (first, width), 0) + 1) + lead
        jump = frequency * (2 * first * steps[:, :width])
        return [cosine(t, 2 * rows) for t in (turn, turn - quarter, jump, jump - quarter)]

    first = rows // 8
    lane = lanes((first, 128))
    c, s, step_c, step_s = spread_out(freq[:, :128], first, jnp.where(lane >= count, quarter, 0))
    for i in range(8):
        table = c * step_c[i : i + 1, :] - s * step_s[i : i + 1, :]
        high, low = parts_of(jnp.where(lane < 2 * count, table, 0.0))
        at = pl.ds(i * first, first)
        u_ref[at, 0:128] = high
        u_ref[at, 128:256] = high
        u_ref[at, 256:384] = low
    first = rows // 16
    lane = lanes((first, 256))
    c, s, step_c, step_s = spread_out(freq[...], first, 0)
    for i in range(8):
        by_c, by_s = step_c[i : i + 1, :], step_s[i : i + 1, :]
        for start, table in ((0, c * by_c - s * by_s), (rows // 2, s * by_c + c * by_s)):
            high, low = parts_of(table)
            both = jnp.where(lane < 2 * count, high.astype(f32), low.astype(f32))
            cs_ref[start + i * first : start + (i + 1) * first, :] = both[:, : 3 * count].astype(bf16)
    side = [jnp.concatenate([w[span - radius : span], w[0 : tap_count - radius]], 0) for w in (wave_hi, wave_lo)]
    scale = jnp.sqrt(weights[...]) * (1.0 / (span * math.sqrt(count)))
    for k in range(kernels):
        parts = parts_of(taps[0, k].reshape(2 * count, tap_count))
        prod = mm3(parts, side)
        amount = scale[0:1, k : k + 1]
        gr_ref[k] = (prod[:count, :span] - prod[count:, span:]) * amount
        gi_ref[k] = (prod[:count, span:] + prod[count:, :span]) * amount


def forward_kernel(
    radius, tiles, tile, scalars, packed, twin, border, gr, gi, cs, wave_hi, wave_lo,
    image_ref, slope_ref, fields_ref, bh, bl, x, total,
):
    kernels, count, span = gr.shape
    nodes, slab, cols = image_ref.shape
    rows = slope_ref.shape[0]
    share = rows // nodes
    half = share // 2
    even = lax.rem(tile[0], 2) == 0
    near = (lanes((2 * count, cols)) < 2 * radius) == even
    pair = []
    for part in range(2):
        at = pl.ds(2 * part * count, 2 * count)
        beyond = jnp.where(near, twin[at, :].astype(f32), border[at, :].astype(f32))
        pair.append(jnp.concatenate([packed[at, :], beyond.astype(bf16)], 1))
    wave = (wave_hi[...], wave_lo[...])
    prod = mm3(pair, wave)
    a_re = prod[:count, :span] + prod[count:, span:]
    a_im = prod[count:, :span] - prod[:count, span:]
    for k in range(kernels):
        b_re = gr[k] * a_re - gi[k] * a_im
        b_im = gr[k] * a_im + gi[k] * a_re
        for d, value in ((0, b_re), (1, b_im)):
            at = pl.ds((2 * k + d) * count, count)
            bh[at, :], bl[at, :] = parts_of(value)
    outer = outer_lanes((count, cols), radius)
    for k in range(kernels):
        if k % 2 == 0:
            at = pl.ds(2 * k * count, 2 * 2 * count)
            qq = mm3((bh[at, :], bl[at, :]), wave)
        q = qq[(k % 2) * 2 * count : (k % 2 + 1) * 2 * count]
        re = q[:count, :span] - q[count:, span:]
        im = q[:count, span:] + q[count:, :span]
        edge = jnp.where(outer, re[:, cols:], turned(im[:, cols:]))
        cross = jnp.where(outer, im[:, cols:], -turned(re[:, cols:]))
        straight = jnp.concatenate([re[:, :cols], im[:, :cols], edge], 1)
        crossed = jnp.concatenate([im[:, :cols], -re[:, :cols], cross], 1)
        for d, value in ((0, straight), (1, crossed)):
            high, low = parts_of(value)
            for place, part in ((0, high), (1, low), (2, high)):
                x[k, d, place * count : (place + 1) * count, :] = part
    total[...] = jnp.zeros(total.shape, f32)

    @pl.loop(0, kernels, unroll=True)
    def _(k):
        even = mm(cs[: rows // 2, :], x[k, 0])
        odd = mm(cs[rows // 2 :, :], x[k, 1])
        for first, field in ((0, even - odd), (rows // 2, even + odd)):
            at = pl.ds(first, rows // 2)
            fields_ref[k, at, :] = field
            square = field * field
            total[at, :cols] += square[:, :cols] + square[:, cols : 2 * cols]
            total[at, cols:] += square[:, 2 * cols :]

    value = scalars[15:16, :]
    inner = total[:, :cols]
    edge = total[:, cols:]
    edge = edge + turned(edge)
    right = right_lanes((rows, cols), radius)
    inside = (right & (tile[0] < tiles - 1)) | (jnp.logical_not(right) & (tile[0] > 0))
    outer = outer_lanes((half, cols), radius)
    for place, intensity in ((0, inner), (1, edge)):
        resist = jax.nn.sigmoid(resist_slope * (value * intensity - resist_level))
        slope = resist * (1.0 - resist) * (2.0 * resist_slope * value)
        if place:
            slope = jnp.where(inside, slope, 0.0)
        slope_ref[:, place * cols : (place + 1) * cols] = slope
        for n in range(nodes):
            rows_n = resist[n * share : (n + 1) * share]
            if place:
                image_ref[n, share:slab, :] = jnp.where(outer, rows_n[:half], rows_n[half:]).astype(bf16)
            else:
                image_ref[n, 0:share, :] = rows_n.astype(bf16)


def middle_kernel(radius, offset, tile, images, wanted, twin, border, scalars, pressure_ref):
    nodes, slab, cols = images.shape
    share = wanted.shape[1]
    step = slab - share
    near = right_lanes((step, cols), radius) == (lax.rem(tile[0], 2) == 0)
    for first in range(0, slab, step):
        image = [images[n, first : first + step, :].astype(f32) for n in range(nodes)]
        pressure = [None] * nodes
        for j in range(len(degrees)):
            weight = [scalars[16 * n + j : 16 * n + j + 1, :] for n in range(nodes)]
            coefficient = weight[0] * image[0]
            for n in range(1, nodes):
                coefficient = coefficient + weight[n] * image[n]
            if first < share:
                goal = wanted[j, first : first + step, :].astype(f32)
            else:
                at = pl.ds(offset + j * step, step)
                goal = jnp.where(near, twin[at, :].astype(f32), border[at, :].astype(f32))
            mixed = scalars[16 * nodes + j : 16 * nodes + j + 1, :] * jnp.tanh(coefficient - goal)
            for n in range(nodes):
                term = weight[n] * mixed
                pressure[n] = term if j == 0 else pressure[n] + term
        for n in range(nodes):
            pressure_ref[n, first : first + step, :] = pressure[n]


def backward_kernel(radius, pressure, slope, fields, fh, fl, gr, gi, u, wave_hi, wave_lo, out_ref, dh, dl, scale):
    kernels, count, span = gr.shape
    nodes, slab, cols = pressure.shape
    rows = slope.shape[0]
    share = rows // nodes
    half = share // 2
    outer = outer_lanes((half, cols), radius)
    for n in range(nodes):
        at = pl.ds(n * share, share)
        scale[at, :cols] = slope[at, :cols] * pressure[n, :share, :]
        edge = pressure[n, share:, :]
        back = turned(edge)
        top, bottom = pl.ds(n * share, half), pl.ds(n * share + half, half)
        scale[top, cols:] = slope[top, cols:] * jnp.where(outer, edge, back)
        scale[bottom, cols:] = slope[bottom, cols:] * jnp.where(outer, back, edge)
    table = []
    for first in (0, count):
        table.append(jnp.concatenate([fh[first : first + count, : rows // 2], fl[first : first + count, : rows // 2]], 0))
    outer = outer_lanes((count, cols), radius)

    @pl.loop(0, kernels, unroll=True)
    def _(k):
        halves = []
        for first in (0, rows // 2):
            at = pl.ds(first, rows // 2)
            inner, edge = scale[at, :cols], scale[at, cols:]
            halves.append(fields[k, at, :] * jnp.concatenate([inner, inner, edge], 1))
        grads = []
        for lhs, value in zip(table, (halves[0] + halves[1], halves[0] - halves[1])):
            high, low = parts_of(value)
            prod = mm(lhs, high)
            grads.append(prod[:count] + prod[count:] + mm(lhs[:count], low))
        straight, crossed = grads
        edge, cross = straight[:, 2 * cols :], crossed[:, 2 * cols :]
        re_edge = jnp.where(outer, edge - turned(cross), 0.0)
        im_edge = jnp.where(outer, cross + turned(edge), 0.0)
        re = jnp.concatenate([straight[:, :cols] - crossed[:, cols : 2 * cols], re_edge], 1)
        im = jnp.concatenate([straight[:, cols : 2 * cols] + crossed[:, :cols], im_edge], 1)
        at = pl.multiple_of(2 * k * count, 2 * count)
        dh[pl.ds(at, count), :], dl[pl.ds(at, count), :] = parts_of(re)
        at = pl.multiple_of(at + count, count)
        dh[pl.ds(at, count), :], dl[pl.ds(at, count), :] = parts_of(im)

    wave = (wave_hi[...], wave_lo[...])
    a_re = jnp.zeros((count, span), f32)
    a_im = jnp.zeros((count, span), f32)
    for k in range(kernels):
        if k % 2 == 0:
            at = pl.ds(2 * k * count, 2 * 2 * count)
            qq = mm3((dh[at, :], dl[at, :]), wave)
        q = qq[(k % 2) * 2 * count : (k % 2 + 1) * 2 * count]
        b_re = q[:count, :span] + q[count:, span:]
        b_im = q[count:, :span] - q[:count, span:]
        a_re = a_re + gr[k] * b_re + gi[k] * b_im
        a_im = a_im + gr[k] * b_im - gi[k] * b_re
    near = [jnp.concatenate([w[:, 0:cols], w[:, span : span + cols]], 1) for w in (wave_hi, wave_lo)]
    prod = mm3(parts_of(jnp.concatenate([a_re, a_im], 0)), near)
    d_re = prod[:count, :cols] - prod[count:, cols:]
    d_im = prod[:count, cols:] + prod[count:, :cols]
    rest = jnp.zeros((128 - 2 * count, cols), f32)
    high, low = parts_of(jnp.concatenate([d_re, d_im, rest], 0))
    spread = mm(u[...], jnp.concatenate([high, low, high], 0)) * (1.0 / math.sqrt(rows))
    largest = jnp.max(jnp.abs(spread), axis=0, keepdims=True)
    power = jnp.ceil(jnp.log2(jnp.maximum(largest, 1e-30)))
    spread = spread * jnp.exp2(-power)
    for n in range(nodes):
        out_ref[n, :share, :] = spread[n * share : (n + 1) * share]
        out_ref[n, share:, :] = jnp.broadcast_to(power, (out_ref.shape[1] - share, cols))


def shape_of(*shape, dtype=f32):
    return jax.ShapeDtypeStruct(shape, dtype)


def call(kernel, mebibytes, spaces, outs, scratch=()):
    return pl.pallas_call(
        kernel,
        in_specs=spaces,
        out_specs=[vmem] * len(outs),
        out_shape=list(outs),
        scratch_shapes=list(scratch),
        compiler_params=pltpu.CompilerParams(vmem_limit_bytes=mebibytes << 20),
    )


def kept(*arrays):
    return [pltpu.with_memory_space_constraint(a, pltpu.HBM) for a in arrays]


def local(mask, taps, weights, node_weights, node_index, freq, chaos, target):
    rows, cols = mask.shape
    kernels, count, tap_count = taps.shape[1], taps.shape[3], taps.shape[4]
    terms = target.shape[0]
    radius = (tap_count - 1) // 2
    span = 2 * cols
    nodes, tiles = lax.axis_size("node"), lax.axis_size("tile")
    node, tile = lax.axis_index("node").reshape(1), lax.axis_index("tile").reshape(1)
    share = rows // nodes
    half = share // 2
    slab = share + half
    inside = [(i, i ^ 1) for i in range(tiles) if i ^ 1 < tiles]
    across = [(i, ((i + 1) ^ 1) - 1) for i in range(tiles) if 0 <= ((i + 1) ^ 1) - 1 < tiles]
    wave_hi, wave_lo = (jnp.asarray(w) for w in column_waves(span))
    packed, wanted, fh, fl, turns, scalars, wave_hi, wave_lo, staged, loads = call(
        functools.partial(first_kernel, radius),
        16,
        [smem] + [hbm] * 10,
        [
            shape_of(4 * count + half * terms, cols, dtype=bf16),
            shape_of(terms, share, cols, dtype=bf16),
            shape_of(2 * count, rows, dtype=bf16),
            shape_of(2 * count, rows, dtype=bf16),
            shape_of(8, 256, dtype=jnp.int32),
            shape_of(16 * nodes + 16, 128),
            shape_of(span, 2 * span, dtype=bf16),
            shape_of(span, 2 * span, dtype=bf16),
            shape_of(*taps.shape),
            shape_of(*weights.shape),
        ],
        [
            pltpu.SMEM(freq.shape, jnp.int32),
            pltpu.SMEM((2, nodes), jnp.int32),
            pltpu.SMEM((nodes,), f32),
            pltpu.SMEM(chaos.shape, f32),
            pltpu.VMEM((terms, share, cols), bf16),
            pltpu.VMEM(mask.shape, f32),
            pltpu.SemaphoreType.DMA((10,)),
        ],
    )(node, *kept(freq, node_index.T, node_weights, chaos, target, mask, wave_hi, wave_lo, taps, weights))
    border = lax.ppermute(packed, "tile", across)
    twin = lax.ppermute(packed, "tile", inside)
    u, cs, gr, gi = call(
        taps_kernel,
        8,
        [vmem] * 5,
        [
            shape_of(rows, 384, dtype=bf16),
            shape_of(rows, 3 * count, dtype=bf16),
            shape_of(kernels, count, span),
            shape_of(kernels, count, span),
        ],
    )(turns, loads, staged, wave_hi, wave_lo)
    image, slope, fields = call(
        functools.partial(forward_kernel, radius, tiles),
        20,
        [smem] + [vmem] * 9,
        [
            shape_of(nodes, slab, cols, dtype=bf16),
            shape_of(rows, 2 * cols),
            shape_of(kernels, rows, 3 * cols),
        ],
        [
            pltpu.VMEM((2 * kernels * count, span), bf16),
            pltpu.VMEM((2 * kernels * count, span), bf16),
            pltpu.VMEM((kernels, 2, 3 * count, 3 * cols), bf16),
            pltpu.VMEM((rows, 2 * cols), f32),
        ],
    )(tile, scalars, packed, twin, border, gr, gi, cs, wave_hi, wave_lo)
    images = lax.all_to_all(image, "node", 0, 0)
    (pressure,) = call(
        functools.partial(middle_kernel, radius, 4 * count), 8, [smem] + [vmem] * 5, [shape_of(nodes, slab, cols)]
    )(tile, images, wanted, twin, border, scalars)
    pressure = lax.all_to_all((pressure * 8192.0).astype(jnp.float16), "node", 0, 0).astype(f32) * (1.0 / 8192.0)
    (spread,) = call(
        functools.partial(backward_kernel, radius),
        16,
        [vmem] * 10,
        [shape_of(nodes, share + 8, cols)],
        [
            pltpu.VMEM((2 * kernels * count, span), bf16),
            pltpu.VMEM((2 * kernels * count, span), bf16),
            pltpu.VMEM((rows, 2 * cols), f32),
        ],
    )(pressure, slope, fields, fh, fl, gr, gi, u, wave_hi, wave_lo)
    spread = lax.all_to_all(spread.astype(jnp.float16), "node", 0, 0).astype(f32)
    return (spread[:, :share] * jnp.exp2(spread[:, share : share + 1])).sum(0)


def solution(mesh):
    placed = (
        P(None, "tile"),
        P("node", None, None, None, None),
        P("node", None),
        P(),
        P(),
        P(),
        P(),
        P(None, None, "tile"),
    )
    return jax.shard_map(local, mesh=mesh, in_specs=placed, out_specs=P("node", "tile"), check_vma=False)
```

```python
import functools
import math

import jax
import jax.numpy as jnp
import ml_dtypes
import numpy as np
from jax import lax
from jax.experimental import pallas as pl
from jax.experimental.pallas import tpu as pltpu
from jax.sharding import PartitionSpec as P

LEVELS = 5
resist_slope = 4.0
resist_level = 0.6
degrees = [(d - q, q) for d in range(5) for q in range(d + 1)]
f32, bf16 = jnp.float32, jnp.bfloat16
vmem = pl.BlockSpec(memory_space=pltpu.VMEM)
smem = pl.BlockSpec(memory_space=pltpu.SMEM)
hbm = pl.BlockSpec(memory_space=pltpu.HBM)


def parts_of(value):
    high = value.astype(bf16)
    return high, (value - high.astype(f32)).astype(bf16)


def mm(a, b):
    return jnp.dot(a, b, preferred_element_type=f32)


def mm3(a, b):
    return mm(jnp.concatenate([a[0], a[0], a[1]], 1), jnp.concatenate([b[0], b[1], b[0]], 0))


def cosine(turn, period):
    turn = jnp.bitwise_and(turn, period - 1)
    half = jnp.minimum(turn, period - turn)
    far = half > period // 4
    angle = jnp.where(far, period // 2 - half, half).astype(f32) * (2.0 * math.pi / period)
    z = angle * angle
    poly = jnp.full_like(z, 1.0 / math.factorial(12))
    for order in (10, 8, 6, 4, 2, 0):
        sign = -1.0 if order % 4 == 2 else 1.0
        poly = poly * z + sign / math.factorial(order)
    return jnp.where(far, -poly, poly)


def column_waves(length):
    turn = (np.arange(length)[:, None] * np.arange(length)[None, :]) % length
    wave = np.concatenate([np.cos(2 * np.pi * turn / length), np.sin(2 * np.pi * turn / length)], 1)
    high = wave.astype(np.float32).astype(ml_dtypes.bfloat16)
    low = (wave - high.astype(np.float64)).astype(np.float32).astype(ml_dtypes.bfloat16)
    return high, low


def lanes(shape):
    return lax.broadcasted_iota(jnp.int32, shape, len(shape) - 1)


def turned(value):
    return pltpu.roll(value, value.shape[-1] // 2, len(value.shape) - 1)


def outer_lanes(shape, radius):
    lane = lanes(shape)
    return (lane < radius) | (lane >= shape[-1] - radius)


def right_lanes(shape, radius):
    lane, half = lanes(shape), shape[-1] // 2
    return (lane < radius) | ((lane >= half) & (lane < half + radius))


def spectrum_kernel(radius, node, freq_in, mask_in, target_in, packed_ref, wanted_ref, fh_ref, fl_ref, freq, mask, raw, sems):
    rows, cols = mask.shape
    count = freq.shape[0]
    terms, share = raw.shape[0], raw.shape[1]
    own = node[0]
    mirrored = own >= rows // (2 * share)
    at = jnp.where(mirrored, rows + rows // 2 - share - own * share, own * share)
    at = pl.multiple_of(at, share)
    moves = [(freq_in, freq), (mask_in, mask), (target_in.at[:, pl.ds(at, share), :], raw)]
    copies = [pltpu.make_async_copy(source, goal, sems.at[i]) for i, (source, goal) in enumerate(moves)]
    for copy in copies:
        copy.start()
    copies[0].wait()
    line = lax.broadcasted_iota(jnp.int32, (2 * count, 128), 0)
    f_freq = jnp.zeros((2 * count, 128), jnp.int32)
    for i in range(count):
        f_freq = jnp.where((line == i) | (line == i + count), freq[i], f_freq)
    f_full = jnp.concatenate([f_freq] * (rows // 128), 1)
    f_row = lax.broadcasted_iota(jnp.int32, (2 * count, rows), 0)
    turn = f_full * (2 * lanes((2 * count, rows)) + 1) + jnp.where(f_row >= count, rows // 2, 0)
    f_parts = parts_of(cosine(turn, 2 * rows))
    fh_ref[...], fl_ref[...] = f_parts
    copies[2].wait()
    row = lax.broadcasted_iota(jnp.int32, (share, share), 0)
    chosen = jnp.where(mirrored, share - 1 - row, row) == lanes((share, share))
    order = jnp.where(chosen, 1.0, 0.0).astype(bf16)
    half = share // 2
    outer = outer_lanes((half, cols), radius)
    for j in range(terms):
        goal = mm(order, raw[j])
        wanted_ref[j] = goal.astype(bf16)
        edge = jnp.where(outer, goal[:half], turned(goal[half:]))
        packed_ref[4 * count + half * j : 4 * count + half * (j + 1), :] = edge.astype(bf16)
    copies[1].wait()
    high, low = parts_of(mm3(f_parts, parts_of(mask[...])) * (1.0 / math.sqrt(rows)))
    packed_ref[0 : 2 * count, :] = high
    packed_ref[2 * count : 4 * count, :] = low


def tables_kernel(
    node, freq_in, index_in, node_weights_in, chaos_in, weights_in, taps_in, wave_hi_in, wave_lo_in,
    u_ref, cs_ref, gr_ref, gi_ref, wave_hi, wave_lo, scalars_ref,
    freq, index, node_weights, chaos, weights, taps, sems,
):
    rows = u_ref.shape[0]
    count = freq.shape[0]
    kernels, tap_count = taps.shape[1], taps.shape[4]
    span = wave_hi.shape[0]
    radius = (tap_count - 1) // 2
    nodes = index.shape[1]
    moves = [
        (freq_in, freq),
        (index_in, index),
        (node_weights_in, node_weights),
        (chaos_in, chaos),
        (weights_in, weights),
        (wave_hi_in, wave_hi),
        (wave_lo_in, wave_lo),
        (taps_in, taps),
    ]
    copies = [pltpu.make_async_copy(source, goal, sems.at[i]) for i, (source, goal) in enumerate(moves)]
    for copy in copies:
        copy.start()
    for copy in copies[:4]:
        copy.wait()
    lane = lanes((8, 256))
    turns = jnp.zeros((8, 256), jnp.int32)
    for i in range(count):
        turns = jnp.where((lane == i) | (lane == i + count) | (lane == i + 2 * count), freq[i], turns)
    quarter = rows // 2
    steps = lax.broadcasted_iota(jnp.int32, (8, 256), 0)

    def spread_out(frequency, first, lead):
        width = frequency.shape[1]
        full = jnp.concatenate([frequency] * (first // 8), 0)
        turn = full * (2 * lax.broadcasted_iota(jnp.int32, (first, width), 0) + 1) + lead
        jump = frequency * (2 * first * steps[:, :width])
        return [cosine(t, 2 * rows) for t in (turn, turn - quarter, jump, jump - quarter)]

    first = rows // 8
    lane = lanes((first, 128))
    c, s, step_c, step_s = spread_out(turns[:, :128], first, jnp.where(lane >= count, quarter, 0))
    for i in range(8):
        table = c * step_c[i : i + 1, :] - s * step_s[i : i + 1, :]
        high, low = parts_of(jnp.where(lane < 2 * count, table, 0.0))
        at = pl.ds(i * first, first)
        u_ref[at, 0:128] = high
        u_ref[at, 128:256] = high
        u_ref[at, 256:384] = low
    first = rows // 16
    lane = lanes((first, 256))
    c, s, step_c, step_s = spread_out(turns, first, 0)
    for i in range(8):
        by_c, by_s = step_c[i : i + 1, :], step_s[i : i + 1, :]
        for start, table in ((0, c * by_c - s * by_s), (rows // 2, s * by_c + c * by_s)):
            high, low = parts_of(table)
            both = jnp.where(lane < 2 * count, high.astype(f32), low.astype(f32))
            cs_ref[start + i * first : start + (i + 1) * first, :] = both[:, : 3 * count].astype(bf16)
    for n in range(nodes):
        poly = []
        for axis in range(2):
            c = index[axis, n].astype(f32) * (2.0 / (LEVELS - 1)) - 1.0
            s = c * c
            poly.append([None, c, 1.5 * s - 0.5, (2.5 * s - 1.5) * c, (4.375 * s - 3.75) * s + 0.375])
        weight = node_weights[n]
        for j, (p, q) in enumerate(degrees):
            value = weight
            if p:
                value = value * poly[0][p]
            if q:
                value = value * poly[1][q]
            scalars_ref[16 * n + j : 16 * n + j + 1, :] = jnp.full((1, 128), value, f32)
    dose = 1.0 + 0.1 * (index[1, node[0]].astype(f32) * (2.0 / (LEVELS - 1)) - 1.0)
    scalars_ref[15:16, :] = jnp.full((1, 128), dose, f32)
    for j in range(len(degrees)):
        scalars_ref[16 * nodes + j : 16 * nodes + j + 1, :] = jnp.full((1, 128), chaos[j], f32)
    for copy in copies[4:]:
        copy.wait()
    side = [jnp.concatenate([w[span - radius : span], w[0 : tap_count - radius]], 0) for w in (wave_hi, wave_lo)]
    scale = jnp.sqrt(weights[...]) * (1.0 / (span * math.sqrt(count)))
    for k in range(kernels):
        parts = parts_of(taps[0, k].reshape(2 * count, tap_count))
        prod = mm3(parts, side)
        amount = scale[0:1, k : k + 1]
        gr_ref[k] = (prod[:count, :span] - prod[count:, span:]) * amount
        gi_ref[k] = (prod[:count, span:] + prod[count:, :span]) * amount


def forward_kernel(
    radius, tiles, tile, scalars, packed, twin, border, gr, gi, cs, wave_hi, wave_lo,
    image_ref, slope_ref, fields_ref, bh, bl, x, total,
):
    kernels, count, span = gr.shape
    nodes, slab, cols = image_ref.shape
    rows = slope_ref.shape[0]
    share = rows // nodes
    half = share // 2
    even = lax.rem(tile[0], 2) == 0
    near = (lanes((2 * count, cols)) < 2 * radius) == even
    pair = []
    for part in range(2):
        at = pl.ds(2 * part * count, 2 * count)
        beyond = jnp.where(near, twin[at, :].astype(f32), border[at, :].astype(f32))
        pair.append(jnp.concatenate([packed[at, :], beyond.astype(bf16)], 1))
    wave = (wave_hi[...], wave_lo[...])
    prod = mm3(pair, wave)
    a_re = prod[:count, :span] + prod[count:, span:]
    a_im = prod[count:, :span] - prod[:count, span:]
    for k in range(kernels):
        b_re = gr[k] * a_re - gi[k] * a_im
        b_im = gr[k] * a_im + gi[k] * a_re
        for d, value in ((0, b_re), (1, b_im)):
            at = pl.ds((2 * k + d) * count, count)
            bh[at, :], bl[at, :] = parts_of(value)
    outer = outer_lanes((count, cols), radius)
    for k in range(kernels):
        if k % 2 == 0:
            at = pl.ds(2 * k * count, 2 * 2 * count)
            qq = mm3((bh[at, :], bl[at, :]), wave)
        q = qq[(k % 2) * 2 * count : (k % 2 + 1) * 2 * count]
        re = q[:count, :span] - q[count:, span:]
        im = q[:count, span:] + q[count:, :span]
        edge = jnp.where(outer, re[:, cols:], turned(im[:, cols:]))
        cross = jnp.where(outer, im[:, cols:], -turned(re[:, cols:]))
        straight = jnp.concatenate([re[:, :cols], im[:, :cols], edge], 1)
        crossed = jnp.concatenate([im[:, :cols], -re[:, :cols], cross], 1)
        for d, value in ((0, straight), (1, crossed)):
            high, low = parts_of(value)
            at = 3 * cols * (k % 2)
            for place, part in ((0, high), (1, low), (2, high)):
                x[k // 2, d, place * count : (place + 1) * count, at : at + 3 * cols] = part
    for pair in range(kernels // 2):
        even_part = mm(cs[: rows // 2, :], x[pair, 0])
        odd_part = mm(cs[rows // 2 :, :], x[pair, 1])
        for first, field in ((0, even_part - odd_part), (rows // 2, even_part + odd_part)):
            at = pl.ds(first, rows // 2)
            fields_ref[2 * pair, at, :] = field[:, : 3 * cols]
            fields_ref[2 * pair + 1, at, :] = field[:, 3 * cols :]
            square = field * field
            inner = square[:, :cols] + square[:, cols : 2 * cols]
            inner = inner + (square[:, 3 * cols : 4 * cols] + square[:, 4 * cols : 5 * cols])
            edge = square[:, 2 * cols : 3 * cols] + square[:, 5 * cols :]
            if pair:
                inner, edge = inner + total[at, :cols], edge + total[at, cols:]
            total[at, :cols] = inner
            total[at, cols:] = edge

    value = scalars[15:16, :]
    inner = total[:, :cols]
    edge = total[:, cols:]
    edge = edge + turned(edge)
    right = right_lanes((rows, cols), radius)
    inside = (right & (tile[0] < tiles - 1)) | (jnp.logical_not(right) & (tile[0] > 0))
    outer = outer_lanes((half, cols), radius)
    for place, intensity in ((0, inner), (1, edge)):
        resist = jax.nn.sigmoid(resist_slope * (value * intensity - resist_level))
        slope = resist * (1.0 - resist) * (2.0 * resist_slope * value)
        if place:
            slope = jnp.where(inside, slope, 0.0)
        slope_ref[:, place * cols : (place + 1) * cols] = slope
        for n in range(nodes):
            rows_n = resist[n * share : (n + 1) * share]
            if place:
                image_ref[n, share:slab, :] = jnp.where(outer, rows_n[:half], rows_n[half:]).astype(bf16)
            else:
                image_ref[n, 0:share, :] = rows_n.astype(bf16)


def middle_kernel(radius, offset, tile, images, wanted, twin, border, scalars, pressure_ref):
    nodes, slab, cols = images.shape
    share = wanted.shape[1]
    step = slab - share
    near = right_lanes((step, cols), radius) == (lax.rem(tile[0], 2) == 0)
    for first in range(0, slab, step):
        image = [images[n, first : first + step, :].astype(f32) for n in range(nodes)]
        pressure = [None] * nodes
        for j in range(len(degrees)):
            weight = [scalars[16 * n + j : 16 * n + j + 1, :] for n in range(nodes)]
            coefficient = weight[0] * image[0]
            for n in range(1, nodes):
                coefficient = coefficient + weight[n] * image[n]
            if first < share:
                goal = wanted[j, first : first + step, :].astype(f32)
            else:
                at = pl.ds(offset + j * step, step)
                goal = jnp.where(near, twin[at, :].astype(f32), border[at, :].astype(f32))
            mixed = scalars[16 * nodes + j : 16 * nodes + j + 1, :] * jnp.tanh(coefficient - goal)
            for n in range(nodes):
                term = weight[n] * mixed
                pressure[n] = term if j == 0 else pressure[n] + term
        for n in range(nodes):
            pressure_ref[n, first : first + step, :] = pressure[n]


def backward_kernel(radius, pressure, slope, fields, fh, fl, gr, gi, u, wave_hi, wave_lo, out_ref, dh, dl, scale):
    kernels, count, span = gr.shape
    nodes, slab, cols = pressure.shape
    rows = slope.shape[0]
    share = rows // nodes
    half = share // 2
    outer = outer_lanes((half, cols), radius)
    for n in range(nodes):
        at = pl.ds(n * share, share)
        scale[at, :cols] = slope[at, :cols] * pressure[n, :share, :]
        edge = pressure[n, share:, :]
        back = turned(edge)
        top, bottom = pl.ds(n * share, half), pl.ds(n * share + half, half)
        scale[top, cols:] = slope[top, cols:] * jnp.where(outer, edge, back)
        scale[bottom, cols:] = slope[bottom, cols:] * jnp.where(outer, back, edge)
    table = []
    for first in (0, count):
        table.append(jnp.concatenate([fh[first : first + count, : rows // 2], fl[first : first + count, : rows // 2]], 0))
    outer = outer_lanes((count, cols), radius)

    for pair in range(0, kernels, 2):
        halves = []
        for first in (0, rows // 2):
            at = pl.ds(first, rows // 2)
            inner, edge = scale[at, :cols], scale[at, cols:]
            both = jnp.concatenate([fields[pair, at, :], fields[pair + 1, at, :]], 1)
            halves.append(both * jnp.concatenate([inner, inner, edge] * 2, 1))
        grads = []
        for lhs, value in zip(table, (halves[0] + halves[1], halves[0] - halves[1])):
            high, low = parts_of(value)
            prod = mm(lhs, high)
            grads.append(prod[:count] + prod[count:] + mm(lhs[:count], low))
        for k in (pair, pair + 1):
            straight, crossed = (g[:, 3 * cols * (k - pair) : 3 * cols * (k - pair + 1)] for g in grads)
            edge, cross = straight[:, 2 * cols :], crossed[:, 2 * cols :]
            re_edge = jnp.where(outer, edge - turned(cross), 0.0)
            im_edge = jnp.where(outer, cross + turned(edge), 0.0)
            re = jnp.concatenate([straight[:, :cols] - crossed[:, cols : 2 * cols], re_edge], 1)
            im = jnp.concatenate([straight[:, cols : 2 * cols] + crossed[:, :cols], im_edge], 1)
            for d, value in ((0, re), (1, im)):
                at = pl.ds((2 * k + d) * count, count)
                dh[at, :], dl[at, :] = parts_of(value)

    wave = (wave_hi[...], wave_lo[...])
    a_re = jnp.zeros((count, span), f32)
    a_im = jnp.zeros((count, span), f32)
    for k in range(kernels):
        if k % 2 == 0:
            at = pl.ds(2 * k * count, 2 * 2 * count)
            qq = mm3((dh[at, :], dl[at, :]), wave)
        q = qq[(k % 2) * 2 * count : (k % 2 + 1) * 2 * count]
        b_re = q[:count, :span] + q[count:, span:]
        b_im = q[count:, :span] - q[:count, span:]
        a_re = a_re + gr[k] * b_re + gi[k] * b_im
        a_im = a_im + gr[k] * b_im - gi[k] * b_re
    near = [jnp.concatenate([w[:, 0:cols], w[:, span : span + cols]], 1) for w in (wave_hi, wave_lo)]
    prod = mm3(parts_of(jnp.concatenate([a_re, a_im], 0)), near)
    d_re = prod[:count, :cols] - prod[count:, cols:]
    d_im = prod[:count, cols:] + prod[count:, :cols]
    rest = jnp.zeros((128 - 2 * count, cols), f32)
    high, low = parts_of(jnp.concatenate([d_re, d_im, rest], 0))
    spread = mm(u[...], jnp.concatenate([high, low, high], 0)) * (1.0 / math.sqrt(rows))
    largest = jnp.max(jnp.abs(spread), axis=0, keepdims=True)
    power = jnp.ceil(jnp.log2(jnp.maximum(largest, 1e-30)))
    spread = spread * jnp.exp2(-power)
    for n in range(nodes):
        out_ref[n, :share, :] = spread[n * share : (n + 1) * share]
        out_ref[n, share:, :] = jnp.broadcast_to(power, (out_ref.shape[1] - share, cols))


def shape_of(*shape, dtype=f32):
    return jax.ShapeDtypeStruct(shape, dtype)


def call(kernel, mebibytes, spaces, outs, scratch=()):
    return pl.pallas_call(
        kernel,
        in_specs=spaces,
        out_specs=[vmem] * len(outs),
        out_shape=list(outs),
        scratch_shapes=list(scratch),
        compiler_params=pltpu.CompilerParams(vmem_limit_bytes=mebibytes << 20),
    )


def kept(*arrays):
    return [pltpu.with_memory_space_constraint(a, pltpu.HBM) for a in arrays]


def local(mask, taps, weights, node_weights, node_index, freq, chaos, target):
    rows, cols = mask.shape
    kernels, count, tap_count = taps.shape[1], taps.shape[3], taps.shape[4]
    terms = target.shape[0]
    radius = (tap_count - 1) // 2
    span = 2 * cols
    nodes, tiles = lax.axis_size("node"), lax.axis_size("tile")
    node, tile = lax.axis_index("node").reshape(1), lax.axis_index("tile").reshape(1)
    share = rows // nodes
    half = share // 2
    slab = share + half
    inside = [(i, i ^ 1) for i in range(tiles) if i ^ 1 < tiles]
    across = [(i, ((i + 1) ^ 1) - 1) for i in range(tiles) if 0 <= ((i + 1) ^ 1) - 1 < tiles]
    wave_hi, wave_lo = (jnp.asarray(w) for w in column_waves(span))
    packed, wanted, fh, fl = call(
        functools.partial(spectrum_kernel, radius),
        8,
        [smem] + [hbm] * 3,
        [
            shape_of(4 * count + half * terms, cols, dtype=bf16),
            shape_of(terms, share, cols, dtype=bf16),
            shape_of(2 * count, rows, dtype=bf16),
            shape_of(2 * count, rows, dtype=bf16),
        ],
        [
            pltpu.SMEM(freq.shape, jnp.int32),
            pltpu.VMEM(mask.shape, f32),
            pltpu.VMEM((terms, share, cols), bf16),
            pltpu.SemaphoreType.DMA((3,)),
        ],
    )(node, *kept(freq, mask, target))
    border = lax.ppermute(packed, "tile", across)
    u, cs, gr, gi, wave_hi, wave_lo, scalars = call(
        tables_kernel,
        16,
        [smem] + [hbm] * 8,
        [
            shape_of(rows, 384, dtype=bf16),
            shape_of(rows, 3 * count, dtype=bf16),
            shape_of(kernels, count, span),
            shape_of(kernels, count, span),
            shape_of(span, 2 * span, dtype=bf16),
            shape_of(span, 2 * span, dtype=bf16),
            shape_of(16 * nodes + 16, 128),
        ],
        [
            pltpu.SMEM(freq.shape, jnp.int32),
            pltpu.SMEM((2, nodes), jnp.int32),
            pltpu.SMEM((nodes,), f32),
            pltpu.SMEM(chaos.shape, f32),
            pltpu.VMEM(weights.shape, f32),
            pltpu.VMEM(taps.shape, f32),
            pltpu.SemaphoreType.DMA((8,)),
        ],
    )(node, *kept(freq, node_index.T, node_weights, chaos, weights, taps, wave_hi, wave_lo))
    ready, scalars = lax.optimization_barrier((packed, scalars))
    twin = lax.ppermute(ready, "tile", inside)
    image, slope, fields = call(
        functools.partial(forward_kernel, radius, tiles),
        20,
        [smem] + [vmem] * 9,
        [
            shape_of(nodes, slab, cols, dtype=bf16),
            shape_of(rows, 2 * cols),
            shape_of(kernels, rows, 3 * cols),
        ],
        [
            pltpu.VMEM((2 * kernels * count, span), bf16),
            pltpu.VMEM((2 * kernels * count, span), bf16),
            pltpu.VMEM((kernels // 2, 2, 3 * count, 6 * cols), bf16),
            pltpu.VMEM((rows, 2 * cols), f32),
        ],
    )(tile, scalars, packed, twin, border, gr, gi, cs, wave_hi, wave_lo)
    images = lax.all_to_all(image, "node", 0, 0)
    (pressure,) = call(
        functools.partial(middle_kernel, radius, 4 * count), 8, [smem] + [vmem] * 5, [shape_of(nodes, slab, cols)]
    )(tile, images, wanted, twin, border, scalars)
    pressure = lax.all_to_all((pressure * 8192.0).astype(jnp.float16), "node", 0, 0).astype(f32) * (1.0 / 8192.0)
    (spread,) = call(
        functools.partial(backward_kernel, radius),
        16,
        [vmem] * 10,
        [shape_of(nodes, share + 8, cols)],
        [
            pltpu.VMEM((2 * kernels * count, span), bf16),
            pltpu.VMEM((2 * kernels * count, span), bf16),
            pltpu.VMEM((rows, 2 * cols), f32),
        ],
    )(pressure, slope, fields, fh, fl, gr, gi, u, wave_hi, wave_lo)
    spread = lax.all_to_all(spread.astype(jnp.float16), "node", 0, 0).astype(f32)
    return (spread[:, :share] * jnp.exp2(spread[:, share : share + 1])).sum(0)


def solution(mesh):
    placed = (
        P(None, "tile"),
        P("node", None, None, None, None),
        P("node", None),
        P(),
        P(),
        P(),
        P(),
        P(None, None, "tile"),
    )
    return jax.shard_map(local, mesh=mesh, in_specs=placed, out_specs=P("node", "tile"), check_vma=False)
```

```python
import functools
import math

import jax
import jax.numpy as jnp
import ml_dtypes
import numpy as np
from jax import lax
from jax.experimental import pallas as pl
from jax.experimental.pallas import tpu as pltpu
from jax.sharding import PartitionSpec as P

LEVELS = 5
resist_slope = 4.0
resist_level = 0.6
degrees = [(d - q, q) for d in range(5) for q in range(d + 1)]
f32, bf16 = jnp.float32, jnp.bfloat16
vmem = pl.BlockSpec(memory_space=pltpu.VMEM)
smem = pl.BlockSpec(memory_space=pltpu.SMEM)
hbm = pl.BlockSpec(memory_space=pltpu.HBM)


def parts_of(value):
    high = value.astype(bf16)
    return high, (value - high.astype(f32)).astype(bf16)


def mm(a, b):
    return jnp.dot(a, b, preferred_element_type=f32)


def mm3(a, b):
    return mm(jnp.concatenate([a[0], a[0], a[1]], 1), jnp.concatenate([b[0], b[1], b[0]], 0))


def cosine(turn, period):
    turn = jnp.bitwise_and(turn, period - 1)
    half = jnp.minimum(turn, period - turn)
    far = half > period // 4
    angle = jnp.where(far, period // 2 - half, half).astype(f32) * (2.0 * math.pi / period)
    z = angle * angle
    poly = jnp.full_like(z, 1.0 / math.factorial(12))
    for order in (10, 8, 6, 4, 2, 0):
        sign = -1.0 if order % 4 == 2 else 1.0
        poly = poly * z + sign / math.factorial(order)
    return jnp.where(far, -poly, poly)


def column_waves(length):
    turn = (np.arange(length)[:, None] * np.arange(length)[None, :]) % length
    wave = np.concatenate([np.cos(2 * np.pi * turn / length), np.sin(2 * np.pi * turn / length)], 1)
    high = wave.astype(np.float32).astype(ml_dtypes.bfloat16)
    low = (wave - high.astype(np.float64)).astype(np.float32).astype(ml_dtypes.bfloat16)
    return high, low


def lanes(shape):
    return lax.broadcasted_iota(jnp.int32, shape, len(shape) - 1)


def turned(value):
    return pltpu.roll(value, value.shape[-1] // 2, len(value.shape) - 1)


def outer_lanes(shape, radius):
    lane = lanes(shape)
    return (lane < radius) | (lane >= shape[-1] - radius)


def right_lanes(shape, radius):
    lane, half = lanes(shape), shape[-1] // 2
    return (lane < radius) | ((lane >= half) & (lane < half + radius))


def spectrum_kernel(
    radius, node, freq_in, mask_in, target_in, taps_in, wave_hi_in, wave_lo_in,
    packed_ref, wanted_ref, fh_ref, fl_ref, taps, wave_hi, wave_lo, turns_ref, freq, mask, raw, sems,
):
    rows, cols = mask.shape
    count = freq.shape[0]
    terms, share = raw.shape[0], raw.shape[1]
    own = node[0]
    mirrored = own >= rows // (2 * share)
    at = jnp.where(mirrored, rows + rows // 2 - share - own * share, own * share)
    at = pl.multiple_of(at, share)
    moves = [(freq_in, freq), (mask_in, mask), (target_in.at[:, pl.ds(at, share), :], raw)]
    moves += [(taps_in, taps), (wave_hi_in, wave_hi), (wave_lo_in, wave_lo)]
    copies = [pltpu.make_async_copy(source, goal, sems.at[i]) for i, (source, goal) in enumerate(moves)]
    for copy in copies:
        copy.start()
    copies[0].wait()
    line = lax.broadcasted_iota(jnp.int32, (2 * count, 128), 0)
    f_freq = jnp.zeros((2 * count, 128), jnp.int32)
    lane = lanes((8, 256))
    turns = jnp.zeros((8, 256), jnp.int32)
    for i in range(count):
        f_freq = jnp.where((line == i) | (line == i + count), freq[i], f_freq)
        turns = jnp.where((lane == i) | (lane == i + count) | (lane == i + 2 * count), freq[i], turns)
    turns_ref[...] = turns
    f_full = jnp.concatenate([f_freq] * (rows // 128), 1)
    f_row = lax.broadcasted_iota(jnp.int32, (2 * count, rows), 0)
    turn = f_full * (2 * lanes((2 * count, rows)) + 1) + jnp.where(f_row >= count, rows // 2, 0)
    f_parts = parts_of(cosine(turn, 2 * rows))
    fh_ref[...], fl_ref[...] = f_parts
    copies[2].wait()
    row = lax.broadcasted_iota(jnp.int32, (share, share), 0)
    chosen = jnp.where(mirrored, share - 1 - row, row) == lanes((share, share))
    order = jnp.where(chosen, 1.0, 0.0).astype(bf16)
    half = share // 2
    outer = outer_lanes((half, cols), radius)
    for j in range(terms):
        goal = mm(order, raw[j])
        wanted_ref[j] = goal.astype(bf16)
        edge = jnp.where(outer, goal[:half], turned(goal[half:]))
        packed_ref[4 * count + half * j : 4 * count + half * (j + 1), :] = edge.astype(bf16)
    copies[1].wait()
    high, low = parts_of(mm3(f_parts, parts_of(mask[...])) * (1.0 / math.sqrt(rows)))
    packed_ref[0 : 2 * count, :] = high
    packed_ref[2 * count : 4 * count, :] = low
    for copy in copies[3:]:
        copy.wait()


def tables_kernel(
    node, turns_ref, index_in, node_weights_in, chaos_in, weights_in, taps, wave_hi, wave_lo,
    u_ref, cs_ref, gr_ref, gi_ref, scalars_ref,
    index, node_weights, chaos, weights, sems,
):
    rows = u_ref.shape[0]
    kernels, count, tap_count = taps.shape[1], taps.shape[3], taps.shape[4]
    span = wave_hi.shape[0]
    radius = (tap_count - 1) // 2
    nodes = index.shape[1]
    moves = [
        (index_in, index),
        (node_weights_in, node_weights),
        (chaos_in, chaos),
        (weights_in, weights),
    ]
    copies = [pltpu.make_async_copy(source, goal, sems.at[i]) for i, (source, goal) in enumerate(moves)]
    for copy in copies:
        copy.start()
    turns = turns_ref[...]
    quarter = rows // 2
    steps = lax.broadcasted_iota(jnp.int32, (8, 256), 0)

    def spread_out(frequency, first, lead):
        width = frequency.shape[1]
        full = jnp.concatenate([frequency] * (first // 8), 0)
        turn = full * (2 * lax.broadcasted_iota(jnp.int32, (first, width), 0) + 1) + lead
        jump = frequency * (2 * first * steps[:, :width])
        return [cosine(t, 2 * rows) for t in (turn, turn - quarter, jump, jump - quarter)]

    first = rows // 8
    lane = lanes((first, 128))
    c, s, step_c, step_s = spread_out(turns[:, :128], first, jnp.where(lane >= count, quarter, 0))
    for i in range(8):
        table = c * step_c[i : i + 1, :] - s * step_s[i : i + 1, :]
        high, low = parts_of(jnp.where(lane < 2 * count, table, 0.0))
        at = pl.ds(i * first, first)
        u_ref[at, 0:128] = high
        u_ref[at, 128:256] = high
        u_ref[at, 256:384] = low
    first = rows // 16
    lane = lanes((first, 256))
    c, s, step_c, step_s = spread_out(turns, first, 0)
    for i in range(8):
        by_c, by_s = step_c[i : i + 1, :], step_s[i : i + 1, :]
        for start, table in ((0, c * by_c - s * by_s), (rows // 2, s * by_c + c * by_s)):
            high, low = parts_of(table)
            both = jnp.where(lane < 2 * count, high.astype(f32), low.astype(f32))
            cs_ref[start + i * first : start + (i + 1) * first, :] = both[:, : 3 * count].astype(bf16)
    for copy in copies[:3]:
        copy.wait()
    for n in range(nodes):
        poly = []
        for axis in range(2):
            c = index[axis, n].astype(f32) * (2.0 / (LEVELS - 1)) - 1.0
            s = c * c
            poly.append([None, c, 1.5 * s - 0.5, (2.5 * s - 1.5) * c, (4.375 * s - 3.75) * s + 0.375])
        weight = node_weights[n]
        for j, (p, q) in enumerate(degrees):
            value = weight
            if p:
                value = value * poly[0][p]
            if q:
                value = value * poly[1][q]
            scalars_ref[16 * n + j : 16 * n + j + 1, :] = jnp.full((1, 128), value, f32)
    dose = 1.0 + 0.1 * (index[1, node[0]].astype(f32) * (2.0 / (LEVELS - 1)) - 1.0)
    scalars_ref[15:16, :] = jnp.full((1, 128), dose, f32)
    for j in range(len(degrees)):
        scalars_ref[16 * nodes + j : 16 * nodes + j + 1, :] = jnp.full((1, 128), chaos[j], f32)
    for copy in copies[3:]:
        copy.wait()
    side = [jnp.concatenate([w[span - radius : span], w[0 : tap_count - radius]], 0) for w in (wave_hi, wave_lo)]
    scale = jnp.sqrt(weights[...]) * (1.0 / (span * math.sqrt(count)))
    for k in range(kernels):
        parts = parts_of(taps[0, k].reshape(2 * count, tap_count))
        prod = mm3(parts, side)
        amount = scale[0:1, k : k + 1]
        gr_ref[k] = (prod[:count, :span] - prod[count:, span:]) * amount
        gi_ref[k] = (prod[:count, span:] + prod[count:, :span]) * amount


def forward_kernel(
    radius, tiles, tile, scalars, packed, twin, border, gr, gi, cs, wave_hi, wave_lo,
    image_ref, slope_ref, fields_ref, bh, bl, x, total,
):
    kernels, count, span = gr.shape
    nodes, slab, cols = image_ref.shape
    rows = slope_ref.shape[0]
    share = rows // nodes
    half = share // 2
    even = lax.rem(tile[0], 2) == 0
    near = (lanes((2 * count, cols)) < 2 * radius) == even
    pair = []
    for part in range(2):
        at = pl.ds(2 * part * count, 2 * count)
        beyond = jnp.where(near, twin[at, :].astype(f32), border[at, :].astype(f32))
        pair.append(jnp.concatenate([packed[at, :], beyond.astype(bf16)], 1))
    wave = (wave_hi[...], wave_lo[...])
    prod = mm3(pair, wave)
    a_re = prod[:count, :span] + prod[count:, span:]
    a_im = prod[count:, :span] - prod[:count, span:]
    for k in range(kernels):
        b_re = gr[k] * a_re - gi[k] * a_im
        b_im = gr[k] * a_im + gi[k] * a_re
        for d, value in ((0, b_re), (1, b_im)):
            at = pl.ds((2 * k + d) * count, count)
            bh[at, :], bl[at, :] = parts_of(value)
    outer = outer_lanes((count, cols), radius)
    for k in range(kernels):
        if k % 2 == 0:
            at = pl.ds(2 * k * count, 2 * 2 * count)
            qq = mm3((bh[at, :], bl[at, :]), wave)
        q = qq[(k % 2) * 2 * count : (k % 2 + 1) * 2 * count]
        re = q[:count, :span] - q[count:, span:]
        im = q[:count, span:] + q[count:, :span]
        edge = jnp.where(outer, re[:, cols:], turned(im[:, cols:]))
        cross = jnp.where(outer, im[:, cols:], -turned(re[:, cols:]))
        straight = jnp.concatenate([re[:, :cols], im[:, :cols], edge], 1)
        crossed = jnp.concatenate([im[:, :cols], -re[:, :cols], cross], 1)
        for d, value in ((0, straight), (1, crossed)):
            high, low = parts_of(value)
            at = 3 * cols * (k % 2)
            for place, part in ((0, high), (1, low), (2, high)):
                x[k // 2, d, place * count : (place + 1) * count, at : at + 3 * cols] = part
    for pair in range(kernels // 2):
        even_part = mm(cs[: rows // 2, :], x[pair, 0])
        odd_part = mm(cs[rows // 2 :, :], x[pair, 1])
        for first, field in ((0, even_part - odd_part), (rows // 2, even_part + odd_part)):
            at = pl.ds(first, rows // 2)
            fields_ref[2 * pair, at, :] = field[:, : 3 * cols]
            fields_ref[2 * pair + 1, at, :] = field[:, 3 * cols :]
            square = field * field
            inner = square[:, :cols] + square[:, cols : 2 * cols]
            inner = inner + (square[:, 3 * cols : 4 * cols] + square[:, 4 * cols : 5 * cols])
            edge = square[:, 2 * cols : 3 * cols] + square[:, 5 * cols :]
            if pair:
                inner, edge = inner + total[at, :cols], edge + total[at, cols:]
            total[at, :cols] = inner
            total[at, cols:] = edge

    value = scalars[15:16, :]
    inner = total[:, :cols]
    edge = total[:, cols:]
    edge = edge + turned(edge)
    right = right_lanes((rows, cols), radius)
    inside = (right & (tile[0] < tiles - 1)) | (jnp.logical_not(right) & (tile[0] > 0))
    outer = outer_lanes((half, cols), radius)
    for place, intensity in ((0, inner), (1, edge)):
        resist = jax.nn.sigmoid(resist_slope * (value * intensity - resist_level))
        slope = resist * (1.0 - resist) * (2.0 * resist_slope * value)
        if place:
            slope = jnp.where(inside, slope, 0.0)
        slope_ref[:, place * cols : (place + 1) * cols] = slope
        for n in range(nodes):
            rows_n = resist[n * share : (n + 1) * share]
            if place:
                image_ref[n, share:slab, :] = jnp.where(outer, rows_n[:half], rows_n[half:]).astype(bf16)
            else:
                image_ref[n, 0:share, :] = rows_n.astype(bf16)


def middle_kernel(radius, offset, tile, images, wanted, twin, border, scalars, pressure_ref):
    nodes, slab, cols = images.shape
    share = wanted.shape[1]
    step = slab - share
    near = right_lanes((step, cols), radius) == (lax.rem(tile[0], 2) == 0)
    for first in range(0, slab, step):
        image = [images[n, first : first + step, :].astype(f32) for n in range(nodes)]
        pressure = [None] * nodes
        for j in range(len(degrees)):
            weight = [scalars[16 * n + j : 16 * n + j + 1, :] for n in range(nodes)]
            coefficient = weight[0] * image[0]
            for n in range(1, nodes):
                coefficient = coefficient + weight[n] * image[n]
            if first < share:
                goal = wanted[j, first : first + step, :].astype(f32)
            else:
                at = pl.ds(offset + j * step, step)
                goal = jnp.where(near, twin[at, :].astype(f32), border[at, :].astype(f32))
            mixed = scalars[16 * nodes + j : 16 * nodes + j + 1, :] * jnp.tanh(coefficient - goal)
            for n in range(nodes):
                term = weight[n] * mixed
                pressure[n] = term if j == 0 else pressure[n] + term
        for n in range(nodes):
            pressure_ref[n, first : first + step, :] = pressure[n]


def backward_kernel(radius, pressure, slope, fields, fh, fl, gr, gi, u, wave_hi, wave_lo, out_ref, dh, dl, scale):
    kernels, count, span = gr.shape
    nodes, slab, cols = pressure.shape
    rows = slope.shape[0]
    share = rows // nodes
    half = share // 2
    outer = outer_lanes((half, cols), radius)
    for n in range(nodes):
        at = pl.ds(n * share, share)
        scale[at, :cols] = slope[at, :cols] * pressure[n, :share, :]
        edge = pressure[n, share:, :]
        back = turned(edge)
        top, bottom = pl.ds(n * share, half), pl.ds(n * share + half, half)
        scale[top, cols:] = slope[top, cols:] * jnp.where(outer, edge, back)
        scale[bottom, cols:] = slope[bottom, cols:] * jnp.where(outer, back, edge)
    table = []
    for first in (0, count):
        table.append(jnp.concatenate([fh[first : first + count, : rows // 2], fl[first : first + count, : rows // 2]], 0))
    outer = outer_lanes((count, cols), radius)

    for pair in range(0, kernels, 2):
        halves = []
        for first in (0, rows // 2):
            at = pl.ds(first, rows // 2)
            inner, edge = scale[at, :cols], scale[at, cols:]
            both = jnp.concatenate([fields[pair, at, :], fields[pair + 1, at, :]], 1)
            halves.append(both * jnp.concatenate([inner, inner, edge] * 2, 1))
        grads = []
        for lhs, value in zip(table, (halves[0] + halves[1], halves[0] - halves[1])):
            high, low = parts_of(value)
            prod = mm(lhs, high)
            grads.append(prod[:count] + prod[count:] + mm(lhs[:count], low))
        for k in (pair, pair + 1):
            straight, crossed = (g[:, 3 * cols * (k - pair) : 3 * cols * (k - pair + 1)] for g in grads)
            edge, cross = straight[:, 2 * cols :], crossed[:, 2 * cols :]
            re_edge = jnp.where(outer, edge - turned(cross), 0.0)
            im_edge = jnp.where(outer, cross + turned(edge), 0.0)
            re = jnp.concatenate([straight[:, :cols] - crossed[:, cols : 2 * cols], re_edge], 1)
            im = jnp.concatenate([straight[:, cols : 2 * cols] + crossed[:, :cols], im_edge], 1)
            for d, value in ((0, re), (1, im)):
                at = pl.ds((2 * k + d) * count, count)
                dh[at, :], dl[at, :] = parts_of(value)

    wave = (wave_hi[...], wave_lo[...])
    a_re = jnp.zeros((count, span), f32)
    a_im = jnp.zeros((count, span), f32)
    for k in range(kernels):
        if k % 2 == 0:
            at = pl.ds(2 * k * count, 2 * 2 * count)
            qq = mm3((dh[at, :], dl[at, :]), wave)
        q = qq[(k % 2) * 2 * count : (k % 2 + 1) * 2 * count]
        b_re = q[:count, :span] + q[count:, span:]
        b_im = q[count:, :span] - q[:count, span:]
        a_re = a_re + gr[k] * b_re + gi[k] * b_im
        a_im = a_im + gr[k] * b_im - gi[k] * b_re
    near = [jnp.concatenate([w[:, 0:cols], w[:, span : span + cols]], 1) for w in (wave_hi, wave_lo)]
    prod = mm3(parts_of(jnp.concatenate([a_re, a_im], 0)), near)
    d_re = prod[:count, :cols] - prod[count:, cols:]
    d_im = prod[:count, cols:] + prod[count:, :cols]
    rest = jnp.zeros((128 - 2 * count, cols), f32)
    high, low = parts_of(jnp.concatenate([d_re, d_im, rest], 0))
    spread = mm(u[...], jnp.concatenate([high, low, high], 0)) * (1.0 / math.sqrt(rows))
    largest = jnp.max(jnp.abs(spread), axis=0, keepdims=True)
    power = jnp.ceil(jnp.log2(jnp.maximum(largest, 1e-30)))
    spread = spread * jnp.exp2(-power)
    for n in range(nodes):
        out_ref[n, :share, :] = spread[n * share : (n + 1) * share]
        out_ref[n, share:, :] = jnp.broadcast_to(power, (out_ref.shape[1] - share, cols))


def shape_of(*shape, dtype=f32):
    return jax.ShapeDtypeStruct(shape, dtype)


def call(kernel, mebibytes, spaces, outs, scratch=()):
    return pl.pallas_call(
        kernel,
        in_specs=spaces,
        out_specs=[vmem] * len(outs),
        out_shape=list(outs),
        scratch_shapes=list(scratch),
        compiler_params=pltpu.CompilerParams(vmem_limit_bytes=mebibytes << 20),
    )


def kept(*arrays):
    return [pltpu.with_memory_space_constraint(a, pltpu.HBM) for a in arrays]


def local(mask, taps, weights, node_weights, node_index, freq, chaos, target):
    rows, cols = mask.shape
    kernels, count, tap_count = taps.shape[1], taps.shape[3], taps.shape[4]
    terms = target.shape[0]
    radius = (tap_count - 1) // 2
    span = 2 * cols
    nodes, tiles = lax.axis_size("node"), lax.axis_size("tile")
    node, tile = lax.axis_index("node").reshape(1), lax.axis_index("tile").reshape(1)
    share = rows // nodes
    half = share // 2
    slab = share + half
    inside = [(i, i ^ 1) for i in range(tiles) if i ^ 1 < tiles]
    across = [(i, ((i + 1) ^ 1) - 1) for i in range(tiles) if 0 <= ((i + 1) ^ 1) - 1 < tiles]
    wave_hi, wave_lo = (jnp.asarray(w) for w in column_waves(span))
    packed, wanted, fh, fl, staged, wave_hi, wave_lo, turns = call(
        functools.partial(spectrum_kernel, radius),
        8,
        [smem] + [hbm] * 6,
        [
            shape_of(4 * count + half * terms, cols, dtype=bf16),
            shape_of(terms, share, cols, dtype=bf16),
            shape_of(2 * count, rows, dtype=bf16),
            shape_of(2 * count, rows, dtype=bf16),
            shape_of(*taps.shape),
            shape_of(span, 2 * span, dtype=bf16),
            shape_of(span, 2 * span, dtype=bf16),
            shape_of(8, 256, dtype=jnp.int32),
        ],
        [
            pltpu.SMEM(freq.shape, jnp.int32),
            pltpu.VMEM(mask.shape, f32),
            pltpu.VMEM((terms, share, cols), bf16),
            pltpu.SemaphoreType.DMA((6,)),
        ],
    )(node, *kept(freq, mask, target, taps, wave_hi, wave_lo))
    border = lax.ppermute(packed, "tile", across)
    twin = lax.ppermute(packed, "tile", inside)
    u, cs, gr, gi, scalars = call(
        tables_kernel,
        16,
        [smem, vmem] + [hbm] * 4 + [vmem] + [vmem] * 2,
        [
            shape_of(rows, 384, dtype=bf16),
            shape_of(rows, 3 * count, dtype=bf16),
            shape_of(kernels, count, span),
            shape_of(kernels, count, span),
            shape_of(16 * nodes + 16, 128),
        ],
        [
            pltpu.SMEM((2, nodes), jnp.int32),
            pltpu.SMEM((nodes,), f32),
            pltpu.SMEM(chaos.shape, f32),
            pltpu.VMEM(weights.shape, f32),
            pltpu.SemaphoreType.DMA((4,)),
        ],
    )(node, turns, *kept(node_index.T, node_weights, chaos, weights), staged, wave_hi, wave_lo)
    image, slope, fields = call(
        functools.partial(forward_kernel, radius, tiles),
        20,
        [smem] + [vmem] * 9,
        [
            shape_of(nodes, slab, cols, dtype=bf16),
            shape_of(rows, 2 * cols),
            shape_of(kernels, rows, 3 * cols),
        ],
        [
            pltpu.VMEM((2 * kernels * count, span), bf16),
            pltpu.VMEM((2 * kernels * count, span), bf16),
            pltpu.VMEM((kernels // 2, 2, 3 * count, 6 * cols), bf16),
            pltpu.VMEM((rows, 2 * cols), f32),
        ],
    )(tile, scalars, packed, twin, border, gr, gi, cs, wave_hi, wave_lo)
    images = lax.all_to_all(image, "node", 0, 0)
    (pressure,) = call(
        functools.partial(middle_kernel, radius, 4 * count), 8, [smem] + [vmem] * 5, [shape_of(nodes, slab, cols)]
    )(tile, images, wanted, twin, border, scalars)
    pressure = lax.all_to_all((pressure * 8192.0).astype(jnp.float16), "node", 0, 0).astype(f32) * (1.0 / 8192.0)
    (spread,) = call(
        functools.partial(backward_kernel, radius),
        16,
        [vmem] * 10,
        [shape_of(nodes, share + 8, cols)],
        [
            pltpu.VMEM((2 * kernels * count, span), bf16),
            pltpu.VMEM((2 * kernels * count, span), bf16),
            pltpu.VMEM((rows, 2 * cols), f32),
        ],
    )(pressure, slope, fields, fh, fl, gr, gi, u, wave_hi, wave_lo)
    spread = lax.all_to_all(spread.astype(jnp.float16), "node", 0, 0).astype(f32)
    return (spread[:, :share] * jnp.exp2(spread[:, share : share + 1])).sum(0)


def solution(mesh):
    placed = (
        P(None, "tile"),
        P("node", None, None, None, None),
        P("node", None),
        P(),
        P(),
        P(),
        P(),
        P(None, None, "tile"),
    )
    return jax.shard_map(local, mesh=mesh, in_specs=placed, out_specs=P("node", "tile"), check_vma=False)
```

```python
import functools
import math

import jax
import jax.numpy as jnp
import ml_dtypes
import numpy as np
from jax import lax
from jax.experimental import pallas as pl
from jax.experimental.pallas import tpu as pltpu
from jax.sharding import PartitionSpec as P

LEVELS = 5
resist_slope = 4.0
resist_level = 0.6
degrees = [(d - q, q) for d in range(5) for q in range(d + 1)]
f32, bf16 = jnp.float32, jnp.bfloat16
vmem = pl.BlockSpec(memory_space=pltpu.VMEM)
smem = pl.BlockSpec(memory_space=pltpu.SMEM)
hbm = pl.BlockSpec(memory_space=pltpu.HBM)


def parts_of(value):
    high = value.astype(bf16)
    return high, (value - high.astype(f32)).astype(bf16)


def mm(a, b):
    return jnp.dot(a, b, preferred_element_type=f32)


def mm3(a, b):
    return mm(jnp.concatenate([a[0], a[0], a[1]], 1), jnp.concatenate([b[0], b[1], b[0]], 0))


def cosine(turn, period):
    turn = jnp.bitwise_and(turn, period - 1)
    half = jnp.minimum(turn, period - turn)
    far = half > period // 4
    angle = jnp.where(far, period // 2 - half, half).astype(f32) * (2.0 * math.pi / period)
    z = angle * angle
    poly = jnp.full_like(z, 1.0 / math.factorial(12))
    for order in (10, 8, 6, 4, 2, 0):
        sign = -1.0 if order % 4 == 2 else 1.0
        poly = poly * z + sign / math.factorial(order)
    return jnp.where(far, -poly, poly)


def column_waves(length):
    turn = (np.arange(length)[:, None] * np.arange(length)[None, :]) % length
    wave = np.concatenate([np.cos(2 * np.pi * turn / length), np.sin(2 * np.pi * turn / length)], 1)
    high = wave.astype(np.float32).astype(ml_dtypes.bfloat16)
    low = (wave - high.astype(np.float64)).astype(np.float32).astype(ml_dtypes.bfloat16)
    return high, low


def lanes(shape):
    return lax.broadcasted_iota(jnp.int32, shape, len(shape) - 1)


def turned(value):
    return pltpu.roll(value, value.shape[-1] // 2, len(value.shape) - 1)


def outer_lanes(shape, radius):
    lane = lanes(shape)
    return (lane < radius) | (lane >= shape[-1] - radius)


def right_lanes(shape, radius):
    lane, half = lanes(shape), shape[-1] // 2
    return (lane < radius) | ((lane >= half) & (lane < half + radius))


def spectrum_kernel(
    radius, node, freq_in, mask_in, target_in, taps_in, wave_hi_in, wave_lo_in,
    packed_ref, wanted_ref, fh_ref, fl_ref, taps, wave_hi, wave_lo, turns_ref, freq, mask, raw, sems,
):
    rows, cols = mask.shape
    count = freq.shape[0]
    terms, share = raw.shape[0], raw.shape[1]
    own = node[0]
    mirrored = own >= rows // (2 * share)
    at = jnp.where(mirrored, rows + rows // 2 - share - own * share, own * share)
    at = pl.multiple_of(at, share)
    moves = [(freq_in, freq), (mask_in, mask), (target_in.at[:, pl.ds(at, share), :], raw)]
    moves += [(taps_in, taps), (wave_hi_in, wave_hi), (wave_lo_in, wave_lo)]
    copies = [pltpu.make_async_copy(source, goal, sems.at[i]) for i, (source, goal) in enumerate(moves)]
    for copy in copies:
        copy.start()
    copies[0].wait()
    line = lax.broadcasted_iota(jnp.int32, (2 * count, 128), 0)
    f_freq = jnp.zeros((2 * count, 128), jnp.int32)
    lane = lanes((8, 256))
    turns = jnp.zeros((8, 256), jnp.int32)
    for i in range(count):
        f_freq = jnp.where((line == i) | (line == i + count), freq[i], f_freq)
        turns = jnp.where((lane == i) | (lane == i + count) | (lane == i + 2 * count), freq[i], turns)
    turns_ref[...] = turns
    f_full = jnp.concatenate([f_freq] * (rows // 128), 1)
    f_row = lax.broadcasted_iota(jnp.int32, (2 * count, rows), 0)
    turn = f_full * (2 * lanes((2 * count, rows)) + 1) + jnp.where(f_row >= count, rows // 2, 0)
    f_parts = parts_of(cosine(turn, 2 * rows))
    fh_ref[...], fl_ref[...] = f_parts
    copies[2].wait()
    row = lax.broadcasted_iota(jnp.int32, (share, share), 0)
    chosen = jnp.where(mirrored, share - 1 - row, row) == lanes((share, share))
    order = jnp.where(chosen, 1.0, 0.0).astype(bf16)
    half = share // 2
    outer = outer_lanes((half, cols), radius)
    for j in range(terms):
        goal = mm(order, raw[j])
        wanted_ref[j] = goal.astype(bf16)
        edge = jnp.where(outer, goal[:half], turned(goal[half:]))
        packed_ref[4 * count + half * j : 4 * count + half * (j + 1), :] = edge.astype(bf16)
    copies[1].wait()
    high, low = parts_of(mm3(f_parts, parts_of(mask[...])) * (1.0 / math.sqrt(rows)))
    packed_ref[0 : 2 * count, :] = high
    packed_ref[2 * count : 4 * count, :] = low
    for copy in copies[3:]:
        copy.wait()


def tables_kernel(
    node, turns_ref, index_in, node_weights_in, chaos_in, weights_in, taps, wave_hi, wave_lo,
    u_ref, cs_ref, gr_ref, gi_ref, scalars_ref,
    index, node_weights, chaos, weights, sems,
):
    rows = u_ref.shape[0]
    kernels, count, tap_count = taps.shape[1], taps.shape[3], taps.shape[4]
    span = wave_hi.shape[0]
    radius = (tap_count - 1) // 2
    nodes = index.shape[1]
    moves = [
        (index_in, index),
        (node_weights_in, node_weights),
        (chaos_in, chaos),
        (weights_in, weights),
    ]
    copies = [pltpu.make_async_copy(source, goal, sems.at[i]) for i, (source, goal) in enumerate(moves)]
    for copy in copies:
        copy.start()
    turns = turns_ref[...]
    quarter = rows // 2
    steps = lax.broadcasted_iota(jnp.int32, (8, 256), 0)

    def spread_out(frequency, first, lead):
        width = frequency.shape[1]
        full = jnp.concatenate([frequency] * (first // 8), 0)
        turn = full * (2 * lax.broadcasted_iota(jnp.int32, (first, width), 0) + 1) + lead
        jump = frequency * (2 * first * steps[:, :width])
        return [cosine(t, 2 * rows) for t in (turn, turn - quarter, jump, jump - quarter)]

    first = rows // 8
    lane = lanes((first, 128))
    c, s, step_c, step_s = spread_out(turns[:, :128], first, jnp.where(lane >= count, quarter, 0))
    for i in range(8):
        table = c * step_c[i : i + 1, :] - s * step_s[i : i + 1, :]
        high, low = parts_of(jnp.where(lane < 2 * count, table, 0.0))
        at = pl.ds(i * first, first)
        u_ref[at, 0:128] = high
        u_ref[at, 128:256] = high
        u_ref[at, 256:384] = low
    first = rows // 16
    lane = lanes((first, 256))
    c, s, step_c, step_s = spread_out(turns, first, 0)
    for i in range(8):
        by_c, by_s = step_c[i : i + 1, :], step_s[i : i + 1, :]
        for start, table in ((0, c * by_c - s * by_s), (rows // 2, s * by_c + c * by_s)):
            high, low = parts_of(table)
            both = jnp.where(lane < 2 * count, high.astype(f32), low.astype(f32))
            cs_ref[start + i * first : start + (i + 1) * first, :] = both[:, : 3 * count].astype(bf16)
    for copy in copies[:3]:
        copy.wait()
    for n in range(nodes):
        poly = []
        for axis in range(2):
            c = index[axis, n].astype(f32) * (2.0 / (LEVELS - 1)) - 1.0
            s = c * c
            poly.append([None, c, 1.5 * s - 0.5, (2.5 * s - 1.5) * c, (4.375 * s - 3.75) * s + 0.375])
        weight = node_weights[n]
        for j, (p, q) in enumerate(degrees):
            value = weight
            if p:
                value = value * poly[0][p]
            if q:
                value = value * poly[1][q]
            scalars_ref[16 * n + j : 16 * n + j + 1, :] = jnp.full((1, 128), value, f32)
    dose = 1.0 + 0.1 * (index[1, node[0]].astype(f32) * (2.0 / (LEVELS - 1)) - 1.0)
    scalars_ref[15:16, :] = jnp.full((1, 128), dose, f32)
    for j in range(len(degrees)):
        scalars_ref[16 * nodes + j : 16 * nodes + j + 1, :] = jnp.full((1, 128), chaos[j], f32)
    for copy in copies[3:]:
        copy.wait()
    side = [jnp.concatenate([w[span - radius : span], w[0 : tap_count - radius]], 0) for w in (wave_hi, wave_lo)]
    scale = jnp.sqrt(weights[...]) * (1.0 / (span * math.sqrt(count)))
    for k in range(kernels):
        parts = parts_of(taps[0, k].reshape(2 * count, tap_count))
        prod = mm3(parts, side)
        amount = scale[0:1, k : k + 1]
        gr_ref[k] = (prod[:count, :span] - prod[count:, span:]) * amount
        gi_ref[k] = (prod[:count, span:] + prod[count:, :span]) * amount


def forward_kernel(
    radius, tiles, tile, scalars, packed, border, twin, gr, gi, cs, wave_hi, wave_lo,
    image_ref, slope_ref, fields_ref, bh, bl, x, total,
):
    kernels, count, span = gr.shape
    nodes, slab, cols = image_ref.shape
    rows = slope_ref.shape[0]
    share = rows // nodes
    half = share // 2
    even = lax.rem(tile[0], 2) == 0
    near = (lanes((2 * count, cols)) < 2 * radius) == even
    pair = []
    for part in range(2):
        at = pl.ds(2 * part * count, 2 * count)
        beyond = jnp.where(near, twin[at, :].astype(f32), border[at, :].astype(f32))
        pair.append(jnp.concatenate([packed[at, :], beyond.astype(bf16)], 1))
    wave = (wave_hi[...], wave_lo[...])
    prod = mm3(pair, wave)
    a_re = prod[:count, :span] + prod[count:, span:]
    a_im = prod[count:, :span] - prod[:count, span:]
    for k in range(kernels):
        b_re = gr[k] * a_re - gi[k] * a_im
        b_im = gr[k] * a_im + gi[k] * a_re
        for d, value in ((0, b_re), (1, b_im)):
            at = pl.ds((2 * k + d) * count, count)
            bh[at, :], bl[at, :] = parts_of(value)
    outer = outer_lanes((count, cols), radius)
    for k in range(kernels):
        if k % 2 == 0:
            at = pl.ds(2 * k * count, 2 * 2 * count)
            qq = mm3((bh[at, :], bl[at, :]), wave)
        q = qq[(k % 2) * 2 * count : (k % 2 + 1) * 2 * count]
        re = q[:count, :span] - q[count:, span:]
        im = q[:count, span:] + q[count:, :span]
        edge = jnp.where(outer, re[:, cols:], turned(im[:, cols:]))
        cross = jnp.where(outer, im[:, cols:], -turned(re[:, cols:]))
        straight = jnp.concatenate([re[:, :cols], im[:, :cols], edge], 1)
        crossed = jnp.concatenate([im[:, :cols], -re[:, :cols], cross], 1)
        for d, value in ((0, straight), (1, crossed)):
            high, low = parts_of(value)
            at = 3 * cols * (k % 2)
            for place, part in ((0, high), (1, low), (2, high)):
                x[k // 2, d, place * count : (place + 1) * count, at : at + 3 * cols] = part
    for pair in range(kernels // 2):
        even_part = mm(cs[: rows // 2, :], x[pair, 0])
        odd_part = mm(cs[rows // 2 :, :], x[pair, 1])
        for first, field in ((0, even_part - odd_part), (rows // 2, even_part + odd_part)):
            at = pl.ds(first, rows // 2)
            fields_ref[2 * pair, at, :] = field[:, : 3 * cols]
            fields_ref[2 * pair + 1, at, :] = field[:, 3 * cols :]
            square = field * field
            inner = square[:, :cols] + square[:, cols : 2 * cols]
            inner = inner + (square[:, 3 * cols : 4 * cols] + square[:, 4 * cols : 5 * cols])
            edge = square[:, 2 * cols : 3 * cols] + square[:, 5 * cols :]
            if pair:
                inner, edge = inner + total[at, :cols], edge + total[at, cols:]
            total[at, :cols] = inner
            total[at, cols:] = edge

    value = scalars[15:16, :]
    inner = total[:, :cols]
    edge = total[:, cols:]
    edge = edge + turned(edge)
    right = right_lanes((rows, cols), radius)
    inside = (right & (tile[0] < tiles - 1)) | (jnp.logical_not(right) & (tile[0] > 0))
    outer = outer_lanes((half, cols), radius)
    for place, intensity in ((0, inner), (1, edge)):
        resist = jax.nn.sigmoid(resist_slope * (value * intensity - resist_level))
        slope = resist * (1.0 - resist) * (2.0 * resist_slope * value)
        if place:
            slope = jnp.where(inside, slope, 0.0)
        slope_ref[:, place * cols : (place + 1) * cols] = slope
        for n in range(nodes):
            rows_n = resist[n * share : (n + 1) * share]
            if place:
                image_ref[n, share:slab, :] = jnp.where(outer, rows_n[:half], rows_n[half:]).astype(bf16)
            else:
                image_ref[n, 0:share, :] = rows_n.astype(bf16)


def middle_kernel(radius, offset, tile, images, wanted, border, twin, scalars, pressure_ref):
    nodes, slab, cols = images.shape
    share = wanted.shape[1]
    step = slab - share
    near = right_lanes((step, cols), radius) == (lax.rem(tile[0], 2) == 0)
    for first in range(0, slab, step):
        image = [images[n, first : first + step, :].astype(f32) for n in range(nodes)]
        pressure = [None] * nodes
        for j in range(len(degrees)):
            weight = [scalars[16 * n + j : 16 * n + j + 1, :] for n in range(nodes)]
            coefficient = weight[0] * image[0]
            for n in range(1, nodes):
                coefficient = coefficient + weight[n] * image[n]
            if first < share:
                goal = wanted[j, first : first + step, :].astype(f32)
            else:
                at = pl.ds(offset + j * step, step)
                goal = jnp.where(near, twin[at, :].astype(f32), border[at, :].astype(f32))
            mixed = scalars[16 * nodes + j : 16 * nodes + j + 1, :] * jnp.tanh(coefficient - goal)
            for n in range(nodes):
                term = weight[n] * mixed
                pressure[n] = term if j == 0 else pressure[n] + term
        for n in range(nodes):
            pressure_ref[n, first : first + step, :] = pressure[n]


def backward_kernel(radius, pressure, slope, fields, fh, fl, gr, gi, u, wave_hi, wave_lo, out_ref, dh, dl, scale):
    kernels, count, span = gr.shape
    nodes, slab, cols = pressure.shape
    rows = slope.shape[0]
    share = rows // nodes
    half = share // 2
    outer = outer_lanes((half, cols), radius)
    for n in range(nodes):
        at = pl.ds(n * share, share)
        scale[at, :cols] = slope[at, :cols] * pressure[n, :share, :]
        edge = pressure[n, share:, :]
        back = turned(edge)
        top, bottom = pl.ds(n * share, half), pl.ds(n * share + half, half)
        scale[top, cols:] = slope[top, cols:] * jnp.where(outer, edge, back)
        scale[bottom, cols:] = slope[bottom, cols:] * jnp.where(outer, back, edge)
    table = []
    for first in (0, count):
        table.append(jnp.concatenate([fh[first : first + count, : rows // 2], fl[first : first + count, : rows // 2]], 0))
    outer = outer_lanes((count, cols), radius)

    for pair in range(0, kernels, 2):
        halves = []
        for first in (0, rows // 2):
            at = pl.ds(first, rows // 2)
            inner, edge = scale[at, :cols], scale[at, cols:]
            both = jnp.concatenate([fields[pair, at, :], fields[pair + 1, at, :]], 1)
            halves.append(both * jnp.concatenate([inner, inner, edge] * 2, 1))
        grads = []
        for lhs, value in zip(table, (halves[0] + halves[1], halves[0] - halves[1])):
            high, low = parts_of(value)
            prod = mm(lhs, high)
            grads.append(prod[:count] + prod[count:] + mm(lhs[:count], low))
        for k in (pair, pair + 1):
            straight, crossed = (g[:, 3 * cols * (k - pair) : 3 * cols * (k - pair + 1)] for g in grads)
            edge, cross = straight[:, 2 * cols :], crossed[:, 2 * cols :]
            re_edge = jnp.where(outer, edge - turned(cross), 0.0)
            im_edge = jnp.where(outer, cross + turned(edge), 0.0)
            re = jnp.concatenate([straight[:, :cols] - crossed[:, cols : 2 * cols], re_edge], 1)
            im = jnp.concatenate([straight[:, cols : 2 * cols] + crossed[:, :cols], im_edge], 1)
            for d, value in ((0, re), (1, im)):
                at = pl.ds((2 * k + d) * count, count)
                dh[at, :], dl[at, :] = parts_of(value)

    wave = (wave_hi[...], wave_lo[...])
    a_re = jnp.zeros((count, span), f32)
    a_im = jnp.zeros((count, span), f32)
    for k in range(kernels):
        if k % 2 == 0:
            at = pl.ds(2 * k * count, 2 * 2 * count)
            qq = mm3((dh[at, :], dl[at, :]), wave)
        q = qq[(k % 2) * 2 * count : (k % 2 + 1) * 2 * count]
        b_re = q[:count, :span] + q[count:, span:]
        b_im = q[count:, :span] - q[:count, span:]
        a_re = a_re + gr[k] * b_re + gi[k] * b_im
        a_im = a_im + gr[k] * b_im - gi[k] * b_re
    near = [jnp.concatenate([w[:, 0:cols], w[:, span : span + cols]], 1) for w in (wave_hi, wave_lo)]
    prod = mm3(parts_of(jnp.concatenate([a_re, a_im], 0)), near)
    d_re = prod[:count, :cols] - prod[count:, cols:]
    d_im = prod[:count, cols:] + prod[count:, :cols]
    rest = jnp.zeros((128 - 2 * count, cols), f32)
    high, low = parts_of(jnp.concatenate([d_re, d_im, rest], 0))
    spread = mm(u[...], jnp.concatenate([high, low, high], 0)) * (1.0 / math.sqrt(rows))
    largest = jnp.max(jnp.abs(spread), axis=0, keepdims=True)
    power = jnp.ceil(jnp.log2(jnp.maximum(largest, 1e-30)))
    spread = spread * jnp.exp2(-power)
    for n in range(nodes):
        out_ref[n, :share, :] = spread[n * share : (n + 1) * share]
        out_ref[n, share:, :] = jnp.broadcast_to(power, (out_ref.shape[1] - share, cols))


def shape_of(*shape, dtype=f32):
    return jax.ShapeDtypeStruct(shape, dtype)


def call(kernel, mebibytes, spaces, outs, scratch=()):
    return pl.pallas_call(
        kernel,
        in_specs=spaces,
        out_specs=[vmem] * len(outs),
        out_shape=list(outs),
        scratch_shapes=list(scratch),
        compiler_params=pltpu.CompilerParams(vmem_limit_bytes=mebibytes << 20),
    )


def kept(*arrays):
    return [pltpu.with_memory_space_constraint(a, pltpu.HBM) for a in arrays]


def local(mask, taps, weights, node_weights, node_index, freq, chaos, target):
    rows, cols = mask.shape
    kernels, count, tap_count = taps.shape[1], taps.shape[3], taps.shape[4]
    terms = target.shape[0]
    radius = (tap_count - 1) // 2
    span = 2 * cols
    nodes, tiles = lax.axis_size("node"), lax.axis_size("tile")
    node, tile = lax.axis_index("node").reshape(1), lax.axis_index("tile").reshape(1)
    share = rows // nodes
    half = share // 2
    slab = share + half
    inside = [(i, i ^ 1) for i in range(tiles) if i ^ 1 < tiles]
    across = [(i, ((i + 1) ^ 1) - 1) for i in range(tiles) if 0 <= ((i + 1) ^ 1) - 1 < tiles]
    wave_hi, wave_lo = (jnp.asarray(w) for w in column_waves(span))
    packed, wanted, fh, fl, staged, wave_hi, wave_lo, turns = call(
        functools.partial(spectrum_kernel, radius),
        8,
        [smem] + [hbm] * 6,
        [
            shape_of(4 * count + half * terms, cols, dtype=bf16),
            shape_of(terms, share, cols, dtype=bf16),
            shape_of(2 * count, rows, dtype=bf16),
            shape_of(2 * count, rows, dtype=bf16),
            shape_of(*taps.shape),
            shape_of(span, 2 * span, dtype=bf16),
            shape_of(span, 2 * span, dtype=bf16),
            shape_of(8, 256, dtype=jnp.int32),
        ],
        [
            pltpu.SMEM(freq.shape, jnp.int32),
            pltpu.VMEM(mask.shape, f32),
            pltpu.VMEM((terms, share, cols), bf16),
            pltpu.SemaphoreType.DMA((6,)),
        ],
    )(node, *kept(freq, mask, target, taps, wave_hi, wave_lo))
    twin = lax.ppermute(packed, "tile", inside)
    border = lax.ppermute(packed, "tile", across)
    u, cs, gr, gi, scalars = call(
        tables_kernel,
        16,
        [smem, vmem] + [hbm] * 4 + [vmem] + [vmem] * 2,
        [
            shape_of(rows, 384, dtype=bf16),
            shape_of(rows, 3 * count, dtype=bf16),
            shape_of(kernels, count, span),
            shape_of(kernels, count, span),
            shape_of(16 * nodes + 16, 128),
        ],
        [
            pltpu.SMEM((2, nodes), jnp.int32),
            pltpu.SMEM((nodes,), f32),
            pltpu.SMEM(chaos.shape, f32),
            pltpu.VMEM(weights.shape, f32),
            pltpu.SemaphoreType.DMA((4,)),
        ],
    )(node, turns, *kept(node_index.T, node_weights, chaos, weights), staged, wave_hi, wave_lo)
    image, slope, fields = call(
        functools.partial(forward_kernel, radius, tiles),
        20,
        [smem] + [vmem] * 9,
        [
            shape_of(nodes, slab, cols, dtype=bf16),
            shape_of(rows, 2 * cols),
            shape_of(kernels, rows, 3 * cols),
        ],
        [
            pltpu.VMEM((2 * kernels * count, span), bf16),
            pltpu.VMEM((2 * kernels * count, span), bf16),
            pltpu.VMEM((kernels // 2, 2, 3 * count, 6 * cols), bf16),
            pltpu.VMEM((rows, 2 * cols), f32),
        ],
    )(tile, scalars, packed, border, twin, gr, gi, cs, wave_hi, wave_lo)
    images = lax.all_to_all(image, "node", 0, 0)
    (pressure,) = call(
        functools.partial(middle_kernel, radius, 4 * count), 8, [smem] + [vmem] * 5, [shape_of(nodes, slab, cols)]
    )(tile, images, wanted, border, twin, scalars)
    pressure = lax.all_to_all((pressure * 8192.0).astype(jnp.float16), "node", 0, 0).astype(f32) * (1.0 / 8192.0)
    (spread,) = call(
        functools.partial(backward_kernel, radius),
        16,
        [vmem] * 10,
        [shape_of(nodes, share + 8, cols)],
        [
            pltpu.VMEM((2 * kernels * count, span), bf16),
            pltpu.VMEM((2 * kernels * count, span), bf16),
            pltpu.VMEM((rows, 2 * cols), f32),
        ],
    )(pressure, slope, fields, fh, fl, gr, gi, u, wave_hi, wave_lo)
    spread = lax.all_to_all(spread.astype(jnp.float16), "node", 0, 0).astype(f32)
    return (spread[:, :share] * jnp.exp2(spread[:, share : share + 1])).sum(0)


def solution(mesh):
    placed = (
        P(None, "tile"),
        P("node", None, None, None, None),
        P("node", None),
        P(),
        P(),
        P(),
        P(),
        P(None, None, "tile"),
    )
    return jax.shard_map(local, mesh=mesh, in_specs=placed, out_specs=P("node", "tile"), check_vma=False)
```

```python
import functools
import math

import jax
import jax.numpy as jnp
import ml_dtypes
import numpy as np
from jax import lax
from jax.experimental import pallas as pl
from jax.experimental.pallas import tpu as pltpu
from jax.sharding import PartitionSpec as P

LEVELS = 5
resist_slope = 4.0
resist_level = 0.6
degrees = [(d - q, q) for d in range(5) for q in range(d + 1)]
f32, bf16 = jnp.float32, jnp.bfloat16
vmem = pl.BlockSpec(memory_space=pltpu.VMEM)
smem = pl.BlockSpec(memory_space=pltpu.SMEM)
hbm = pl.BlockSpec(memory_space=pltpu.HBM)


def parts_of(value):
    high = value.astype(bf16)
    return high, (value - high.astype(f32)).astype(bf16)


def mm(a, b):
    return jnp.dot(a, b, preferred_element_type=f32)


def mm3(a, b):
    return mm(jnp.concatenate([a[0], a[0], a[1]], 1), jnp.concatenate([b[0], b[1], b[0]], 0))


def cosine(turn, period):
    turn = jnp.bitwise_and(turn, period - 1)
    half = jnp.minimum(turn, period - turn)
    far = half > period // 4
    angle = jnp.where(far, period // 2 - half, half).astype(f32) * (2.0 * math.pi / period)
    z = angle * angle
    poly = jnp.full_like(z, 1.0 / math.factorial(12))
    for order in (10, 8, 6, 4, 2, 0):
        sign = -1.0 if order % 4 == 2 else 1.0
        poly = poly * z + sign / math.factorial(order)
    return jnp.where(far, -poly, poly)


def column_waves(length):
    turn = (np.arange(length)[:, None] * np.arange(length)[None, :]) % length
    wave = np.concatenate([np.cos(2 * np.pi * turn / length), np.sin(2 * np.pi * turn / length)], 1)
    high = wave.astype(np.float32).astype(ml_dtypes.bfloat16)
    low = (wave - high.astype(np.float64)).astype(np.float32).astype(ml_dtypes.bfloat16)
    return high, low


def lanes(shape):
    return lax.broadcasted_iota(jnp.int32, shape, len(shape) - 1)


def turned(value):
    return pltpu.roll(value, value.shape[-1] // 2, len(value.shape) - 1)


def outer_lanes(shape, radius):
    lane = lanes(shape)
    return (lane < radius) | (lane >= shape[-1] - radius)


def right_lanes(shape, radius):
    lane, half = lanes(shape), shape[-1] // 2
    return (lane < radius) | ((lane >= half) & (lane < half + radius))


def spectrum_kernel(
    radius, node, freq_in, mask_in, target_in, taps_in, wave_hi_in, wave_lo_in,
    packed_ref, wanted_ref, fh_ref, fl_ref, taps, wave_hi, wave_lo, turns_ref, freq, mask, raw, sems,
):
    rows, cols = mask.shape
    count = freq.shape[0]
    terms, share = raw.shape[0], raw.shape[1]
    own = node[0]
    mirrored = own >= rows // (2 * share)
    at = jnp.where(mirrored, rows + rows // 2 - share - own * share, own * share)
    at = pl.multiple_of(at, share)
    moves = [(freq_in, freq), (mask_in, mask), (target_in.at[:, pl.ds(at, share), :], raw)]
    moves += [(taps_in, taps), (wave_hi_in, wave_hi), (wave_lo_in, wave_lo)]
    copies = [pltpu.make_async_copy(source, goal, sems.at[i]) for i, (source, goal) in enumerate(moves)]
    for copy in copies:
        copy.start()
    copies[0].wait()
    line = lax.broadcasted_iota(jnp.int32, (2 * count, 128), 0)
    f_freq = jnp.zeros((2 * count, 128), jnp.int32)
    lane = lanes((8, 256))
    turns = jnp.zeros((8, 256), jnp.int32)
    for i in range(count):
        f_freq = jnp.where((line == i) | (line == i + count), freq[i], f_freq)
        turns = jnp.where((lane == i) | (lane == i + count) | (lane == i + 2 * count), freq[i], turns)
    turns_ref[...] = turns
    f_full = jnp.concatenate([f_freq] * (rows // 128), 1)
    f_row = lax.broadcasted_iota(jnp.int32, (2 * count, rows), 0)
    turn = f_full * (2 * lanes((2 * count, rows)) + 1) + jnp.where(f_row >= count, rows // 2, 0)
    f_parts = parts_of(cosine(turn, 2 * rows))
    fh_ref[...], fl_ref[...] = f_parts
    copies[2].wait()
    row = lax.broadcasted_iota(jnp.int32, (share, share), 0)
    chosen = jnp.where(mirrored, share - 1 - row, row) == lanes((share, share))
    order = jnp.where(chosen, 1.0, 0.0).astype(bf16)
    half = share // 2
    outer = outer_lanes((half, cols), radius)
    for j in range(terms):
        goal = mm(order, raw[j])
        wanted_ref[j] = goal.astype(bf16)
        edge = jnp.where(outer, goal[:half], turned(goal[half:]))
        packed_ref[4 * count + half * j : 4 * count + half * (j + 1), :] = edge.astype(bf16)
    copies[1].wait()
    high, low = parts_of(mm3(f_parts, parts_of(mask[...])) * (1.0 / math.sqrt(rows)))
    packed_ref[0 : 2 * count, :] = high
    packed_ref[2 * count : 4 * count, :] = low
    for copy in copies[3:]:
        copy.wait()


def tables_kernel(
    node, turns_ref, index_in, node_weights_in, chaos_in, weights_in, taps, wave_hi, wave_lo,
    u_ref, cs_ref, gr_ref, gi_ref, scalars_ref,
    index, node_weights, chaos, weights, sems,
):
    rows = u_ref.shape[0]
    kernels, count, tap_count = taps.shape[1], taps.shape[3], taps.shape[4]
    span = wave_hi.shape[0]
    radius = (tap_count - 1) // 2
    nodes = index.shape[1]
    moves = [
        (index_in, index),
        (node_weights_in, node_weights),
        (chaos_in, chaos),
        (weights_in, weights),
    ]
    copies = [pltpu.make_async_copy(source, goal, sems.at[i]) for i, (source, goal) in enumerate(moves)]
    for copy in copies:
        copy.start()
    turns = turns_ref[...]
    quarter = rows // 2
    steps = lax.broadcasted_iota(jnp.int32, (8, 256), 0)

    def spread_out(frequency, first, lead):
        width = frequency.shape[1]
        full = jnp.concatenate([frequency] * (first // 8), 0)
        turn = full * (2 * lax.broadcasted_iota(jnp.int32, (first, width), 0) + 1) + lead
        jump = frequency * (2 * first * steps[:, :width])
        return [cosine(t, 2 * rows) for t in (turn, turn - quarter, jump, jump - quarter)]

    first = rows // 8
    lane = lanes((first, 128))
    c, s, step_c, step_s = spread_out(turns[:, :128], first, jnp.where(lane >= count, quarter, 0))
    for i in range(8):
        table = c * step_c[i : i + 1, :] - s * step_s[i : i + 1, :]
        high, low = parts_of(jnp.where(lane < 2 * count, table, 0.0))
        at = pl.ds(i * first, first)
        u_ref[at, 0:128] = high
        u_ref[at, 128:256] = high
        u_ref[at, 256:384] = low
    first = rows // 16
    lane = lanes((first, 256))
    c, s, step_c, step_s = spread_out(turns, first, 0)
    for i in range(8):
        by_c, by_s = step_c[i : i + 1, :], step_s[i : i + 1, :]
        for start, table in ((0, c * by_c - s * by_s), (rows // 2, s * by_c + c * by_s)):
            high, low = parts_of(table)
            both = jnp.where(lane < 2 * count, high.astype(f32), low.astype(f32))
            cs_ref[start + i * first : start + (i + 1) * first, :] = both[:, : 3 * count].astype(bf16)
    for copy in copies[:3]:
        copy.wait()
    for n in range(nodes):
        poly = []
        for axis in range(2):
            c = index[axis, n].astype(f32) * (2.0 / (LEVELS - 1)) - 1.0
            s = c * c
            poly.append([None, c, 1.5 * s - 0.5, (2.5 * s - 1.5) * c, (4.375 * s - 3.75) * s + 0.375])
        weight = node_weights[n]
        for j, (p, q) in enumerate(degrees):
            value = weight
            if p:
                value = value * poly[0][p]
            if q:
                value = value * poly[1][q]
            scalars_ref[16 * n + j : 16 * n + j + 1, :] = jnp.full((1, 128), value, f32)
    dose = 1.0 + 0.1 * (index[1, node[0]].astype(f32) * (2.0 / (LEVELS - 1)) - 1.0)
    scalars_ref[15:16, :] = jnp.full((1, 128), dose, f32)
    for j in range(len(degrees)):
        scalars_ref[16 * nodes + j : 16 * nodes + j + 1, :] = jnp.full((1, 128), chaos[j], f32)
    for copy in copies[3:]:
        copy.wait()
    side = [jnp.concatenate([w[span - radius : span], w[0 : tap_count - radius]], 0) for w in (wave_hi, wave_lo)]
    scale = jnp.sqrt(weights[...]) * (1.0 / (span * math.sqrt(count)))
    for k in range(kernels):
        parts = parts_of(taps[0, k].reshape(2 * count, tap_count))
        prod = mm3(parts, side)
        amount = scale[0:1, k : k + 1]
        gr_ref[k] = (prod[:count, :span] - prod[count:, span:]) * amount
        gi_ref[k] = (prod[:count, span:] + prod[count:, :span]) * amount


def forward_kernel(
    radius, tiles, tile, scalars, packed, after, before, gr, gi, cs, wave_hi, wave_lo,
    image_ref, slope_ref, fields_ref, bh, bl, x, total,
):
    kernels, count, span = gr.shape
    nodes, slab, cols = image_ref.shape
    rows = slope_ref.shape[0]
    share = rows // nodes
    half = share // 2
    near = lanes((2 * count, cols)) < 2 * radius
    pair = []
    for part in range(2):
        at = pl.ds(2 * part * count, 2 * count)
        beyond = jnp.where(near, after[at, :].astype(f32), before[at, :].astype(f32))
        pair.append(jnp.concatenate([packed[at, :], beyond.astype(bf16)], 1))
    wave = (wave_hi[...], wave_lo[...])
    prod = mm3(pair, wave)
    a_re = prod[:count, :span] + prod[count:, span:]
    a_im = prod[count:, :span] - prod[:count, span:]
    for k in range(kernels):
        b_re = gr[k] * a_re - gi[k] * a_im
        b_im = gr[k] * a_im + gi[k] * a_re
        for d, value in ((0, b_re), (1, b_im)):
            at = pl.ds((2 * k + d) * count, count)
            bh[at, :], bl[at, :] = parts_of(value)
    outer = outer_lanes((count, cols), radius)
    for k in range(kernels):
        if k % 2 == 0:
            at = pl.ds(2 * k * count, 2 * 2 * count)
            qq = mm3((bh[at, :], bl[at, :]), wave)
        q = qq[(k % 2) * 2 * count : (k % 2 + 1) * 2 * count]
        re = q[:count, :span] - q[count:, span:]
        im = q[:count, span:] + q[count:, :span]
        edge = jnp.where(outer, re[:, cols:], turned(im[:, cols:]))
        cross = jnp.where(outer, im[:, cols:], -turned(re[:, cols:]))
        straight = jnp.concatenate([re[:, :cols], im[:, :cols], edge], 1)
        crossed = jnp.concatenate([im[:, :cols], -re[:, :cols], cross], 1)
        for d, value in ((0, straight), (1, crossed)):
            high, low = parts_of(value)
            at = 3 * cols * (k % 2)
            for place, part in ((0, high), (1, low), (2, high)):
                x[k // 2, d, place * count : (place + 1) * count, at : at + 3 * cols] = part
    for pair in range(kernels // 2):
        even_part = mm(cs[: rows // 2, :], x[pair, 0])
        odd_part = mm(cs[rows // 2 :, :], x[pair, 1])
        for first, field in ((0, even_part - odd_part), (rows // 2, even_part + odd_part)):
            at = pl.ds(first, rows // 2)
            fields_ref[2 * pair, at, :] = field[:, : 3 * cols]
            fields_ref[2 * pair + 1, at, :] = field[:, 3 * cols :]
            square = field * field
            inner = square[:, :cols] + square[:, cols : 2 * cols]
            inner = inner + (square[:, 3 * cols : 4 * cols] + square[:, 4 * cols : 5 * cols])
            edge = square[:, 2 * cols : 3 * cols] + square[:, 5 * cols :]
            if pair:
                inner, edge = inner + total[at, :cols], edge + total[at, cols:]
            total[at, :cols] = inner
            total[at, cols:] = edge

    value = scalars[15:16, :]
    inner = total[:, :cols]
    edge = total[:, cols:]
    edge = edge + turned(edge)
    right = right_lanes((rows, cols), radius)
    inside = (right & (tile[0] < tiles - 1)) | (jnp.logical_not(right) & (tile[0] > 0))
    outer = outer_lanes((half, cols), radius)
    for place, intensity in ((0, inner), (1, edge)):
        resist = jax.nn.sigmoid(resist_slope * (value * intensity - resist_level))
        slope = resist * (1.0 - resist) * (2.0 * resist_slope * value)
        if place:
            slope = jnp.where(inside, slope, 0.0)
        slope_ref[:, place * cols : (place + 1) * cols] = slope
        for n in range(nodes):
            rows_n = resist[n * share : (n + 1) * share]
            if place:
                image_ref[n, share:slab, :] = jnp.where(outer, rows_n[:half], rows_n[half:]).astype(bf16)
            else:
                image_ref[n, 0:share, :] = rows_n.astype(bf16)


def middle_kernel(radius, offset, images, wanted, after, before, scalars, pressure_ref):
    nodes, slab, cols = images.shape
    share = wanted.shape[1]
    step = slab - share
    near = right_lanes((step, cols), radius)
    for first in range(0, slab, step):
        image = [images[n, first : first + step, :].astype(f32) for n in range(nodes)]
        pressure = [None] * nodes
        for j in range(len(degrees)):
            weight = [scalars[16 * n + j : 16 * n + j + 1, :] for n in range(nodes)]
            coefficient = weight[0] * image[0]
            for n in range(1, nodes):
                coefficient = coefficient + weight[n] * image[n]
            if first < share:
                goal = wanted[j, first : first + step, :].astype(f32)
            else:
                at = pl.ds(offset + j * step, step)
                goal = jnp.where(near, after[at, :].astype(f32), before[at, :].astype(f32))
            mixed = scalars[16 * nodes + j : 16 * nodes + j + 1, :] * jnp.tanh(coefficient - goal)
            for n in range(nodes):
                term = weight[n] * mixed
                pressure[n] = term if j == 0 else pressure[n] + term
        for n in range(nodes):
            pressure_ref[n, first : first + step, :] = pressure[n]


def backward_kernel(radius, pressure, slope, fields, fh, fl, gr, gi, u, wave_hi, wave_lo, out_ref, dh, dl, scale):
    kernels, count, span = gr.shape
    nodes, slab, cols = pressure.shape
    rows = slope.shape[0]
    share = rows // nodes
    half = share // 2
    outer = outer_lanes((half, cols), radius)
    for n in range(nodes):
        at = pl.ds(n * share, share)
        scale[at, :cols] = slope[at, :cols] * pressure[n, :share, :]
        edge = pressure[n, share:, :]
        back = turned(edge)
        top, bottom = pl.ds(n * share, half), pl.ds(n * share + half, half)
        scale[top, cols:] = slope[top, cols:] * jnp.where(outer, edge, back)
        scale[bottom, cols:] = slope[bottom, cols:] * jnp.where(outer, back, edge)
    table = []
    for first in (0, count):
        table.append(jnp.concatenate([fh[first : first + count, : rows // 2], fl[first : first + count, : rows // 2]], 0))
    outer = outer_lanes((count, cols), radius)

    for pair in range(0, kernels, 2):
        halves = []
        for first in (0, rows // 2):
            at = pl.ds(first, rows // 2)
            inner, edge = scale[at, :cols], scale[at, cols:]
            both = jnp.concatenate([fields[pair, at, :], fields[pair + 1, at, :]], 1)
            halves.append(both * jnp.concatenate([inner, inner, edge] * 2, 1))
        grads = []
        for lhs, value in zip(table, (halves[0] + halves[1], halves[0] - halves[1])):
            high, low = parts_of(value)
            prod = mm(lhs, high)
            grads.append(prod[:count] + prod[count:] + mm(lhs[:count], low))
        for k in (pair, pair + 1):
            straight, crossed = (g[:, 3 * cols * (k - pair) : 3 * cols * (k - pair + 1)] for g in grads)
            edge, cross = straight[:, 2 * cols :], crossed[:, 2 * cols :]
            re_edge = jnp.where(outer, edge - turned(cross), 0.0)
            im_edge = jnp.where(outer, cross + turned(edge), 0.0)
            re = jnp.concatenate([straight[:, :cols] - crossed[:, cols : 2 * cols], re_edge], 1)
            im = jnp.concatenate([straight[:, cols : 2 * cols] + crossed[:, :cols], im_edge], 1)
            for d, value in ((0, re), (1, im)):
                at = pl.ds((2 * k + d) * count, count)
                dh[at, :], dl[at, :] = parts_of(value)

    wave = (wave_hi[...], wave_lo[...])
    a_re = jnp.zeros((count, span), f32)
    a_im = jnp.zeros((count, span), f32)
    for k in range(kernels):
        if k % 2 == 0:
            at = pl.ds(2 * k * count, 2 * 2 * count)
            qq = mm3((dh[at, :], dl[at, :]), wave)
        q = qq[(k % 2) * 2 * count : (k % 2 + 1) * 2 * count]
        b_re = q[:count, :span] + q[count:, span:]
        b_im = q[count:, :span] - q[:count, span:]
        a_re = a_re + gr[k] * b_re + gi[k] * b_im
        a_im = a_im + gr[k] * b_im - gi[k] * b_re
    near = [jnp.concatenate([w[:, 0:cols], w[:, span : span + cols]], 1) for w in (wave_hi, wave_lo)]
    prod = mm3(parts_of(jnp.concatenate([a_re, a_im], 0)), near)
    d_re = prod[:count, :cols] - prod[count:, cols:]
    d_im = prod[:count, cols:] + prod[count:, :cols]
    rest = jnp.zeros((128 - 2 * count, cols), f32)
    high, low = parts_of(jnp.concatenate([d_re, d_im, rest], 0))
    spread = mm(u[...], jnp.concatenate([high, low, high], 0)) * (1.0 / math.sqrt(rows))
    largest = jnp.max(jnp.abs(spread), axis=0, keepdims=True)
    power = jnp.ceil(jnp.log2(jnp.maximum(largest, 1e-30)))
    spread = spread * jnp.exp2(-power)
    for n in range(nodes):
        out_ref[n, :share, :] = spread[n * share : (n + 1) * share]
        out_ref[n, share:, :] = jnp.broadcast_to(power, (out_ref.shape[1] - share, cols))


def shape_of(*shape, dtype=f32):
    return jax.ShapeDtypeStruct(shape, dtype)


def call(kernel, mebibytes, spaces, outs, scratch=()):
    return pl.pallas_call(
        kernel,
        in_specs=spaces,
        out_specs=[vmem] * len(outs),
        out_shape=list(outs),
        scratch_shapes=list(scratch),
        compiler_params=pltpu.CompilerParams(vmem_limit_bytes=mebibytes << 20),
    )


def kept(*arrays):
    return [pltpu.with_memory_space_constraint(a, pltpu.HBM) for a in arrays]


def local(mask, taps, weights, node_weights, node_index, freq, chaos, target):
    rows, cols = mask.shape
    kernels, count, tap_count = taps.shape[1], taps.shape[3], taps.shape[4]
    terms = target.shape[0]
    radius = (tap_count - 1) // 2
    span = 2 * cols
    nodes, tiles = lax.axis_size("node"), lax.axis_size("tile")
    node, tile = lax.axis_index("node").reshape(1), lax.axis_index("tile").reshape(1)
    share = rows // nodes
    half = share // 2
    slab = share + half
    up = [(i, i + 1) for i in range(tiles - 1)]
    down = [(i + 1, i) for i in range(tiles - 1)]
    wave_hi, wave_lo = (jnp.asarray(w) for w in column_waves(span))
    packed, wanted, fh, fl, staged, wave_hi, wave_lo, turns = call(
        functools.partial(spectrum_kernel, radius),
        8,
        [smem] + [hbm] * 6,
        [
            shape_of(4 * count + half * terms, cols, dtype=bf16),
            shape_of(terms, share, cols, dtype=bf16),
            shape_of(2 * count, rows, dtype=bf16),
            shape_of(2 * count, rows, dtype=bf16),
            shape_of(*taps.shape),
            shape_of(span, 2 * span, dtype=bf16),
            shape_of(span, 2 * span, dtype=bf16),
            shape_of(8, 256, dtype=jnp.int32),
        ],
        [
            pltpu.SMEM(freq.shape, jnp.int32),
            pltpu.VMEM(mask.shape, f32),
            pltpu.VMEM((terms, share, cols), bf16),
            pltpu.SemaphoreType.DMA((6,)),
        ],
    )(node, *kept(freq, mask, target, taps, wave_hi, wave_lo))
    before = lax.ppermute(packed, "tile", up)
    after = lax.ppermute(packed, "tile", down)
    u, cs, gr, gi, scalars = call(
        tables_kernel,
        16,
        [smem, vmem] + [hbm] * 4 + [vmem] + [vmem] * 2,
        [
            shape_of(rows, 384, dtype=bf16),
            shape_of(rows, 3 * count, dtype=bf16),
            shape_of(kernels, count, span),
            shape_of(kernels, count, span),
            shape_of(16 * nodes + 16, 128),
        ],
        [
            pltpu.SMEM((2, nodes), jnp.int32),
            pltpu.SMEM((nodes,), f32),
            pltpu.SMEM(chaos.shape, f32),
            pltpu.VMEM(weights.shape, f32),
            pltpu.SemaphoreType.DMA((4,)),
        ],
    )(node, turns, *kept(node_index.T, node_weights, chaos, weights), staged, wave_hi, wave_lo)
    image, slope, fields = call(
        functools.partial(forward_kernel, radius, tiles),
        20,
        [smem] + [vmem] * 9,
        [
            shape_of(nodes, slab, cols, dtype=bf16),
            shape_of(rows, 2 * cols),
            shape_of(kernels, rows, 3 * cols),
        ],
        [
            pltpu.VMEM((2 * kernels * count, span), bf16),
            pltpu.VMEM((2 * kernels * count, span), bf16),
            pltpu.VMEM((kernels // 2, 2, 3 * count, 6 * cols), bf16),
            pltpu.VMEM((rows, 2 * cols), f32),
        ],
    )(tile, scalars, packed, after, before, gr, gi, cs, wave_hi, wave_lo)
    images = lax.all_to_all(image, "node", 0, 0)
    (pressure,) = call(
        functools.partial(middle_kernel, radius, 4 * count), 8, [vmem] * 5, [shape_of(nodes, slab, cols)]
    )(images, wanted, after, before, scalars)
    pressure = lax.all_to_all((pressure * 8192.0).astype(jnp.float16), "node", 0, 0).astype(f32) * (1.0 / 8192.0)
    (spread,) = call(
        functools.partial(backward_kernel, radius),
        16,
        [vmem] * 10,
        [shape_of(nodes, share + 8, cols)],
        [
            pltpu.VMEM((2 * kernels * count, span), bf16),
            pltpu.VMEM((2 * kernels * count, span), bf16),
            pltpu.VMEM((rows, 2 * cols), f32),
        ],
    )(pressure, slope, fields, fh, fl, gr, gi, u, wave_hi, wave_lo)
    spread = lax.all_to_all(spread.astype(jnp.float16), "node", 0, 0).astype(f32)
    return (spread[:, :share] * jnp.exp2(spread[:, share : share + 1])).sum(0)


def solution(mesh):
    placed = (
        P(None, "tile"),
        P("node", None, None, None, None),
        P("node", None),
        P(),
        P(),
        P(),
        P(),
        P(None, None, "tile"),
    )
    return jax.shard_map(local, mesh=mesh, in_specs=placed, out_specs=P("node", "tile"), check_vma=False)
```

```python
import functools
import math

import jax
import jax.numpy as jnp
import ml_dtypes
import numpy as np
from jax import lax
from jax.experimental import pallas as pl
from jax.experimental.pallas import tpu as pltpu
from jax.sharding import PartitionSpec as P

LEVELS = 5
resist_slope = 4.0
resist_level = 0.6
degrees = [(d - q, q) for d in range(5) for q in range(d + 1)]
f32, bf16 = jnp.float32, jnp.bfloat16
vmem = pl.BlockSpec(memory_space=pltpu.VMEM)
smem = pl.BlockSpec(memory_space=pltpu.SMEM)
hbm = pl.BlockSpec(memory_space=pltpu.HBM)


def parts_of(value):
    high = value.astype(bf16)
    return high, (value - high.astype(f32)).astype(bf16)


def mm(a, b):
    return jnp.dot(a, b, preferred_element_type=f32)


def mm3(a, b):
    return mm(jnp.concatenate([a[0], a[0], a[1]], 1), jnp.concatenate([b[0], b[1], b[0]], 0))


def cosine(turn, period):
    turn = jnp.bitwise_and(turn, period - 1)
    half = jnp.minimum(turn, period - turn)
    far = half > period // 4
    angle = jnp.where(far, period // 2 - half, half).astype(f32) * (2.0 * math.pi / period)
    z = angle * angle
    poly = jnp.full_like(z, 1.0 / math.factorial(12))
    for order in (10, 8, 6, 4, 2, 0):
        sign = -1.0 if order % 4 == 2 else 1.0
        poly = poly * z + sign / math.factorial(order)
    return jnp.where(far, -poly, poly)


def column_waves(length):
    turn = (np.arange(length)[:, None] * np.arange(length)[None, :]) % length
    wave = np.concatenate([np.cos(2 * np.pi * turn / length), np.sin(2 * np.pi * turn / length)], 1)
    high = wave.astype(np.float32).astype(ml_dtypes.bfloat16)
    low = (wave - high.astype(np.float64)).astype(np.float32).astype(ml_dtypes.bfloat16)
    return high, low


def lanes(shape):
    return lax.broadcasted_iota(jnp.int32, shape, len(shape) - 1)


def turned(value):
    return pltpu.roll(value, value.shape[-1] // 2, len(value.shape) - 1)


def outer_lanes(shape, radius):
    lane = lanes(shape)
    return (lane < radius) | (lane >= shape[-1] - radius)


def right_lanes(shape, radius):
    lane, half = lanes(shape), shape[-1] // 2
    return (lane < radius) | ((lane >= half) & (lane < half + radius))


def spectrum_kernel(radius, node, freq_in, mask_in, target_in, packed_ref, wanted_ref, fh_ref, fl_ref, freq, mask, raw, sems):
    rows, cols = mask.shape
    count = freq.shape[0]
    terms, share = raw.shape[0], raw.shape[1]
    own = node[0]
    mirrored = own >= rows // (2 * share)
    at = jnp.where(mirrored, rows + rows // 2 - share - own * share, own * share)
    at = pl.multiple_of(at, share)
    moves = [(freq_in, freq), (mask_in, mask), (target_in.at[:, pl.ds(at, share), :], raw)]
    copies = [pltpu.make_async_copy(source, goal, sems.at[i]) for i, (source, goal) in enumerate(moves)]
    for copy in copies:
        copy.start()
    copies[0].wait()
    line = lax.broadcasted_iota(jnp.int32, (2 * count, 128), 0)
    f_freq = jnp.zeros((2 * count, 128), jnp.int32)
    for i in range(count):
        f_freq = jnp.where((line == i) | (line == i + count), freq[i], f_freq)
    f_full = jnp.concatenate([f_freq] * (rows // 128), 1)
    f_row = lax.broadcasted_iota(jnp.int32, (2 * count, rows), 0)
    turn = f_full * (2 * lanes((2 * count, rows)) + 1) + jnp.where(f_row >= count, rows // 2, 0)
    f_parts = parts_of(cosine(turn, 2 * rows))
    fh_ref[...], fl_ref[...] = f_parts
    copies[2].wait()
    row = lax.broadcasted_iota(jnp.int32, (share, share), 0)
    chosen = jnp.where(mirrored, share - 1 - row, row) == lanes((share, share))
    order = jnp.where(chosen, 1.0, 0.0).astype(bf16)
    half = share // 2
    outer = outer_lanes((half, cols), radius)
    for j in range(terms):
        goal = mm(order, raw[j])
        wanted_ref[j] = goal.astype(bf16)
        edge = jnp.where(outer, goal[:half], turned(goal[half:]))
        packed_ref[4 * count + half * j : 4 * count + half * (j + 1), :] = edge.astype(bf16)
    copies[1].wait()
    high, low = parts_of(mm3(f_parts, parts_of(mask[...])) * (1.0 / math.sqrt(rows)))
    packed_ref[0 : 2 * count, :] = high
    packed_ref[2 * count : 4 * count, :] = low


def tables_kernel(
    node, freq_in, index_in, node_weights_in, chaos_in, weights_in, taps_in, wave_hi_in, wave_lo_in,
    u_ref, cs_ref, gr_ref, gi_ref, wave_hi, wave_lo, scalars_ref,
    freq, index, node_weights, chaos, weights, taps, sems,
):
    rows = u_ref.shape[0]
    count = freq.shape[0]
    kernels, tap_count = taps.shape[1], taps.shape[4]
    span = wave_hi.shape[0]
    radius = (tap_count - 1) // 2
    nodes = index.shape[1]
    moves = [
        (freq_in, freq),
        (index_in, index),
        (node_weights_in, node_weights),
        (chaos_in, chaos),
        (weights_in, weights),
        (wave_hi_in, wave_hi),
        (wave_lo_in, wave_lo),
        (taps_in, taps),
    ]
    copies = [pltpu.make_async_copy(source, goal, sems.at[i]) for i, (source, goal) in enumerate(moves)]
    for copy in copies:
        copy.start()
    for copy in copies[:4]:
        copy.wait()
    lane = lanes((8, 256))
    turns = jnp.zeros((8, 256), jnp.int32)
    for i in range(count):
        turns = jnp.where((lane == i) | (lane == i + count) | (lane == i + 2 * count), freq[i], turns)
    quarter = rows // 2
    steps = lax.broadcasted_iota(jnp.int32, (8, 256), 0)

    def spread_out(frequency, first, lead):
        width = frequency.shape[1]
        full = jnp.concatenate([frequency] * (first // 8), 0)
        turn = full * (2 * lax.broadcasted_iota(jnp.int32, (first, width), 0) + 1) + lead
        jump = frequency * (2 * first * steps[:, :width])
        return [cosine(t, 2 * rows) for t in (turn, turn - quarter, jump, jump - quarter)]

    first = rows // 8
    lane = lanes((first, 128))
    c, s, step_c, step_s = spread_out(turns[:, :128], first, jnp.where(lane >= count, quarter, 0))
    for i in range(8):
        table = c * step_c[i : i + 1, :] - s * step_s[i : i + 1, :]
        high, low = parts_of(jnp.where(lane < 2 * count, table, 0.0))
        at = pl.ds(i * first, first)
        u_ref[at, 0:128] = high
        u_ref[at, 128:256] = high
        u_ref[at, 256:384] = low
    first = rows // 16
    lane = lanes((first, 256))
    c, s, step_c, step_s = spread_out(turns, first, 0)
    for i in range(8):
        by_c, by_s = step_c[i : i + 1, :], step_s[i : i + 1, :]
        for start, table in ((0, c * by_c - s * by_s), (rows // 2, s * by_c + c * by_s)):
            high, low = parts_of(table)
            both = jnp.where(lane < 2 * count, high.astype(f32), low.astype(f32))
            cs_ref[start + i * first : start + (i + 1) * first, :] = both[:, : 3 * count].astype(bf16)
    for n in range(nodes):
        poly = []
        for axis in range(2):
            c = index[axis, n].astype(f32) * (2.0 / (LEVELS - 1)) - 1.0
            s = c * c
            poly.append([None, c, 1.5 * s - 0.5, (2.5 * s - 1.5) * c, (4.375 * s - 3.75) * s + 0.375])
        weight = node_weights[n]
        for j, (p, q) in enumerate(degrees):
            value = weight
            if p:
                value = value * poly[0][p]
            if q:
                value = value * poly[1][q]
            scalars_ref[16 * n + j : 16 * n + j + 1, :] = jnp.full((1, 128), value, f32)
    dose = 1.0 + 0.1 * (index[1, node[0]].astype(f32) * (2.0 / (LEVELS - 1)) - 1.0)
    scalars_ref[15:16, :] = jnp.full((1, 128), dose, f32)
    for j in range(len(degrees)):
        scalars_ref[16 * nodes + j : 16 * nodes + j + 1, :] = jnp.full((1, 128), chaos[j], f32)
    for copy in copies[4:]:
        copy.wait()
    side = [jnp.concatenate([w[span - radius : span], w[0 : tap_count - radius]], 0) for w in (wave_hi, wave_lo)]
    scale = jnp.sqrt(weights[...]) * (1.0 / (span * math.sqrt(count)))
    for k in range(kernels):
        parts = parts_of(taps[0, k].reshape(2 * count, tap_count))
        prod = mm3(parts, side)
        amount = scale[0:1, k : k + 1]
        gr_ref[k] = (prod[:count, :span] - prod[count:, span:]) * amount
        gi_ref[k] = (prod[:count, span:] + prod[count:, :span]) * amount


def forward_kernel(
    radius, tiles, tile, scalars, packed, twin, border, gr, gi, cs, wave_hi, wave_lo,
    image_ref, slope_ref, fields_ref, bh, bl, x, total,
):
    kernels, count, span = gr.shape
    nodes, slab, cols = image_ref.shape
    rows = slope_ref.shape[0]
    share = rows // nodes
    half = share // 2
    even = lax.rem(tile[0], 2) == 0
    near = (lanes((2 * count, cols)) < 2 * radius) == even
    pair = []
    for part in range(2):
        at = pl.ds(2 * part * count, 2 * count)
        beyond = jnp.where(near, twin[at, :].astype(f32), border[at, :].astype(f32))
        pair.append(jnp.concatenate([packed[at, :], beyond.astype(bf16)], 1))
    wave = (wave_hi[...], wave_lo[...])
    prod = mm3(pair, wave)
    a_re = prod[:count, :span] + prod[count:, span:]
    a_im = prod[count:, :span] - prod[:count, span:]
    for k in range(kernels):
        b_re = gr[k] * a_re - gi[k] * a_im
        b_im = gr[k] * a_im + gi[k] * a_re
        for d, value in ((0, b_re), (1, b_im)):
            at = pl.ds((2 * k + d) * count, count)
            bh[at, :], bl[at, :] = parts_of(value)
    outer = outer_lanes((count, cols), radius)
    for k in range(kernels):
        if k % 2 == 0:
            at = pl.ds(2 * k * count, 2 * 2 * count)
            qq = mm3((bh[at, :], bl[at, :]), wave)
        q = qq[(k % 2) * 2 * count : (k % 2 + 1) * 2 * count]
        re = q[:count, :span] - q[count:, span:]
        im = q[:count, span:] + q[count:, :span]
        edge = jnp.where(outer, re[:, cols:], turned(im[:, cols:]))
        cross = jnp.where(outer, im[:, cols:], -turned(re[:, cols:]))
        straight = jnp.concatenate([re[:, :cols], im[:, :cols], edge], 1)
        crossed = jnp.concatenate([im[:, :cols], -re[:, :cols], cross], 1)
        for d, value in ((0, straight), (1, crossed)):
            high, low = parts_of(value)
            at = 3 * cols * (k % 2)
            for place, part in ((0, high), (1, low), (2, high)):
                x[k // 2, d, place * count : (place + 1) * count, at : at + 3 * cols] = part
    for pair in range(kernels // 2):
        even_part = mm(cs[: rows // 2, :], x[pair, 0])
        odd_part = mm(cs[rows // 2 :, :], x[pair, 1])
        for first, field in ((0, even_part - odd_part), (rows // 2, even_part + odd_part)):
            at = pl.ds(first, rows // 2)
            fields_ref[2 * pair, at, :] = field[:, : 3 * cols]
            fields_ref[2 * pair + 1, at, :] = field[:, 3 * cols :]
            square = field * field
            inner = square[:, :cols] + square[:, cols : 2 * cols]
            inner = inner + (square[:, 3 * cols : 4 * cols] + square[:, 4 * cols : 5 * cols])
            edge = square[:, 2 * cols : 3 * cols] + square[:, 5 * cols :]
            if pair:
                inner, edge = inner + total[at, :cols], edge + total[at, cols:]
            total[at, :cols] = inner
            total[at, cols:] = edge

    value = scalars[15:16, :]
    inner = total[:, :cols]
    edge = total[:, cols:]
    edge = edge + turned(edge)
    right = right_lanes((rows, cols), radius)
    inside = (right & (tile[0] < tiles - 1)) | (jnp.logical_not(right) & (tile[0] > 0))
    outer = outer_lanes((half, cols), radius)
    for place, intensity in ((0, inner), (1, edge)):
        resist = jax.nn.sigmoid(resist_slope * (value * intensity - resist_level))
        slope = resist * (1.0 - resist) * (2.0 * resist_slope * value)
        if place:
            slope = jnp.where(inside, slope, 0.0)
        slope_ref[:, place * cols : (place + 1) * cols] = slope
        for n in range(nodes):
            rows_n = resist[n * share : (n + 1) * share]
            if place:
                image_ref[n, share:slab, :] = jnp.where(outer, rows_n[:half], rows_n[half:]).astype(bf16)
            else:
                image_ref[n, 0:share, :] = rows_n.astype(bf16)


def middle_kernel(radius, offset, tile, images, wanted, twin, border, scalars, pressure_ref):
    nodes, slab, cols = images.shape
    share = wanted.shape[1]
    step = slab - share
    near = right_lanes((step, cols), radius) == (lax.rem(tile[0], 2) == 0)
    for first in range(0, slab, step):
        image = [images[n, first : first + step, :].astype(f32) for n in range(nodes)]
        pressure = [None] * nodes
        for j in range(len(degrees)):
            weight = [scalars[16 * n + j : 16 * n + j + 1, :] for n in range(nodes)]
            coefficient = weight[0] * image[0]
            for n in range(1, nodes):
                coefficient = coefficient + weight[n] * image[n]
            if first < share:
                goal = wanted[j, first : first + step, :].astype(f32)
            else:
                at = pl.ds(offset + j * step, step)
                goal = jnp.where(near, twin[at, :].astype(f32), border[at, :].astype(f32))
            mixed = scalars[16 * nodes + j : 16 * nodes + j + 1, :] * jnp.tanh(coefficient - goal)
            for n in range(nodes):
                term = weight[n] * mixed
                pressure[n] = term if j == 0 else pressure[n] + term
        for n in range(nodes):
            pressure_ref[n, first : first + step, :] = pressure[n]


def backward_kernel(radius, pressure, slope, fields, fh, fl, gr, gi, u, wave_hi, wave_lo, out_ref, dh, dl, scale):
    kernels, count, span = gr.shape
    nodes, slab, cols = pressure.shape
    rows = slope.shape[0]
    share = rows // nodes
    half = share // 2
    outer = outer_lanes((half, cols), radius)
    for n in range(nodes):
        at = pl.ds(n * share, share)
        scale[at, :cols] = slope[at, :cols] * pressure[n, :share, :]
        edge = pressure[n, share:, :]
        back = turned(edge)
        top, bottom = pl.ds(n * share, half), pl.ds(n * share + half, half)
        scale[top, cols:] = slope[top, cols:] * jnp.where(outer, edge, back)
        scale[bottom, cols:] = slope[bottom, cols:] * jnp.where(outer, back, edge)
    table = []
    for first in (0, count):
        table.append(jnp.concatenate([fh[first : first + count, : rows // 2], fl[first : first + count, : rows // 2]], 0))
    outer = outer_lanes((count, cols), radius)

    for pair in range(0, kernels, 2):
        halves = []
        for first in (0, rows // 2):
            at = pl.ds(first, rows // 2)
            inner, edge = scale[at, :cols], scale[at, cols:]
            both = jnp.concatenate([fields[pair, at, :], fields[pair + 1, at, :]], 1)
            halves.append(both * jnp.concatenate([inner, inner, edge] * 2, 1))
        grads = []
        for lhs, value in zip(table, (halves[0] + halves[1], halves[0] - halves[1])):
            high, low = parts_of(value)
            prod = mm(lhs, high)
            grads.append(prod[:count] + prod[count:] + mm(lhs[:count], low))
        for k in (pair, pair + 1):
            straight, crossed = (g[:, 3 * cols * (k - pair) : 3 * cols * (k - pair + 1)] for g in grads)
            edge, cross = straight[:, 2 * cols :], crossed[:, 2 * cols :]
            re_edge = jnp.where(outer, edge - turned(cross), 0.0)
            im_edge = jnp.where(outer, cross + turned(edge), 0.0)
            re = jnp.concatenate([straight[:, :cols] - crossed[:, cols : 2 * cols], re_edge], 1)
            im = jnp.concatenate([straight[:, cols : 2 * cols] + crossed[:, :cols], im_edge], 1)
            for d, value in ((0, re), (1, im)):
                at = pl.ds((2 * k + d) * count, count)
                dh[at, :], dl[at, :] = parts_of(value)

    wave = (wave_hi[...], wave_lo[...])
    a_re = jnp.zeros((count, span), f32)
    a_im = jnp.zeros((count, span), f32)
    for k in range(kernels):
        if k % 2 == 0:
            at = pl.ds(2 * k * count, 2 * 2 * count)
            qq = mm3((dh[at, :], dl[at, :]), wave)
        q = qq[(k % 2) * 2 * count : (k % 2 + 1) * 2 * count]
        b_re = q[:count, :span] + q[count:, span:]
        b_im = q[count:, :span] - q[:count, span:]
        a_re = a_re + gr[k] * b_re + gi[k] * b_im
        a_im = a_im + gr[k] * b_im - gi[k] * b_re
    near = [jnp.concatenate([w[:, 0:cols], w[:, span : span + cols]], 1) for w in (wave_hi, wave_lo)]
    prod = mm3(parts_of(jnp.concatenate([a_re, a_im], 0)), near)
    d_re = prod[:count, :cols] - prod[count:, cols:]
    d_im = prod[:count, cols:] + prod[count:, :cols]
    rest = jnp.zeros((128 - 2 * count, cols), f32)
    high, low = parts_of(jnp.concatenate([d_re, d_im, rest], 0))
    spread = mm(u[...], jnp.concatenate([high, low, high], 0)) * (1.0 / math.sqrt(rows))
    largest = jnp.max(jnp.abs(spread), axis=0, keepdims=True)
    power = jnp.ceil(jnp.log2(jnp.maximum(largest, 1e-30)))
    spread = spread * jnp.exp2(-power)
    for n in range(nodes):
        out_ref[n, :share, :] = spread[n * share : (n + 1) * share]
        out_ref[n, share:, :] = jnp.broadcast_to(power, (out_ref.shape[1] - share, cols))


def shape_of(*shape, dtype=f32):
    return jax.ShapeDtypeStruct(shape, dtype)


def call(kernel, mebibytes, spaces, outs, scratch=()):
    return pl.pallas_call(
        kernel,
        in_specs=spaces,
        out_specs=[vmem] * len(outs),
        out_shape=list(outs),
        scratch_shapes=list(scratch),
        compiler_params=pltpu.CompilerParams(vmem_limit_bytes=mebibytes << 20),
    )


def kept(*arrays):
    return [pltpu.with_memory_space_constraint(a, pltpu.HBM) for a in arrays]


def local(mask, taps, weights, node_weights, node_index, freq, chaos, target):
    rows, cols = mask.shape
    kernels, count, tap_count = taps.shape[1], taps.shape[3], taps.shape[4]
    terms = target.shape[0]
    radius = (tap_count - 1) // 2
    span = 2 * cols
    nodes, tiles = lax.axis_size("node"), lax.axis_size("tile")
    node, tile = lax.axis_index("node").reshape(1), lax.axis_index("tile").reshape(1)
    share = rows // nodes
    half = share // 2
    slab = share + half
    inside = [(i, i ^ 1) for i in range(tiles) if i ^ 1 < tiles]
    across = [(i, ((i + 1) ^ 1) - 1) for i in range(tiles) if 0 <= ((i + 1) ^ 1) - 1 < tiles]
    wave_hi, wave_lo = (jnp.asarray(w) for w in column_waves(span))
    packed, wanted, fh, fl = call(
        functools.partial(spectrum_kernel, radius),
        8,
        [smem] + [hbm] * 3,
        [
            shape_of(4 * count + half * terms, cols, dtype=bf16),
            shape_of(terms, share, cols, dtype=bf16),
            shape_of(2 * count, rows, dtype=bf16),
            shape_of(2 * count, rows, dtype=bf16),
        ],
        [
            pltpu.SMEM(freq.shape, jnp.int32),
            pltpu.VMEM(mask.shape, f32),
            pltpu.VMEM((terms, share, cols), bf16),
            pltpu.SemaphoreType.DMA((3,)),
        ],
    )(node, *kept(freq, mask, target))
    border = lax.ppermute(packed, "tile", across)
    twin = lax.ppermute(packed, "tile", inside)
    u, cs, gr, gi, wave_hi, wave_lo, scalars = call(
        tables_kernel,
        16,
        [smem] + [hbm] * 8,
        [
            shape_of(rows, 384, dtype=bf16),
            shape_of(rows, 3 * count, dtype=bf16),
            shape_of(kernels, count, span),
            shape_of(kernels, count, span),
            shape_of(span, 2 * span, dtype=bf16),
            shape_of(span, 2 * span, dtype=bf16),
            shape_of(16 * nodes + 16, 128),
        ],
        [
            pltpu.SMEM(freq.shape, jnp.int32),
            pltpu.SMEM((2, nodes), jnp.int32),
            pltpu.SMEM((nodes,), f32),
            pltpu.SMEM(chaos.shape, f32),
            pltpu.VMEM(weights.shape, f32),
            pltpu.VMEM(taps.shape, f32),
            pltpu.SemaphoreType.DMA((8,)),
        ],
    )(node, *kept(freq, node_index.T, node_weights, chaos, weights, taps, wave_hi, wave_lo))
    image, slope, fields = call(
        functools.partial(forward_kernel, radius, tiles),
        20,
        [smem] + [vmem] * 9,
        [
            shape_of(nodes, slab, cols, dtype=bf16),
            shape_of(rows, 2 * cols),
            shape_of(kernels, rows, 3 * cols),
        ],
        [
            pltpu.VMEM((2 * kernels * count, span), bf16),
            pltpu.VMEM((2 * kernels * count, span), bf16),
            pltpu.VMEM((kernels // 2, 2, 3 * count, 6 * cols), bf16),
            pltpu.VMEM((rows, 2 * cols), f32),
        ],
    )(tile, scalars, packed, twin, border, gr, gi, cs, wave_hi, wave_lo)
    images = lax.all_to_all(image, "node", 0, 0)
    (pressure,) = call(
        functools.partial(middle_kernel, radius, 4 * count), 8, [smem] + [vmem] * 5, [shape_of(nodes, slab, cols)]
    )(tile, images, wanted, twin, border, scalars)
    pressure = lax.all_to_all((pressure * 8192.0).astype(jnp.float16), "node", 0, 0).astype(f32) * (1.0 / 8192.0)
    (spread,) = call(
        functools.partial(backward_kernel, radius),
        16,
        [vmem] * 10,
        [shape_of(nodes, share + 8, cols)],
        [
            pltpu.VMEM((2 * kernels * count, span), bf16),
            pltpu.VMEM((2 * kernels * count, span), bf16),
            pltpu.VMEM((rows, 2 * cols), f32),
        ],
    )(pressure, slope, fields, fh, fl, gr, gi, u, wave_hi, wave_lo)
    spread = lax.all_to_all(spread.astype(jnp.float16), "node", 0, 0).astype(f32)
    return (spread[:, :share] * jnp.exp2(spread[:, share : share + 1])).sum(0)


def solution(mesh):
    placed = (
        P(None, "tile"),
        P("node", None, None, None, None),
        P("node", None),
        P(),
        P(),
        P(),
        P(),
        P(None, None, "tile"),
    )
    return jax.shard_map(local, mesh=mesh, in_specs=placed, out_specs=P("node", "tile"), check_vma=False)
```
